32 devices in a mesh: groups: 2 (over x), lon: 16 (over z, y, core).
Axes of the slice: x: 2, y: 2, z: 4, core: 2. Of those that a mesh axis runs over, the one named last changes fastest.
Arguments:
- atm_in: bfloat16 [256, 48, 640], P(('groups', 'lon')), parts along dimension 0, may hold values from -6 to 6
- ocean_in: bfloat16 [512, 95, 128], P(('groups', 'lon')), parts along dimension 0, may hold values from -6 to 6
- lift_weight: bfloat16 [48, 256], replicated, may hold values from -0.875 to 0.875
- conv_weight: bfloat16 [3, 3, 256, 256], replicated, may hold values from -0.125 to 0.125
- flux_weight: bfloat16 [256, 16], replicated, may hold values from -0.375 to 0.375
- ocean_weight: bfloat16 [95, 256], replicated, may hold values from -0.625 to 0.625
- couple_weight: bfloat16 [16, 256], replicated, may hold values from -3 to 3
- mix_weight: bfloat16 [256, 256], replicated, may hold values from -0.375 to 0.375
- regrid_weight: bfloat16 [256, 4, 128, 128], P('lon'), may hold values from 0 to 1, as said below
- pair_tile: int32 [256, 3], P('lon'), may hold values from 0 to 39, as said below
- ocean_mask: int32 [256], P('lon'), may hold values from 0 to 1, as said below
Outputs:
- atm_hidden: bfloat16 [256, 256, 640], P(('groups', 'lon')), parts along dimension 0
- ocean_hidden: bfloat16 [512, 256, 128], P(('groups', 'lon')), parts along dimension 0
The draws below stay inside these ranges and needn't reach their ends.
There are 2 independent parts, one for each index of `groups`. The reference program is written for one: setup_inputs(seed, part) draws one part's arguments, and reference() takes and returns one part's arrays. A program takes and returns all parts, laid end to end along the dimension named above; an argument that names none is the same for every part. Nothing has to cross between parts.
Inputs may be any that keep to these rules, and one draw needn't show every extreme that they name: `regrid_weight`: block p = 3 is zero except for the northernmost 2 tiles of each strip (local index 14 and above); blocks 0 to 2 are positive. `pair_tile`: within one of the band of the ocean tile's latitude; column 1 is the band itself. `ocean_mask`: each device's 16 tiles hold between 2 and 8 ones, its northernmost 2 tiles always among them; some device has exactly 8.
All inputs are finite; a program needn't handle non-finite values.
Results may differ from the reference program's by a relative error of at most 0.0053.
Values may be sent and summed in bfloat16 or wider, within the bound.
No kernel may reach another device: no remote copies, remote signals or barrier semaphores. Data moves between devices by JAX's collectives and lax.ppermute only.
A program may use at most 128 MiB of HBM per device.

```python
import jax
import jax.numpy as jnp
from jax import lax

ACH = 48
OCH = 95
WIDTH = 256
FLUX = 16
PAIRS = 4
FOLDB = 2
ALON = 8
LAT = 640
TLAT = 16
OT = 16
MAXACT = 8
LONS = 16
AT = 40
TA = 128
TO = 128
NLON = 128
OTILES = 256


def ocean_layout(key):
    base_key = jax.random.fold_in(key, 11)
    key_counts, key_full, key_chosen, key_score = jax.random.split(base_key, 4)
    lowest = max(FOLDB, MAXACT // 4)
    counts = jax.random.randint(key_counts, (LONS,), lowest, MAXACT // 2 + 1)
    full = jax.random.randint(key_full, (LONS,), 0, 8) == 0
    chosen = jax.random.randint(key_chosen, (), 0, LONS)
    full = full | (jnp.arange(LONS) == chosen)
    counts = jnp.where(full, MAXACT, counts).astype(jnp.int32)
    local = jnp.arange(OT, dtype=jnp.int32)
    score = jax.random.randint(key_score, (LONS, OT), 0, 2 ** 20) * OT + local[None, :]
    score = jnp.where(local[None, :] >= OT - FOLDB, local[None, :] - OT, score)
    ranks = jnp.argsort(jnp.argsort(score, axis=1), axis=1)
    water = (ranks < counts[:, None]).astype(jnp.int32)
    return water


def draw_ocean_mask(key, part):
    return ocean_layout(key).reshape(-1)


def draw_pair_tile(key, part):
    bands = jnp.arange(OTILES, dtype=jnp.int32) % OT
    center = jnp.minimum(bands * AT // (OT - 1), AT - 1)
    offsets = jax.random.randint(jax.random.fold_in(key, 5), (OTILES, 3), -1, 2)
    offsets = jnp.where(jnp.arange(3)[None, :] == 1, 0, offsets)
    return jnp.clip(center[:, None] + offsets, 0, AT - 1).astype(jnp.int32)


def draw_regrid_weight(key, part):
    uniform_part = jax.random.uniform(jax.random.fold_in(key, 3), (OTILES, PAIRS, TO, TA), jnp.float32)
    values = jnp.exp(jnp.log(0.01) + uniform_part * jnp.log(100.0))
    bands = jnp.arange(OTILES) % OT
    near_fold = bands >= OT - FOLDB
    last_pair = jnp.arange(PAIRS) == PAIRS - 1
    keep = jnp.where(last_pair[None, :] & jnp.logical_not(near_fold)[:, None], 0.0, 1.0)
    return (values * keep[:, :, None, None]).astype(jnp.bfloat16)


def shard_levels(own_key, dims, cuts, smallest, high):
    def one(position, blocks):
        steps = jax.random.uniform(jax.random.fold_in(jax.random.fold_in(own_key, 6), position), (blocks,), jnp.float32, smallest / len(cuts), high / len(cuts))
        return jnp.repeat(jnp.exp(steps), dims[position] // blocks).reshape((-1,) + (1,) * (len(dims) - position - 1))

    loudness = one(*cuts[0])
    for cut in cuts[1:]:
        loudness = loudness * one(*cut)
    return loudness


def noise(own_key, extent, spread, limit, cuts=(), kind=jnp.bfloat16):
    level = shard_levels(own_key, extent, cuts, -0.22, 0.18) if cuts else 1.0
    array = jax.random.normal(own_key, extent, jnp.float32) * spread * level
    return jnp.minimum(jnp.maximum(array, -limit), limit).astype(kind)


def setup_inputs(seed: int = 0, part: int = 0) -> dict:
    arg_keys = jax.random.split(jax.random.key(seed), 12)
    part_splits = jax.random.split(jax.random.fold_in(arg_keys[11], part), 12)
    return {
        "atm_in": noise(part_splits[0], (NLON, ACH, LAT), 1.0, 6.0, ((0, 16),)),
        "ocean_in": noise(part_splits[1], (OTILES, OCH, TO), 1.0, 6.0, ((0, 16),)),
        "lift_weight": noise(arg_keys[2], (ACH, WIDTH), ACH ** -0.5, 0.875),
        "conv_weight": noise(arg_keys[3], (3, 3, WIDTH, WIDTH), (9 * WIDTH) ** -0.5, 0.125),
        "flux_weight": noise(arg_keys[4], (WIDTH, FLUX), WIDTH ** -0.5, 0.375),
        "ocean_weight": noise(arg_keys[5], (OCH, WIDTH), OCH ** -0.5, 0.625),
        "couple_weight": noise(arg_keys[6], (FLUX, WIDTH), (FLUX // 4) ** -0.5, 3.0),
        "mix_weight": noise(arg_keys[7], (WIDTH, WIDTH), WIDTH ** -0.5, 0.375),
        "regrid_weight": draw_regrid_weight(jax.random.fold_in(arg_keys[11], 71), part),
        "pair_tile": draw_pair_tile(jax.random.fold_in(arg_keys[11], 71), part),
        "ocean_mask": draw_ocean_mask(jax.random.fold_in(arg_keys[11], 71), part),
    }


def reference(atm_in, ocean_in, lift_weight, conv_weight, flux_weight, ocean_weight, couple_weight, mix_weight, regrid_weight, pair_tile, ocean_mask):
    single = jnp.float32
    lifted = jnp.einsum('xcy,co->xoy', atm_in.astype(single), lift_weight.astype(single)).astype(jnp.bfloat16)
    wrapped = jnp.concatenate([lifted[-1:], lifted, lifted[:1]], 0)
    wrapped = jnp.pad(wrapped, ((0, 0), (0, 0), (1, 1)))
    taps = conv_weight.astype(single)

    def conv_block(index):
        slab_part = lax.dynamic_slice_in_dim(wrapped, (index * ALON).astype(jnp.int32), ALON + 2, 0).astype(single)
        total = jnp.zeros((ALON, WIDTH, LAT), single)
        for shift_x in range(3):
            for shift_y in range(3):
                total = total + jnp.einsum('xcy,co->xoy', slab_part[shift_x:shift_x + ALON, :, shift_y:shift_y + LAT], taps[shift_x, shift_y])
        return total

    conv = lax.map(conv_block, jnp.arange(LONS, dtype=jnp.int32)).reshape(NLON, WIDTH, LAT)
    atm_hidden = (lifted.astype(single) + jax.nn.gelu(conv)).astype(jnp.bfloat16)
    flux = jnp.einsum('xhy,hf->xfy', atm_hidden.astype(single), flux_weight.astype(single)).astype(jnp.bfloat16)
    flux_tile = flux.reshape(LONS, ALON, FLUX, AT, TLAT).transpose(0, 3, 2, 1, 4).reshape(LONS, AT, FLUX, TA)

    def ocean_device(device):
        west = jnp.mod(device - 1 + LONS, LONS).astype(jnp.int32)
        east = jnp.mod(device + 1, LONS).astype(jnp.int32)
        mirror = (LONS - 1 - device).astype(jnp.int32)
        table = jnp.concatenate([flux_tile[west], flux_tile[device], flux_tile[east], flux_tile[mirror, AT - 1][None]], 0)
        start = (device * OT).astype(jnp.int32)
        states = lax.dynamic_slice_in_dim(ocean_in, start, OT, 0).astype(single)
        blocks = lax.dynamic_slice_in_dim(regrid_weight, start, OT, 0).astype(single)
        bands = lax.dynamic_slice_in_dim(pair_tile, start, OT, 0)
        water = lax.dynamic_slice_in_dim(ocean_mask, start, OT, 0)
        index = jnp.concatenate([bands + jnp.arange(3, dtype=jnp.int32)[None, :] * AT, jnp.full((OT, 1), 3 * AT, jnp.int32)], 1)
        got = table[index].astype(single)
        numer = jnp.einsum('spfa,spoa->sfo', got, blocks)
        denom = jnp.sum(blocks, axis=(1, 3))
        regrid = (numer / denom[:, None, :]).astype(jnp.bfloat16)
        base = (jnp.einsum('sco,ch->sho', states, ocean_weight.astype(single)) + jnp.einsum('sfo,fh->sho', regrid.astype(single), couple_weight.astype(single))).astype(jnp.bfloat16)
        mixed = jnp.einsum('sho,hk->sko', base.astype(single), mix_weight.astype(single))
        result = (base.astype(single) + jax.nn.gelu(mixed)).astype(jnp.bfloat16)
        return jnp.where(water[:, None, None] == 1, result, jnp.zeros_like(result))

    ocean_hidden = lax.map(ocean_device, jnp.arange(LONS, dtype=jnp.int32)).reshape(OTILES, WIDTH, TO)
    return atm_hidden, ocean_hidden
```

```python
import functools

import jax
import jax.numpy as jnp
from jax import lax
from jax.experimental import pallas as pl
from jax.experimental.pallas import tpu as pltpu
from jax.sharding import PartitionSpec as P

TLAT = 16
MAXACT = 8
FOLDB = 2
F32 = jnp.float32
BF16 = jnp.bfloat16
ROOT = 0.7978845608028654
CUBIC = ROOT * 0.044715

ANY = pl.BlockSpec(memory_space=pl.ANY)
VM = pl.BlockSpec(memory_space=pltpu.VMEM)
SM = pl.BlockSpec(memory_space=pltpu.SMEM)


def dot(a, b):
    return lax.dot_general(a, b, (((1,), (0,)), ((), ())), preferred_element_type=F32)


def dot_t(a, b):
    return lax.dot_general(a, b, (((1,), (1,)), ((), ())), preferred_element_type=F32)


def gelu(x):
    half = 0.5 * x
    return half + half * jnp.tanh(x * (ROOT + CUBIC * (x * x)))


def put_shifts(taps, row, column):
    chans, lats = column.shape
    wide = column.astype(F32)
    lane = lax.broadcasted_iota(jnp.int32, wide.shape, 1)
    south = jnp.where(lane == 0, 0.0, pltpu.roll(wide, 1, 1))
    north = jnp.where(lane == lats - 1, 0.0, pltpu.roll(wide, lats - 1, 1))
    taps[pl.ds(row, chans), :] = south.astype(BF16)
    taps[pl.ds(row + chans, chans), :] = column
    taps[pl.ds(row + 2 * chans, chans), :] = north.astype(BF16)


def encode_pair(taps, rows, w1_ref, w2_ref, fw, hid, slots, flux, fslots):
    width = hid.shape[1]
    lats = hid.shape[2]
    deep = w1_ref.shape[1]

    def window(which, part, lo, hi):
        return taps[pl.ds(rows[which] + part * deep, deep), lo:hi]

    pieces = []
    full = lats // 256 * 256
    for which in range(2):
        for lo in range(0, full, 256):
            pieces.append(((which, lo, lo + 256),))
    if full < lats:
        pieces.append(((0, full, lats), (1, full, lats)))
    for piece in pieces:
        first = [window(w, 0, lo, hi) for w, lo, hi in piece]
        second = [window(w, 1, lo, hi) for w, lo, hi in piece]
        first = first[0] if len(first) == 1 else jnp.concatenate(first, 1)
        second = second[0] if len(second) == 1 else jnp.concatenate(second, 1)
        both = dot(w1_ref[...], first)
        conv = both[:width] + dot(w2_ref[...], second)
        lifted = both[width:].astype(BF16).astype(F32)
        out = (lifted + gelu(conv)).astype(BF16)
        head = dot(fw, out).astype(BF16).astype(F32)
        at = 0
        for w, lo, hi in piece:
            hid[slots[w], :, lo:hi] = out[:, at : at + hi - lo]
            flux[fslots[w], :, lo:hi] = head[:, at : at + hi - lo]
            at += hi - lo


def inner_kernel(
    x_hbm, lift_hbm, conv_hbm, fw_hbm,
    hid_hbm, flux, w1, w2, fwt,
    x, lift, conv, fw, hid, taps, comp, sems,
):
    columns, chans, lats = x.shape
    width = lift.shape[1]
    copies = [
        pltpu.make_async_copy(lift_hbm, lift, sems.at[0]),
        pltpu.make_async_copy(x_hbm, x, sems.at[1]),
        pltpu.make_async_copy(fw_hbm, fw, sems.at[2]),
    ]
    for a in range(3):
        copies.append(pltpu.make_async_copy(conv_hbm.at[a], conv.at[a], sems.at[3 + a]))
    for c in copies:
        c.start()
    span = 3 * chans
    taps[pl.ds(columns * span, span), :] = jnp.zeros((span, lats), BF16)
    comp[pl.ds(9 * chans, 2 * width - 9 * chans), :] = jnp.zeros((2 * width - 9 * chans, width), F32)
    copies[1].wait()
    for i in range(columns):
        put_shifts(taps, i * span, x[i])
    copies[0].wait()
    liftv = lift[...]
    low = jnp.zeros((4 * chans, width), F32)
    high = jnp.zeros((width - 5 * chans, width), F32)
    place = jnp.concatenate([low, liftv.astype(F32), high], 0)
    w1[pl.ds(width, width), :] = place.T.astype(BF16)
    copies[2].wait()
    fwt[...] = fw[...].astype(F32).T.astype(BF16)
    for a in range(3):
        copies[3 + a].wait()
        for b in range(3):
            comp[pl.ds((3 * a + b) * chans, chans), :] = dot(liftv, conv[a, b])
    w1[pl.ds(0, width), :] = comp[pl.ds(0, width), :].T.astype(BF16)
    w2[...] = comp[pl.ds(width, width), :].T.astype(BF16)

    def pair(i, _):
        rows = [pl.multiple_of(2 * i * span, 16), pl.multiple_of((2 * i + 1) * span, 16)]
        encode_pair(taps, rows, w1, w2, fwt[...], hid, [2 * i, 2 * i + 1], flux, [2 * i + 1, 2 * i + 2])
        pltpu.make_async_copy(hid.at[pl.ds(2 * i, 2)], hid_hbm.at[pl.ds(2 * i + 1, 2)], sems.at[0]).start()
        return 0

    pairs = (columns - 2) // 2
    lax.fori_loop(0, pairs, pair, 0)
    pltpu.make_async_copy(hid, hid_hbm.at[pl.ds(1, 2 * pairs)], sems.at[0]).wait()


def interior(x, lift, conv, fw):
    columns, chans, lats = x.shape
    width = lift.shape[1]
    fluxes = fw.shape[1]
    return pl.pallas_call(
        inner_kernel,
        out_shape=(
            jax.ShapeDtypeStruct((columns, width, lats), BF16),
            jax.ShapeDtypeStruct((columns, fluxes, lats), F32),
            jax.ShapeDtypeStruct((2 * width, width), BF16),
            jax.ShapeDtypeStruct((width, width), BF16),
            jax.ShapeDtypeStruct((fluxes, width), BF16),
        ),
        in_specs=[ANY] * 4,
        out_specs=(ANY, VM, VM, VM, VM),
        scratch_shapes=[
            pltpu.VMEM((columns, chans, lats), BF16),
            pltpu.VMEM((chans, width), BF16),
            pltpu.VMEM((3, 3, width, width), BF16),
            pltpu.VMEM((width, fluxes), BF16),
            pltpu.VMEM((columns - 2, width, lats), BF16),
            pltpu.VMEM(((columns + 1) * 3 * chans, lats), BF16),
            pltpu.VMEM((2 * width, width), F32),
            pltpu.SemaphoreType.DMA((6,)),
        ],
        cost_estimate=pl.CostEstimate(flops=4 * 10**9, bytes_accessed=4 * 10**6, transcendentals=10**6),
        name="interior",
    )(x, lift, conv, fw)


def swap_blocks(values, lanes):
    count = len(values)
    lane = lax.broadcasted_iota(jnp.int32, values[0].shape, 1)
    step = count // 2
    while step:
        shift = step * TLAT
        upper = (lane & shift) != 0
        fresh = list(values)
        for i in range(count):
            if i & step:
                continue
            low, high = values[i], values[i + step]
            fresh[i] = jnp.where(upper, pltpu.roll(high, shift, 1), low)
            fresh[i + step] = jnp.where(upper, high, pltpu.roll(low, lanes - shift, 1))
        values = fresh
        step //= 2
    return values


def edge_kernel(x_hbm, west_hbm, east_hbm, flux_in, w1, w2, fwt, edges, tiles, north, x, taps, flux, sems):
    columns, chans, lats = x_hbm.shape
    span = 3 * chans
    copies = [
        pltpu.make_async_copy(x_hbm.at[pl.ds(0, 2)], x.at[pl.ds(1, 2)], sems.at[0]),
        pltpu.make_async_copy(x_hbm.at[pl.ds(columns - 2, 2)], x.at[pl.ds(3, 2)], sems.at[1]),
        pltpu.make_async_copy(west_hbm, x.at[pl.ds(0, 1)], sems.at[2]),
        pltpu.make_async_copy(east_hbm, x.at[pl.ds(5, 1)], sems.at[3]),
    ]
    for c in copies:
        c.start()
    taps[pl.ds(6 * span, span), :] = jnp.zeros((span, lats), BF16)
    copies[0].wait()
    put_shifts(taps, span, x[1])
    put_shifts(taps, 2 * span, x[2])
    copies[1].wait()
    put_shifts(taps, 3 * span, x[3])
    put_shifts(taps, 4 * span, x[4])
    copies[2].wait()
    put_shifts(taps, 0, x[0])
    copies[3].wait()
    put_shifts(taps, 5 * span, x[5])
    encode_pair(taps, [0, 3 * span], w1, w2, fwt[...], edges, [0, 1], flux, [0, 1])
    group = 128 // TLAT
    for g in range(lats // 128):
        at = slice(g * 128, g * 128 + 128)
        values = [flux[0, :, at]]
        values += [flux_in[i, :, at] for i in range(1, columns - 1)]
        values += [flux[1, :, at]]
        for a, v in enumerate(swap_blocks(values, 128)):
            tiles[g * group + a] = v.astype(BF16)
            if g == lats // 128 - 1 and a == group - 1:
                north[...] = v.astype(BF16)


def edge(x, west, east, flux_in, w1, w2, fwt):
    columns, chans, lats = x.shape
    width = w2.shape[0]
    fluxes = fwt.shape[0]
    cells = columns * TLAT
    return pl.pallas_call(
        edge_kernel,
        out_shape=(
            jax.ShapeDtypeStruct((2, width, lats), BF16),
            jax.ShapeDtypeStruct((lats // TLAT, fluxes, cells), BF16),
            jax.ShapeDtypeStruct((fluxes, cells), BF16),
        ),
        in_specs=[ANY, ANY, ANY, VM, VM, VM, VM],
        out_specs=(VM, VM, VM),
        scratch_shapes=[
            pltpu.VMEM((6, chans, lats), BF16),
            pltpu.VMEM((7 * 3 * chans, lats), BF16),
            pltpu.VMEM((2, fluxes, lats), F32),
            pltpu.SemaphoreType.DMA((4,)),
        ],
        cost_estimate=pl.CostEstimate(flops=10**9, bytes_accessed=10**6, transcendentals=3 * 10**5),
        name="edge",
    )(x, west, east, flux_in, w1, w2, fwt)


def list_tiles(mask, chosen, count):
    for k in range(MAXACT):
        chosen[k] = count - 1
    for k in range(FOLDB):
        chosen[k] = count - FOLDB + k
    found = FOLDB
    for t in range(count - FOLDB):
        water = mask[t] == 1

        @pl.when(jnp.logical_and(water, found < MAXACT))
        def _():
            chosen[found] = t

        found = found + water.astype(jnp.int32)
    return found


def early_kernel(
    hid_in, edges, pair, mask, tiles, ocean_hbm, regrid_hbm, ow_hbm, cw_hbm, mw_hbm,
    hid_out, blocks, sums, base, cwt, mwt,
    ocean, ow, cw, mw, chosen, sems,
):
    count = ocean_hbm.shape[0]
    columns = hid_in.shape[0]
    small = [
        pltpu.make_async_copy(ow_hbm, ow, sems.at[0]),
        pltpu.make_async_copy(cw_hbm, cw, sems.at[1]),
        pltpu.make_async_copy(mw_hbm, mw, sems.at[2]),
    ]
    out = [
        pltpu.make_async_copy(edges.at[0], hid_out.at[0], sems.at[3]),
        pltpu.make_async_copy(edges.at[1], hid_out.at[columns - 1], sems.at[4]),
    ]
    for c in small:
        c.start()
    list_tiles(mask, chosen, count)
    loads = []
    for k in range(MAXACT):
        t = chosen[k]
        loads.append(
            (
                pltpu.make_async_copy(ocean_hbm.at[t], ocean.at[k], sems.at[5 + 2 * k]),
                pltpu.make_async_copy(regrid_hbm.at[t], blocks.at[k], sems.at[6 + 2 * k]),
            )
        )
        for c in loads[-1]:
            c.start()
    for c in out:
        c.start()
    for c in small:
        c.wait()
    cwt[...] = cw[...].astype(F32).T.astype(BF16)
    mwt[...] = mw[...].astype(F32).T.astype(BF16)
    owt = ow[...].astype(F32).T.astype(BF16)
    ones = jnp.ones(tiles.shape[1:], BF16)
    for k in range(MAXACT):
        for c in loads[k]:
            c.wait()
        mine = jnp.concatenate([tiles[pair[chosen[k], 1]], ones], 0)
        sums[k] = dot_t(mine, blocks[k, 1])
        base[k] = dot(owt, ocean[k])
    for c in out:
        c.wait()


def early(hid, edges, pair, mask, tiles, ocean, regrid, ow, cw, mw):
    count, chans, cells = ocean.shape
    width = mw.shape[0]
    fluxes = cw.shape[0]
    pairs = regrid.shape[1]
    return pl.pallas_call(
        early_kernel,
        out_shape=(
            jax.ShapeDtypeStruct(hid.shape, BF16),
            jax.ShapeDtypeStruct((MAXACT,) + regrid.shape[1:], BF16),
            jax.ShapeDtypeStruct((MAXACT, 2 * fluxes, cells), F32),
            jax.ShapeDtypeStruct((MAXACT, width, cells), F32),
            jax.ShapeDtypeStruct((width, fluxes), BF16),
            jax.ShapeDtypeStruct((width, width), BF16),
        ),
        in_specs=[ANY, VM, SM, SM, VM, ANY, ANY, ANY, ANY, ANY],
        out_specs=(ANY, VM, VM, VM, VM, VM),
        scratch_shapes=[
            pltpu.VMEM((MAXACT, chans, cells), BF16),
            pltpu.VMEM(ow.shape, BF16),
            pltpu.VMEM(cw.shape, BF16),
            pltpu.VMEM(mw.shape, BF16),
            pltpu.SMEM((MAXACT,), jnp.int32),
            pltpu.SemaphoreType.DMA((5 + 2 * MAXACT,)),
        ],
        input_output_aliases={0: 0},
        cost_estimate=pl.CostEstimate(flops=10**9, bytes_accessed=3 * 10**6, transcendentals=0),
        name="early",
    )(hid, edges, pair, mask, tiles, ocean, regrid, ow, cw, mw)


def late_kernel(
    pair, mask, west, east, fold, blocks, sums, base, cwt, mwt,
    out_hbm,
    out, zero, chosen, sems,
):
    count = out_hbm.shape[0]
    fluxes = fold.shape[0]
    zero[...] = jnp.zeros(zero.shape, BF16)
    for t in range(count - FOLDB):

        @pl.when(mask[t] != 1)
        def _():
            pltpu.make_async_copy(zero, out_hbm.at[t], sems.at[0]).start()

    found = list_tiles(mask, chosen, count)
    ones = jnp.ones(fold.shape, BF16)
    for k in range(MAXACT):
        t = chosen[k]
        total = sums[k]
        total = total + dot_t(jnp.concatenate([west[pair[t, 0]], ones], 0), blocks[k, 0])
        total = total + dot_t(jnp.concatenate([east[pair[t, 2]], ones], 0), blocks[k, 2])
        if k < FOLDB:
            total = total + dot_t(jnp.concatenate([fold[...], ones], 0), blocks[k, 3])
        regrid = (total[:fluxes] / total[fluxes : fluxes + 1]).astype(BF16)
        state = (base[k] + dot(cwt[...], regrid)).astype(BF16)
        mixed = dot(mwt[...], state)
        out[k] = (state.astype(F32) + gelu(mixed)).astype(BF16)

        @pl.when(k < found)
        def _():
            pltpu.make_async_copy(out.at[k], out_hbm.at[t], sems.at[1]).start()

    for t in range(count - FOLDB):

        @pl.when(mask[t] != 1)
        def _():
            pltpu.make_async_copy(zero, out_hbm.at[t], sems.at[0]).wait()

    for k in range(MAXACT):

        @pl.when(k < found)
        def _():
            pltpu.make_async_copy(out.at[k], out_hbm.at[0], sems.at[1]).wait()


def late(pair, mask, west, east, fold, blocks, sums, base, cwt, mwt):
    count = mask.shape[0]
    width, cells = base.shape[1:]
    return pl.pallas_call(
        late_kernel,
        out_shape=jax.ShapeDtypeStruct((count, width, cells), BF16),
        in_specs=[SM, SM, VM, VM, VM, VM, VM, VM, VM, VM],
        out_specs=ANY,
        scratch_shapes=[
            pltpu.VMEM((MAXACT, width, cells), BF16),
            pltpu.VMEM((width, cells), BF16),
            pltpu.SMEM((MAXACT,), jnp.int32),
            pltpu.SemaphoreType.DMA((2,)),
        ],
        cost_estimate=pl.CostEstimate(flops=10**9, bytes_accessed=10**6, transcendentals=3 * 10**5),
        name="late",
    )(pair, mask, west, east, fold, blocks, sums, base, cwt, mwt)


def per_device(
    atm_in,
    ocean_in,
    lift_weight,
    conv_weight,
    flux_weight,
    ocean_weight,
    couple_weight,
    mix_weight,
    regrid_weight,
    pair_tile,
    ocean_mask,
):
    columns = atm_in.shape[0]
    strips = lax.axis_size("lon")
    forward = [(i, (i + 1) % strips) for i in range(strips)]
    backward = [((i + 1) % strips, i) for i in range(strips)]
    mirror = [(i, strips - 1 - i) for i in range(strips)]
    west = lax.ppermute(atm_in[columns - 1 :], "lon", forward)
    east = lax.ppermute(atm_in[:1], "lon", backward)
    hid, flux, w1, w2, fwt = interior(atm_in, lift_weight, conv_weight, flux_weight)
    edges, tiles, north = edge(atm_in, west, east, flux, w1, w2, fwt)
    tiles_west = lax.ppermute(tiles, "lon", forward)
    tiles_east = lax.ppermute(tiles, "lon", backward)
    fold = lax.ppermute(north, "lon", mirror)
    atm_hidden, blocks, sums, base, cwt, mwt = early(
        hid, edges, pair_tile, ocean_mask, tiles, ocean_in, regrid_weight,
        ocean_weight, couple_weight, mix_weight,
    )
    ocean_hidden = late(
        pair_tile, ocean_mask, tiles_west, tiles_east, fold, blocks, sums, base, cwt, mwt
    )
    return (atm_hidden, ocean_hidden)


def solution(mesh):
    in_specs = (
        P(("groups", "lon"), None, None),
        P(("groups", "lon"), None, None),
        P(),
        P(),
        P(),
        P(),
        P(),
        P(),
        P("lon", None, None, None),
        P("lon", None),
        P("lon"),
    )
    out_specs = (P(("groups", "lon"), None, None), P(("groups", "lon"), None, None))
    return jax.shard_map(
        per_device, mesh=mesh, in_specs=in_specs, out_specs=out_specs, check_vma=False
    )
```

```python
import functools

import jax
import jax.numpy as jnp
from jax import lax
from jax.experimental import pallas as pl
from jax.experimental.pallas import tpu as pltpu
from jax.sharding import PartitionSpec as P

TLAT = 16
MAXACT = 8
FOLDB = 2
F32 = jnp.float32
BF16 = jnp.bfloat16
ROOT = 0.7978845608028654
CUBIC = ROOT * 0.044715

CHUNK = 256
STRIP = 32

HBM = pl.BlockSpec(memory_space=pltpu.HBM)
VM = pl.BlockSpec(memory_space=pltpu.VMEM)
SM = pl.BlockSpec(memory_space=pltpu.SMEM)


def dot(a, b):
    return lax.dot_general(a, b, (((1,), (0,)), ((), ())), preferred_element_type=F32)


def dot_t(a, b):
    return lax.dot_general(a, b, (((1,), (1,)), ((), ())), preferred_element_type=F32)


def gelu(x):
    half = 0.5 * x
    return half + half * jnp.tanh(x * (ROOT + CUBIC * (x * x)))


def put_shifts(taps, at, column):
    chans, lats = column.shape
    wide = column.astype(F32)
    lane = lax.broadcasted_iota(jnp.int32, wide.shape, 1)
    south = jnp.where(lane == 0, 0.0, pltpu.roll(wide, 1, 1))
    north = jnp.where(lane == lats - 1, 0.0, pltpu.roll(wide, lats - 1, 1))
    taps[:chans, at : at + lats] = south.astype(BF16)
    taps[chans : 2 * chans, at : at + lats] = column
    taps[2 * chans :, at : at + lats] = north.astype(BF16)


def join(parts, axis):
    return parts[0] if len(parts) == 1 else jnp.concatenate(parts, axis)


def multiply(segments, wc, lt, conv, lifted):
    chans = lt.shape[1]
    rows = 3 * chans
    parts = []
    for a in range(3):
        parts.append(join([seg[a][0][:, pl.ds(seg[a][1], seg[3])] for seg in segments], 1))
    parts.append(jnp.zeros((wc.shape[1] - 3 * rows, parts[0].shape[1]), BF16))
    own = join([seg[1][0][chans : 2 * chans, pl.ds(seg[1][1], seg[3])] for seg in segments], 1)
    conv[...] = dot(wc[...], jnp.concatenate(parts, 0))
    lifted[...] = dot(lt[...], own).astype(BF16)


def activate(conv, lifted, out, stores):
    for r in range(0, conv.shape[0], STRIP):
        at = slice(r, r + STRIP)
        fresh = (lifted[at, :].astype(F32) + gelu(conv[at, :])).astype(BF16)
        out[at, :] = fresh
        for ref, first, lo, hi in stores:
            ref[at, pl.ds(first, hi - lo)] = fresh[:, lo:hi]


def inner_kernel(
    x_hbm, lift_hbm, conv_hbm, fwt_hbm,
    hid_hbm, flux, taps, wc, lt,
    x, lift, conv, fwt, hid, comp, ca, cb, la, lb, oa, ob, sems,
):
    columns, chans, lats = x.shape
    width = lift.shape[1]
    copies = [
        pltpu.make_async_copy(x_hbm, x, sems.at[0]),
        pltpu.make_async_copy(lift_hbm, lift, sems.at[1]),
        pltpu.make_async_copy(fwt_hbm, fwt, sems.at[2]),
    ]
    for a in range(3):
        copies.append(pltpu.make_async_copy(conv_hbm.at[a], conv.at[a], sems.at[3 + a]))
    for c in copies:
        c.start()
    comp[pl.ds(9 * chans, 2 * width - 9 * chans), :] = jnp.zeros((2 * width - 9 * chans, width), F32)
    copies[0].wait()
    for i in range(columns):
        put_shifts(taps, i * lats, x[i])
    copies[1].wait()
    lt[...] = lift[...].astype(F32).T.astype(BF16)
    for a in range(3):
        copies[3 + a].wait()
        for b in range(3):
            comp[pl.ds((3 * a + b) * chans, chans), :] = dot(lift[...], conv[a, b])
    wc[...] = comp[...].T.astype(BF16)
    copies[2].wait()

    def feed(j, conv_to, lifted_to):
        at = [pl.multiple_of(j * CHUNK + a * lats, 128) for a in range(3)]
        multiply([[(taps, p) for p in at] + [CHUNK]], wc, lt, conv_to, lifted_to)

    def finish(j, conv_of, lifted_of, out):
        activate(conv_of, lifted_of, out, [(hid, pl.multiple_of(j * CHUNK, 128), 0, CHUNK)])

    def head(j, out):
        flux[:, pl.ds(pl.multiple_of(j * CHUNK, 128), CHUNK)] = dot(fwt[...], out[...])

    def send(column):
        return pltpu.make_async_copy(
            hid.at[:, pl.ds(pl.multiple_of(column * lats, 128), lats)], hid_hbm.at[column + 1], sems.at[0]
        )

    chunks = (columns - 2) * lats // CHUNK
    feed(0, ca, la)

    def two(i, _):
        j = 2 * i
        feed(j + 1, cb, lb)
        finish(j, ca, la, oa)
        head(jnp.maximum(j - 1, 0), ob)
        feed(jnp.minimum(j + 2, chunks - 1), ca, la)
        finish(j + 1, cb, lb, ob)
        head(j, oa)
        before = j * CHUNK // lats

        @pl.when((j + 2) * CHUNK // lats > before)
        def _():
            send(before).start()

        return 0

    lax.fori_loop(0, chunks // 2, two, 0)
    head(chunks // 2 * 2 - 1, ob)
    if chunks % 2:
        finish(chunks - 1, ca, la, oa)
        head(chunks - 1, oa)
        send(columns - 3).start()
    for i in range(columns - 2):
        send(i).wait()


def interior(x, lift, conv, fwt):
    columns, chans, lats = x.shape
    width = lift.shape[1]
    fluxes = fwt.shape[0]
    inner = (columns - 2) * lats
    x, lift, conv, fwt = [
        pltpu.with_memory_space_constraint(v, pltpu.HBM) for v in (x, lift, conv, fwt)
    ]
    return pl.pallas_call(
        inner_kernel,
        out_shape=(
            jax.ShapeDtypeStruct((columns, width, lats), BF16),
            jax.ShapeDtypeStruct((fluxes, inner), F32),
            jax.ShapeDtypeStruct((3 * chans, columns * lats), BF16),
            jax.ShapeDtypeStruct((width, 2 * width), BF16),
            jax.ShapeDtypeStruct((width, chans), BF16),
        ),
        in_specs=[HBM] * 4,
        out_specs=(HBM, VM, VM, VM, VM),
        scratch_shapes=[
            pltpu.VMEM((columns, chans, lats), BF16),
            pltpu.VMEM((chans, width), BF16),
            pltpu.VMEM((3, 3, width, width), BF16),
            pltpu.VMEM((fluxes, width), BF16),
            pltpu.VMEM((width, inner), BF16),
            pltpu.VMEM((2 * width, width), F32),
            pltpu.VMEM((width, CHUNK), F32),
            pltpu.VMEM((width, CHUNK), F32),
            pltpu.VMEM((width, CHUNK), BF16),
            pltpu.VMEM((width, CHUNK), BF16),
            pltpu.VMEM((width, CHUNK), BF16),
            pltpu.VMEM((width, CHUNK), BF16),
            pltpu.SemaphoreType.DMA((6,)),
        ],
        compiler_params=pltpu.CompilerParams(vmem_limit_bytes=16 * 2**20),
        cost_estimate=pl.CostEstimate(flops=4 * 10**9, bytes_accessed=4 * 10**6, transcendentals=10**6),
        name="interior",
    )(x, lift, conv, fwt)


def swap_blocks(values, lanes):
    count = len(values)
    lane = lax.broadcasted_iota(jnp.int32, values[0].shape, 1)
    step = count // 2
    while step:
        shift = step * TLAT
        upper = (lane & shift) != 0
        fresh = list(values)
        for i in range(count):
            if i & step:
                continue
            low, high = values[i], values[i + step]
            fresh[i] = jnp.where(upper, pltpu.roll(high, shift, 1), low)
            fresh[i + step] = jnp.where(upper, high, pltpu.roll(low, lanes - shift, 1))
        values = fresh
        step //= 2
    return values


def edge_kernel(
    west, east, flux_in, taps, wc, lt, fwt,
    edges, tiles, north,
    halo, flux, ca, cb, la, lb, oa, ob,
):
    lats = west.shape[2]
    columns = taps.shape[1] // lats
    put_shifts(halo, 0, west[0])
    put_shifts(halo, lats, east[0])
    sides = [
        [(halo, 0), (taps, 0), (taps, lats)],
        [(taps, (columns - 2) * lats), (taps, (columns - 1) * lats), (halo, lats)],
    ]
    work = []
    full = lats // CHUNK * CHUNK
    for side in range(2):
        for lo in range(0, full, CHUNK):
            work.append([(side, lo, CHUNK)])
    if full < lats:
        work.append([(0, full, lats - full), (1, full, lats - full)])
    bufs = [(ca, la, oa), (cb, lb, ob)]

    def feed(j):
        segments = []
        for side, lo, size in work[j]:
            segments.append([(ref, at + lo) for ref, at in sides[side]] + [size])
        multiply(segments, wc, lt, bufs[j % 2][0], bufs[j % 2][1])

    def finish(j):
        stores = []
        at = 0
        for side, lo, size in work[j]:
            stores.append((edges.at[side], lo, at, at + size))
            at += size
        activate(bufs[j % 2][0], bufs[j % 2][1], bufs[j % 2][2], stores)

    def head(j):
        got = dot(fwt[...], bufs[j % 2][2][...])
        at = 0
        for side, lo, size in work[j]:
            flux[side, :, lo : lo + size] = got[:, at : at + size]
            at += size

    feed(0)
    for j in range(len(work)):
        if j + 1 < len(work):
            feed(j + 1)
        finish(j)
        if j:
            head(j - 1)
    head(len(work) - 1)
    group = 128 // TLAT
    for g in range(lats // 128):
        at = slice(g * 128, g * 128 + 128)
        values = [flux[0, :, at]]
        for i in range(columns - 2):
            values.append(flux_in[:, i * lats + g * 128 : i * lats + g * 128 + 128])
        values.append(flux[1, :, at])
        for a, v in enumerate(swap_blocks(values, 128)):
            tiles[g * group + a] = v.astype(BF16)
            if g == lats // 128 - 1 and a == group - 1:
                north[...] = v.astype(BF16)


def edge(west, east, flux_in, taps, wc, lt, fwt):
    lats = west.shape[2]
    columns = taps.shape[1] // lats
    width, chans = lt.shape
    fluxes = fwt.shape[0]
    cells = columns * TLAT
    return pl.pallas_call(
        edge_kernel,
        out_shape=(
            jax.ShapeDtypeStruct((2, width, lats), BF16),
            jax.ShapeDtypeStruct((lats // TLAT, fluxes, cells), BF16),
            jax.ShapeDtypeStruct((fluxes, cells), BF16),
        ),
        in_specs=[VM] * 7,
        out_specs=(VM, VM, VM),
        scratch_shapes=[
            pltpu.VMEM((3 * chans, 2 * lats), BF16),
            pltpu.VMEM((2, fluxes, lats), F32),
            pltpu.VMEM((width, CHUNK), F32),
            pltpu.VMEM((width, CHUNK), F32),
            pltpu.VMEM((width, CHUNK), BF16),
            pltpu.VMEM((width, CHUNK), BF16),
            pltpu.VMEM((width, CHUNK), BF16),
            pltpu.VMEM((width, CHUNK), BF16),
        ],
        compiler_params=pltpu.CompilerParams(vmem_limit_bytes=12 * 2**20),
        cost_estimate=pl.CostEstimate(flops=10**9, bytes_accessed=10**6, transcendentals=3 * 10**5),
        name="edge",
    )(west, east, flux_in, taps, wc, lt, fwt)


def list_tiles(mask, chosen, count):
    for k in range(MAXACT):
        chosen[k] = count - 1
    for k in range(FOLDB):
        chosen[k] = count - FOLDB + k
    found = FOLDB
    for t in range(count - FOLDB):
        water = mask[t] == 1

        @pl.when(jnp.logical_and(water, found < MAXACT))
        def _():
            chosen[found] = t

        found = found + water.astype(jnp.int32)
    return found


def early_kernel(
    hid_in, edges, pair, mask, tiles, ocean, regrid, ow, cw, mw,
    hid_out, sums, base, cwt, mwt,
    chosen, sems,
):
    count = ocean.shape[0]
    columns = hid_in.shape[0]
    out = [
        pltpu.make_async_copy(edges.at[0], hid_out.at[0], sems.at[0]),
        pltpu.make_async_copy(edges.at[1], hid_out.at[columns - 1], sems.at[1]),
    ]
    for c in out:
        c.start()
    list_tiles(mask, chosen, count)
    cwt[...] = cw[...].astype(F32).T.astype(BF16)
    mwt[...] = mw[...].astype(F32).T.astype(BF16)
    owt = ow[...].astype(F32).T.astype(BF16)
    ones = jnp.ones(tiles.shape[1:], BF16)
    for k in range(MAXACT):
        t = chosen[k]
        mine = jnp.concatenate([tiles[pair[1, t]], ones], 0)
        sums[k] = dot_t(mine, regrid[t, 1])
        base[k] = dot(owt, ocean[t])
    for c in out:
        c.wait()


def early(hid, edges, pair, mask, tiles, ocean, regrid, ow, cw, mw):
    cells = ocean.shape[2]
    width = mw.shape[0]
    fluxes = cw.shape[0]
    return pl.pallas_call(
        early_kernel,
        out_shape=(
            jax.ShapeDtypeStruct(hid.shape, BF16),
            jax.ShapeDtypeStruct((MAXACT, 2 * fluxes, cells), F32),
            jax.ShapeDtypeStruct((MAXACT, width, cells), F32),
            jax.ShapeDtypeStruct((width, fluxes), BF16),
            jax.ShapeDtypeStruct((width, width), BF16),
        ),
        in_specs=[HBM, VM, SM, SM, VM, VM, VM, VM, VM, VM],
        out_specs=(HBM, VM, VM, VM, VM),
        scratch_shapes=[
            pltpu.SMEM((MAXACT,), jnp.int32),
            pltpu.SemaphoreType.DMA((2,)),
        ],
        input_output_aliases={0: 0},
        compiler_params=pltpu.CompilerParams(vmem_limit_bytes=12 * 2**20),
        cost_estimate=pl.CostEstimate(flops=10**9, bytes_accessed=3 * 10**6, transcendentals=0),
        name="early",
    )(hid, edges, pair, mask, tiles, ocean, regrid, ow, cw, mw)


def late_kernel(
    pair, mask, west, east, fold, regrid_weight, sums, base, cwt, mwt,
    out_hbm,
    out, zero, chosen, sems,
):
    count = out_hbm.shape[0]
    fluxes = fold.shape[0]
    zero[...] = jnp.zeros(zero.shape, BF16)
    for t in range(count - FOLDB):

        @pl.when(mask[t] != 1)
        def _():
            pltpu.make_async_copy(zero, out_hbm.at[t], sems.at[0]).start()

    found = list_tiles(mask, chosen, count)
    ones = jnp.ones(fold.shape, BF16)
    for k in range(MAXACT):
        t = chosen[k]
        total = sums[k]
        total = total + dot_t(jnp.concatenate([west[pair[0, t]], ones], 0), regrid_weight[t, 0])
        total = total + dot_t(jnp.concatenate([east[pair[2, t]], ones], 0), regrid_weight[t, 2])
        if k < FOLDB:
            total = total + dot_t(jnp.concatenate([fold[...], ones], 0), regrid_weight[t, 3])
        regrid = (total[:fluxes] / total[fluxes : fluxes + 1]).astype(BF16)
        state = (base[k] + dot(cwt[...], regrid)).astype(BF16)
        mixed = dot(mwt[...], state)
        out[k] = (state.astype(F32) + gelu(mixed)).astype(BF16)
    for k in range(MAXACT):

        @pl.when(k < found)
        def _():
            pltpu.make_async_copy(out.at[k], out_hbm.at[chosen[k]], sems.at[1]).start()

    for t in range(count - FOLDB):

        @pl.when(mask[t] != 1)
        def _():
            pltpu.make_async_copy(zero, out_hbm.at[t], sems.at[0]).wait()

    for k in range(MAXACT):

        @pl.when(k < found)
        def _():
            pltpu.make_async_copy(out.at[k], out_hbm.at[0], sems.at[1]).wait()


def late(pair, mask, west, east, fold, regrid, sums, base, cwt, mwt):
    count = mask.shape[0]
    width, cells = base.shape[1:]
    return pl.pallas_call(
        late_kernel,
        out_shape=jax.ShapeDtypeStruct((count, width, cells), BF16),
        in_specs=[SM, SM, VM, VM, VM, VM, VM, VM, VM, VM],
        out_specs=HBM,
        scratch_shapes=[
            pltpu.VMEM((MAXACT, width, cells), BF16),
            pltpu.VMEM((width, cells), BF16),
            pltpu.SMEM((MAXACT,), jnp.int32),
            pltpu.SemaphoreType.DMA((2,)),
        ],
        compiler_params=pltpu.CompilerParams(vmem_limit_bytes=12 * 2**20),
        cost_estimate=pl.CostEstimate(flops=10**9, bytes_accessed=10**6, transcendentals=3 * 10**5),
        name="late",
    )(pair, mask, west, east, fold, regrid, sums, base, cwt, mwt)


def per_device(
    atm_in,
    ocean_in,
    lift_weight,
    conv_weight,
    flux_weight,
    ocean_weight,
    couple_weight,
    mix_weight,
    regrid_weight,
    pair_tile,
    ocean_mask,
):
    columns = atm_in.shape[0]
    strips = lax.axis_size("lon")
    forward = [(i, (i + 1) % strips) for i in range(strips)]
    backward = [((i + 1) % strips, i) for i in range(strips)]
    mirror = [(i, strips - 1 - i) for i in range(strips)]
    west = lax.ppermute(atm_in[columns - 1 :], "lon", forward)
    east = lax.ppermute(atm_in[:1], "lon", backward)
    fwt = flux_weight.T
    pair = pair_tile.T
    hid, flux, taps, wc, lt = interior(atm_in, lift_weight, conv_weight, fwt)
    edges, tiles, north = edge(west, east, flux, taps, wc, lt, fwt)
    tiles_west = lax.ppermute(tiles, "lon", forward)
    tiles_east = lax.ppermute(tiles, "lon", backward)
    fold = lax.ppermute(north, "lon", mirror)
    atm_hidden, sums, base, cwt, mwt = early(
        hid, edges, pair, ocean_mask, tiles, ocean_in, regrid_weight,
        ocean_weight, couple_weight, mix_weight,
    )
    ocean_hidden = late(
        pair, ocean_mask, tiles_west, tiles_east, fold, regrid_weight, sums, base, cwt, mwt
    )
    return (atm_hidden, ocean_hidden)


def solution(mesh):
    in_specs = (
        P(("groups", "lon"), None, None),
        P(("groups", "lon"), None, None),
        P(),
        P(),
        P(),
        P(),
        P(),
        P(),
        P("lon", None, None, None),
        P("lon", None),
        P("lon"),
    )
    out_specs = (P(("groups", "lon"), None, None), P(("groups", "lon"), None, None))
    return jax.shard_map(
        per_device, mesh=mesh, in_specs=in_specs, out_specs=out_specs, check_vma=False
    )
```

```python
import functools

import jax
import jax.numpy as jnp
from jax import lax
from jax.experimental import pallas as pl
from jax.experimental.pallas import tpu as pltpu
from jax.sharding import PartitionSpec as P

TLAT = 16
MAXACT = 8
FOLDB = 2
F32 = jnp.float32
BF16 = jnp.bfloat16
ROOT = 0.7978845608028654
CUBIC = ROOT * 0.044715

CHUNK = 256
STRIP = 32

HBM = pl.BlockSpec(memory_space=pltpu.HBM)
VM = pl.BlockSpec(memory_space=pltpu.VMEM)
SM = pl.BlockSpec(memory_space=pltpu.SMEM)


def dot(a, b):
    return lax.dot_general(a, b, (((1,), (0,)), ((), ())), preferred_element_type=F32)


def dot_t(a, b):
    return lax.dot_general(a, b, (((1,), (1,)), ((), ())), preferred_element_type=F32)


def gelu_of_half(half):
    return half + half * jnp.tanh(half * (2.0 * ROOT + 8.0 * CUBIC * (half * half)))


def put_shifts(taps, at, column):
    chans, lats = column.shape
    wide = column.astype(F32)
    lane = lax.broadcasted_iota(jnp.int32, wide.shape, 1)
    south = jnp.where(lane == 0, 0.0, pltpu.roll(wide, 1, 1))
    north = jnp.where(lane == lats - 1, 0.0, pltpu.roll(wide, lats - 1, 1))
    taps[:chans, pl.ds(at, lats)] = south.astype(BF16)
    taps[chans : 2 * chans, pl.ds(at, lats)] = column
    taps[2 * chans :, pl.ds(at, lats)] = north.astype(BF16)


def join(parts, axis):
    return parts[0] if len(parts) == 1 else jnp.concatenate(parts, axis)


def multiply(segments, wc, lt, conv, lifted):
    chans = lt.shape[1]
    rows = 3 * chans
    parts = []
    for a in range(3):
        parts.append(join([seg[a][0][:, pl.ds(seg[a][1], seg[3])] for seg in segments], 1))
    parts.append(jnp.zeros((wc.shape[1] - 3 * rows, parts[0].shape[1]), BF16))
    own = join([seg[1][0][chans : 2 * chans, pl.ds(seg[1][1], seg[3])] for seg in segments], 1)
    conv[...] = dot(wc[...], jnp.concatenate(parts, 0))
    lifted[...] = dot(lt[...], own).astype(BF16)


def activate(conv, lifted, out, stores):
    for r in range(0, conv.shape[0], STRIP):
        at = slice(r, r + STRIP)
        fresh = (lifted[at, :].astype(F32) + gelu_of_half(conv[at, :])).astype(BF16)
        out[at, :] = fresh
        for ref, first, lo, hi in stores:
            ref[at, pl.ds(first, hi - lo)] = fresh[:, lo:hi]


def parity():
    return lax.rem(lax.axis_index("lon"), 2)


def first_kernel(x_hbm, lift_hbm, conv_hbm, fwt_hbm, one, two, x, lift, conv, fwt, sems):
    odd = parity()
    last = x.shape[0] - 1
    copies = [
        pltpu.make_async_copy(x_hbm.at[pl.ds(last * (1 - odd), 1)], one, sems.at[0]),
        pltpu.make_async_copy(x_hbm.at[pl.ds(last * odd, 1)], two, sems.at[1]),
        pltpu.make_async_copy(x_hbm, x, sems.at[2]),
        pltpu.make_async_copy(lift_hbm, lift, sems.at[3]),
        pltpu.make_async_copy(conv_hbm, conv, sems.at[4]),
        pltpu.make_async_copy(fwt_hbm, fwt, sems.at[5]),
    ]
    for c in copies:
        c.start()
    for c in copies:
        c.wait()


def first(x, lift, conv, fwt):
    column = jax.ShapeDtypeStruct((1,) + x.shape[1:], BF16)
    given = [pltpu.with_memory_space_constraint(v, pltpu.HBM) for v in (x, lift, conv, fwt)]
    return pl.pallas_call(
        first_kernel,
        out_shape=(column, column) + tuple(jax.ShapeDtypeStruct(v.shape, BF16) for v in (x, lift, conv, fwt)),
        in_specs=[HBM] * 4,
        out_specs=(VM,) * 6,
        scratch_shapes=[pltpu.SemaphoreType.DMA((6,))],
        compiler_params=pltpu.CompilerParams(vmem_limit_bytes=4 * 2**20),
        cost_estimate=pl.CostEstimate(flops=0, bytes_accessed=3 * 10**6, transcendentals=0),
        name="first",
    )(*given)


def inner_kernel(
    x, lift, conv, fwt,
    hid, flux, taps, wc, lt,
    comp, ca, cb, la, lb, oa, ob,
):
    columns, chans, lats = x.shape
    width = lift.shape[1]
    comp[pl.ds(9 * chans, 2 * width - 9 * chans), :] = jnp.zeros((2 * width - 9 * chans, width), F32)
    half = 0.5 * lift[...]
    for a in range(3):
        for b in range(3):
            comp[pl.ds((3 * a + b) * chans, chans), :] = dot(half, conv[a, b])
    wc[...] = comp[...].T.astype(BF16)
    lt[...] = lift[...].astype(F32).T.astype(BF16)
    for i in range(columns):
        put_shifts(taps, i * lats, x[i])

    def feed(j, conv_to, lifted_to):
        at = [pl.multiple_of(j * CHUNK + a * lats, 128) for a in range(3)]
        multiply([[(taps, p) for p in at] + [CHUNK]], wc, lt, conv_to, lifted_to)

    def finish(j, conv_of, lifted_of, out):
        activate(conv_of, lifted_of, out, [(hid, pl.multiple_of(j * CHUNK, 128), 0, CHUNK)])

    def head(j, out):
        flux[:, pl.ds(pl.multiple_of(j * CHUNK, 128), CHUNK)] = dot(fwt[...], out[...])

    chunks = (columns - 2) * lats // CHUNK
    feed(0, ca, la)

    def two(i, _):
        j = 2 * i
        feed(j + 1, cb, lb)
        finish(j, ca, la, oa)
        head(jnp.maximum(j - 1, 0), ob)

        feed(jnp.minimum(j + 2, chunks - 1), ca, la)
        finish(j + 1, cb, lb, ob)
        head(j, oa)
        return 0

    lax.fori_loop(0, chunks // 2, two, 0)
    head(chunks // 2 * 2 - 1, ob)
    if chunks % 2:
        finish(chunks - 1, ca, la, oa)
        head(chunks - 1, oa)


def interior(x, lift, conv, fwt):
    columns, chans, lats = x.shape
    width = lift.shape[1]
    fluxes = fwt.shape[0]
    inner = (columns - 2) * lats
    return pl.pallas_call(
        inner_kernel,
        out_shape=(
            jax.ShapeDtypeStruct((width, inner), BF16),
            jax.ShapeDtypeStruct((fluxes, inner), F32),
            jax.ShapeDtypeStruct((3 * chans, columns * lats), BF16),
            jax.ShapeDtypeStruct((width, 2 * width), BF16),
            jax.ShapeDtypeStruct((width, chans), BF16),
        ),
        in_specs=[VM] * 4,
        out_specs=(VM,) * 5,
        scratch_shapes=[
            pltpu.VMEM((2 * width, width), F32),
            pltpu.VMEM((width, CHUNK), F32),
            pltpu.VMEM((width, CHUNK), F32),
            pltpu.VMEM((width, CHUNK), BF16),
            pltpu.VMEM((width, CHUNK), BF16),
            pltpu.VMEM((width, CHUNK), BF16),
            pltpu.VMEM((width, CHUNK), BF16),
        ],
        compiler_params=pltpu.CompilerParams(vmem_limit_bytes=12 * 2**20),
        cost_estimate=pl.CostEstimate(flops=4 * 10**9, bytes_accessed=4 * 10**6, transcendentals=10**6),
        name="interior",
    )(x, lift, conv, fwt)


def swap_blocks(values, lanes):
    count = len(values)
    lane = lax.broadcasted_iota(jnp.int32, values[0].shape, 1)
    step = count // 2
    while step:
        shift = step * TLAT
        upper = (lane & shift) != 0
        fresh = list(values)
        for i in range(count):
            if i & step:
                continue
            low, high = values[i], values[i + step]
            fresh[i] = jnp.where(upper, pltpu.roll(high, shift, 1), low)
            fresh[i + step] = jnp.where(upper, high, pltpu.roll(low, lanes - shift, 1))
        values = fresh
        step //= 2
    return values


def edge_kernel(
    one, two, flux_in, taps, wc, lt, fwt,
    edges, tiles, north,
    halo, flux, ca, cb, la, lb, oa, ob,
):
    lats = one.shape[2]
    columns = taps.shape[1] // lats
    odd = parity()
    put_shifts(halo, pl.multiple_of(lats * (1 - odd), 128), one[0])
    put_shifts(halo, pl.multiple_of(lats * odd, 128), two[0])
    sides = [
        [(halo, 0), (taps, 0), (taps, lats)],
        [(taps, (columns - 2) * lats), (taps, (columns - 1) * lats), (halo, lats)],
    ]
    work = []
    full = lats // CHUNK * CHUNK
    for side in range(2):
        for lo in range(0, full, CHUNK):
            work.append([(side, lo, CHUNK)])
    if full < lats:
        work.append([(0, full, lats - full), (1, full, lats - full)])
    bufs = [(ca, la, oa), (cb, lb, ob)]

    def feed(j):
        segments = []
        for side, lo, size in work[j]:
            segments.append([(ref, at + lo) for ref, at in sides[side]] + [size])
        multiply(segments, wc, lt, bufs[j % 2][0], bufs[j % 2][1])

    def finish(j):
        stores = []
        at = 0
        for side, lo, size in work[j]:
            stores.append((edges.at[side], lo, at, at + size))
            at += size
        activate(bufs[j % 2][0], bufs[j % 2][1], bufs[j % 2][2], stores)

    def head(j):
        got = dot(fwt[...], bufs[j % 2][2][...])
        at = 0
        for side, lo, size in work[j]:
            flux[side, :, lo : lo + size] = got[:, at : at + size]
            at += size

    feed(0)
    for j in range(len(work)):
        if j + 1 < len(work):
            feed(j + 1)
        finish(j)
        if j:
            head(j - 1)
    head(len(work) - 1)
    group = 128 // TLAT
    for g in range(lats // 128):
        at = slice(g * 128, g * 128 + 128)
        values = [flux[0, :, at]]
        for i in range(columns - 2):
            values.append(flux_in[:, i * lats + g * 128 : i * lats + g * 128 + 128])
        values.append(flux[1, :, at])
        for a, v in enumerate(swap_blocks(values, 128)):
            tiles[g * group + a] = v.astype(BF16)
            if g == lats // 128 - 1 and a == group - 1:
                north[...] = v.astype(BF16)


def edge(one, two, flux_in, taps, wc, lt, fwt):
    lats = one.shape[2]
    columns = taps.shape[1] // lats
    width, chans = lt.shape
    fluxes = fwt.shape[0]
    cells = columns * TLAT
    return pl.pallas_call(
        edge_kernel,
        out_shape=(
            jax.ShapeDtypeStruct((2, width, lats), BF16),
            jax.ShapeDtypeStruct((lats // TLAT, fluxes, cells), BF16),
            jax.ShapeDtypeStruct((fluxes, cells), BF16),
        ),
        in_specs=[VM] * 7,
        out_specs=(VM, VM, VM),
        scratch_shapes=[
            pltpu.VMEM((3 * chans, 2 * lats), BF16),
            pltpu.VMEM((2, fluxes, lats), F32),
            pltpu.VMEM((width, CHUNK), F32),
            pltpu.VMEM((width, CHUNK), F32),
            pltpu.VMEM((width, CHUNK), BF16),
            pltpu.VMEM((width, CHUNK), BF16),
            pltpu.VMEM((width, CHUNK), BF16),
            pltpu.VMEM((width, CHUNK), BF16),
        ],
        compiler_params=pltpu.CompilerParams(vmem_limit_bytes=12 * 2**20),
        cost_estimate=pl.CostEstimate(flops=10**9, bytes_accessed=10**6, transcendentals=3 * 10**5),
        name="edge",
    )(one, two, flux_in, taps, wc, lt, fwt)


def list_tiles(mask, chosen, count):
    for k in range(MAXACT):
        chosen[k] = count - 1
    for k in range(FOLDB):
        chosen[k] = count - FOLDB + k
    found = FOLDB
    for t in range(count - FOLDB):
        water = mask[t] == 1

        @pl.when(jnp.logical_and(water, found < MAXACT))
        def _():
            chosen[found] = t

        found = found + water.astype(jnp.int32)
    return found


def early_kernel(
    hid, edges, pair, mask, tiles, ocean, regrid, ow, cw, mw,
    hid_out, out_hbm, sums, base, cwt, mwt,
    zero, chosen, sems,
):
    count = ocean.shape[0]
    cells = ocean.shape[2]
    columns, _, lats = hid_out.shape
    zero[...] = jnp.zeros(zero.shape, BF16)
    out = [
        pltpu.make_async_copy(edges.at[0], hid_out.at[0], sems.at[0]),
        pltpu.make_async_copy(edges.at[1], hid_out.at[columns - 1], sems.at[1]),
    ]
    for i in range(columns - 2):
        out.append(
            pltpu.make_async_copy(hid.at[:, pl.ds(i * lats, lats)], hid_out.at[i + 1], sems.at[2 + i])
        )
    for c in out:
        c.start()
    list_tiles(mask, chosen, count)
    for t in range(count - FOLDB):

        @pl.when(mask[t] != 1)
        def _():
            pltpu.make_async_copy(zero, out_hbm.at[t], sems.at[columns]).start()

    cwt[...] = cw[...].astype(F32).T.astype(BF16)
    mwt[...] = (0.5 * mw[...].astype(F32)).T.astype(BF16)
    owt = ow[...].astype(F32).T.astype(BF16)
    ones = jnp.ones(tiles.shape[1:], BF16)
    for k in range(MAXACT):
        t = chosen[k]
        at = slice(k * cells, k * cells + cells)
        mine = jnp.concatenate([tiles[pair[1, t]], ones], 0)
        sums[:, at] = dot_t(mine, regrid[t, 1])
        base[:, at] = dot(owt, ocean[t])
    for t in range(count - FOLDB):

        @pl.when(mask[t] != 1)
        def _():
            pltpu.make_async_copy(zero, out_hbm.at[t], sems.at[columns]).wait()

    for c in out:
        c.wait()


def early(hid, edges, pair, mask, tiles, ocean, regrid, ow, cw, mw):
    count, _, cells = ocean.shape
    width = mw.shape[0]
    fluxes = cw.shape[0]
    lats = edges.shape[2]
    columns = hid.shape[1] // lats + 2
    return pl.pallas_call(
        early_kernel,
        out_shape=(
            jax.ShapeDtypeStruct((columns, width, lats), BF16),
            jax.ShapeDtypeStruct((count, width, cells), BF16),
            jax.ShapeDtypeStruct((2 * fluxes, MAXACT * cells), F32),
            jax.ShapeDtypeStruct((width, MAXACT * cells), F32),
            jax.ShapeDtypeStruct((width, fluxes), BF16),
            jax.ShapeDtypeStruct((width, width), BF16),
        ),
        in_specs=[VM, VM, SM, SM, VM, VM, VM, VM, VM, VM],
        out_specs=(HBM, HBM, VM, VM, VM, VM),
        scratch_shapes=[
            pltpu.VMEM((width, cells), BF16),
            pltpu.SMEM((MAXACT,), jnp.int32),
            pltpu.SemaphoreType.DMA((columns + 1,)),
        ],
        compiler_params=pltpu.CompilerParams(vmem_limit_bytes=12 * 2**20),
        cost_estimate=pl.CostEstimate(flops=10**9, bytes_accessed=6 * 10**6, transcendentals=0),
        name="early",
    )(hid, edges, pair, mask, tiles, ocean, regrid, ow, cw, mw)


def late_kernel(
    pair, mask, one, two, fold, regrid_weight, sums, base, cwt, mwt, given_hbm,
    out_hbm,
    state, mixed, out, chosen, sems,
):
    count = out_hbm.shape[0]
    fluxes = fold.shape[0]
    cells = out.shape[2]
    found = list_tiles(mask, chosen, count)
    odd = parity() == 1
    ones = jnp.ones(fold.shape, BF16)
    wide = 2 * cells
    totals = []
    for k in range(MAXACT):
        t = chosen[k]
        pw, pe = pair[0, t], pair[2, t]
        west = jnp.where(odd, one[pw], two[pw])
        east = jnp.where(odd, two[pe], one[pe])
        got = jnp.concatenate([jnp.concatenate([west, ones], 0), jnp.concatenate([east, ones], 0)], 1)
        weights = jnp.concatenate([regrid_weight[t, 0], regrid_weight[t, 2]], 1)
        total = sums[:, k * cells : (k + 1) * cells] + dot_t(got, weights)
        if k < FOLDB:
            total = total + dot_t(jnp.concatenate([fold[...], ones], 0), regrid_weight[t, 3])
        totals.append(total)
    for p in range(MAXACT // 2):
        at = slice(p * wide, p * wide + wide)
        total = jnp.concatenate(totals[2 * p : 2 * p + 2], 1)
        regrid = (total[:fluxes] / total[fluxes : fluxes + 1]).astype(BF16)
        state[:, at] = (base[:, at] + dot(cwt[...], regrid)).astype(BF16)

    def mix(p):
        mixed[p % 2][...] = dot(mwt[...], state[:, p * wide : p * wide + wide])

    mix(0)
    for p in range(MAXACT // 2):
        if p + 1 < MAXACT // 2:
            mix(p + 1)
        for r in range(0, state.shape[0], STRIP):
            at = slice(r, r + STRIP)
            for side in range(2):
                k = 2 * p + side
                own = state[at, k * cells : (k + 1) * cells].astype(F32)
                half = mixed[p % 2][at, side * cells : (side + 1) * cells]
                out[k, at, :] = (own + gelu_of_half(half)).astype(BF16)
        for side in range(2):
            k = 2 * p + side

            @pl.when(k < found)
            def _():
                pltpu.make_async_copy(out.at[k], out_hbm.at[chosen[k]], sems.at[k]).start()

    for k in range(MAXACT):

        @pl.when(k < found)
        def _():
            pltpu.make_async_copy(out.at[k], out_hbm.at[0], sems.at[k]).wait()


def late(pair, mask, one, two, fold, regrid, sums, base, cwt, mwt, given):
    count, width, cells = given.shape

    def body(*refs):
        head, (state, ma, mb, out, chosen, sems) = refs[:12], refs[12:]
        late_kernel(*head, state, (ma, mb), out, chosen, sems)

    return pl.pallas_call(
        body,
        out_shape=jax.ShapeDtypeStruct((count, width, cells), BF16),
        in_specs=[SM, SM, VM, VM, VM, VM, VM, VM, VM, VM, HBM],
        out_specs=HBM,
        scratch_shapes=[
            pltpu.VMEM((width, MAXACT * cells), BF16),
            pltpu.VMEM((width, 2 * cells), F32),
            pltpu.VMEM((width, 2 * cells), F32),
            pltpu.VMEM((MAXACT, width, cells), BF16),
            pltpu.SMEM((MAXACT,), jnp.int32),
            pltpu.SemaphoreType.DMA((MAXACT,)),
        ],
        input_output_aliases={10: 0},
        compiler_params=pltpu.CompilerParams(vmem_limit_bytes=12 * 2**20),
        cost_estimate=pl.CostEstimate(flops=10**9, bytes_accessed=10**6, transcendentals=3 * 10**5),
        name="late",
    )(pair, mask, one, two, fold, regrid, sums, base, cwt, mwt, given)


def per_device(
    atm_in,
    ocean_in,
    lift_weight,
    conv_weight,
    flux_weight,
    ocean_weight,
    couple_weight,
    mix_weight,
    regrid_weight,
    pair_tile,
    ocean_mask,
):
    strips = lax.axis_size("lon")
    inward = [(i, i ^ 1) for i in range(strips)]
    outward = [(i, (i + 1 if i % 2 else i - 1) % strips) for i in range(strips)]
    mirror = [(i, strips - 1 - i) for i in range(strips)]
    fwt = flux_weight.T
    pair = pair_tile.T
    send_one, send_two, x, lift, conv, fwt = first(atm_in, lift_weight, conv_weight, fwt)
    one = lax.ppermute(send_one, "lon", inward)
    two = lax.ppermute(send_two, "lon", outward)
    hid, flux, taps, wc, lt = interior(x, lift, conv, fwt)
    edges, tiles, north = edge(one, two, flux, taps, wc, lt, fwt)
    tiles_one = lax.ppermute(tiles, "lon", inward)
    tiles_two = lax.ppermute(tiles, "lon", outward)
    fold = lax.ppermute(north, "lon", mirror)
    atm_hidden, given, sums, base, cwt, mwt = early(
        hid, edges, pair, ocean_mask, tiles, ocean_in, regrid_weight,
        ocean_weight, couple_weight, mix_weight,
    )
    ocean_hidden = late(
        pair, ocean_mask, tiles_one, tiles_two, fold, regrid_weight, sums, base, cwt, mwt, given
    )
    return (atm_hidden, ocean_hidden)


def solution(mesh):
    in_specs = (
        P(("groups", "lon"), None, None),
        P(("groups", "lon"), None, None),
        P(),
        P(),
        P(),
        P(),
        P(),
        P(),
        P("lon", None, None, None),
        P("lon", None),
        P("lon"),
    )
    out_specs = (P(("groups", "lon"), None, None), P(("groups", "lon"), None, None))
    return jax.shard_map(
        per_device, mesh=mesh, in_specs=in_specs, out_specs=out_specs, check_vma=False
    )
```

```python
import functools

import jax
import jax.numpy as jnp
from jax import lax
from jax.experimental import pallas as pl
from jax.experimental.pallas import tpu as pltpu
from jax.sharding import PartitionSpec as P

TLAT = 16
MAXACT = 8
FOLDB = 2
F32 = jnp.float32
BF16 = jnp.bfloat16
ROOT = 0.7978845608028654
CUBIC = ROOT * 0.044715

CHUNK = 256
STRIP = 32
ASK = 16

HBM = pl.BlockSpec(memory_space=pltpu.HBM)
VM = pl.BlockSpec(memory_space=pltpu.VMEM)
SM = pl.BlockSpec(memory_space=pltpu.SMEM)


def dot(a, b):
    return lax.dot_general(a, b, (((1,), (0,)), ((), ())), preferred_element_type=F32)


def dot_t(a, b):
    return lax.dot_general(a, b, (((1,), (1,)), ((), ())), preferred_element_type=F32)


def gelu_of_half(half):
    return half + half * jnp.tanh(half * (2.0 * ROOT + 8.0 * CUBIC * (half * half)))


def put_shifts(taps, at, column):
    chans, lats = column.shape
    wide = column.astype(F32)
    lane = lax.broadcasted_iota(jnp.int32, wide.shape, 1)
    south = jnp.where(lane == 0, 0.0, pltpu.roll(wide, 1, 1))
    north = jnp.where(lane == lats - 1, 0.0, pltpu.roll(wide, lats - 1, 1))
    taps[:chans, pl.ds(at, lats)] = south.astype(BF16)
    taps[chans : 2 * chans, pl.ds(at, lats)] = column
    taps[2 * chans :, pl.ds(at, lats)] = north.astype(BF16)


def join(parts, axis):
    return parts[0] if len(parts) == 1 else jnp.concatenate(parts, axis)


def multiply(segments, wc, lt, conv, lifted):
    chans = lt.shape[1]
    rows = 3 * chans
    parts = []
    for a in range(3):
        parts.append(join([seg[a][0][:, pl.ds(seg[a][1], seg[3])] for seg in segments], 1))
    parts.append(jnp.zeros((wc.shape[1] - 3 * rows, parts[0].shape[1]), BF16))
    own = join([seg[1][0][chans : 2 * chans, pl.ds(seg[1][1], seg[3])] for seg in segments], 1)
    conv[...] = dot(wc[...], jnp.concatenate(parts, 0))
    lifted[...] = dot(lt[...], own).astype(BF16)


def activate(conv, lifted, out, stores):
    for r in range(0, conv.shape[0], STRIP):
        at = slice(r, r + STRIP)
        fresh = (lifted[at, :].astype(F32) + gelu_of_half(conv[at, :])).astype(BF16)
        out[at, :] = fresh
        for ref, first, lo, hi in stores:
            ref[at, pl.ds(first, hi - lo)] = fresh[:, lo:hi]


def parity():
    return lax.rem(lax.axis_index("lon"), 2)


def list_tiles(mask, chosen, count):
    for k in range(FOLDB):
        chosen[k] = count - FOLDB + k
    for k in range(FOLDB, MAXACT + 1):
        chosen[k] = count - 1
    found = jnp.int32(FOLDB)
    for t in range(count - FOLDB):
        chosen[jnp.minimum(found, MAXACT)] = t
        found = found + jnp.where(mask[t] == 1, 1, 0)
    return jnp.minimum(found, MAXACT)


def first_kernel(x_hbm, pair_hbm, mask_hbm, one, two, pair, mask, chosen, sems):
    odd = parity()
    last = x_hbm.shape[0] - 1
    chans = x_hbm.shape[1]
    copies = [
        pltpu.make_async_copy(mask_hbm, mask, sems.at[0]),
        pltpu.make_async_copy(pair_hbm, pair, sems.at[1]),
        pltpu.make_async_copy(x_hbm.at[last * (1 - odd)], one.at[pl.ds(0, chans)], sems.at[2]),
        pltpu.make_async_copy(x_hbm.at[last * odd], two.at[pl.ds(0, chans)], sems.at[3]),
    ]
    for c in copies:
        c.start()
    copies[0].wait()
    list_tiles(mask, chosen, mask.shape[0])
    copies[1].wait()
    lane = lax.broadcasted_iota(jnp.int32, (ASK, 128), 1)
    for ref, side in ((one, 2 - 2 * odd), (two, 2 * odd)):
        asked = jnp.zeros((ASK, 128), jnp.int32)
        for k in range(MAXACT):
            asked = jnp.where(lane == k, pair[side, chosen[k]], asked)
        ref[pl.ds(chans, ASK), :128] = asked.astype(F32).astype(BF16)
        ref[pl.ds(chans, ASK), 128:] = jnp.zeros((ASK, ref.shape[1] - 128), BF16)
    copies[2].wait()
    copies[3].wait()


def first(x, pair, mask):
    column = jax.ShapeDtypeStruct((x.shape[1] + ASK, x.shape[2]), BF16)
    given = [pltpu.with_memory_space_constraint(v, pltpu.HBM) for v in (x, pair, mask)]
    return pl.pallas_call(
        first_kernel,
        out_shape=(column, column),
        in_specs=[HBM] * 3,
        out_specs=(VM, VM),
        scratch_shapes=[
            pltpu.SMEM(pair.shape, jnp.int32),
            pltpu.SMEM(mask.shape, jnp.int32),
            pltpu.SMEM((MAXACT + 1,), jnp.int32),
            pltpu.SemaphoreType.DMA((4,)),
        ],
        compiler_params=pltpu.CompilerParams(vmem_limit_bytes=4 * 2**20),
        cost_estimate=pl.CostEstimate(flops=4 * 10**9, bytes_accessed=10**6, transcendentals=0),
        name="first",
    )(*given)


def inner_kernel(
    x, lift, conv, fwt,
    hid, flux, taps, wc, lt,
    comp, ca, cb, la, lb, oa, ob,
):
    columns, chans, lats = x.shape
    width = lift.shape[1]
    comp[pl.ds(9 * chans, 2 * width - 9 * chans), :] = jnp.zeros((2 * width - 9 * chans, width), F32)
    half = 0.5 * lift[...]
    for a in range(3):
        for b in range(3):
            comp[pl.ds((3 * a + b) * chans, chans), :] = dot(half, conv[a, b])
    wc[...] = comp[...].T.astype(BF16)
    lt[...] = lift[...].astype(F32).T.astype(BF16)
    for i in range(columns):
        put_shifts(taps, i * lats, x[i])

    def feed(j, conv_to, lifted_to):
        at = [pl.multiple_of(j * CHUNK + a * lats, 128) for a in range(3)]
        multiply([[(taps, p) for p in at] + [CHUNK]], wc, lt, conv_to, lifted_to)

    def finish(j, conv_of, lifted_of, out):
        activate(conv_of, lifted_of, out, [(hid, pl.multiple_of(j * CHUNK, 128), 0, CHUNK)])

    def head(j, out):
        flux[:, pl.ds(pl.multiple_of(j * CHUNK, 128), CHUNK)] = dot(fwt[...], out[...])

    chunks = (columns - 2) * lats // CHUNK
    feed(0, ca, la)

    def two(i, _):
        j = 2 * i
        feed(j + 1, cb, lb)
        finish(j, ca, la, oa)
        head(jnp.maximum(j - 1, 0), ob)

        feed(jnp.minimum(j + 2, chunks - 1), ca, la)
        finish(j + 1, cb, lb, ob)
        head(j, oa)
        return 0

    lax.fori_loop(0, chunks // 2, two, 0)
    head(chunks // 2 * 2 - 1, ob)
    if chunks % 2:
        finish(chunks - 1, ca, la, oa)
        head(chunks - 1, oa)


def interior(x, lift, conv, fwt):
    columns, chans, lats = x.shape
    width = lift.shape[1]
    fluxes = fwt.shape[0]
    inner = (columns - 2) * lats
    return pl.pallas_call(
        inner_kernel,
        out_shape=(
            jax.ShapeDtypeStruct((width, inner), BF16),
            jax.ShapeDtypeStruct((fluxes, inner), F32),
            jax.ShapeDtypeStruct((3 * chans, columns * lats), BF16),
            jax.ShapeDtypeStruct((width, 2 * width), BF16),
            jax.ShapeDtypeStruct((width, chans), BF16),
        ),
        in_specs=[VM] * 4,
        out_specs=(VM,) * 5,
        scratch_shapes=[
            pltpu.VMEM((2 * width, width), F32),
            pltpu.VMEM((width, CHUNK), F32),
            pltpu.VMEM((width, CHUNK), F32),
            pltpu.VMEM((width, CHUNK), BF16),
            pltpu.VMEM((width, CHUNK), BF16),
            pltpu.VMEM((width, CHUNK), BF16),
            pltpu.VMEM((width, CHUNK), BF16),
        ],
        compiler_params=pltpu.CompilerParams(vmem_limit_bytes=12 * 2**20),
        cost_estimate=pl.CostEstimate(flops=4 * 10**9, bytes_accessed=4 * 10**6, transcendentals=10**6),
        name="interior",
    )(x, lift, conv, fwt)


def swap_blocks(values, lanes):
    count = len(values)
    lane = lax.broadcasted_iota(jnp.int32, values[0].shape, 1)
    step = count // 2
    while step:
        shift = step * TLAT
        upper = (lane & shift) != 0
        fresh = list(values)
        for i in range(count):
            if i & step:
                continue
            low, high = values[i], values[i + step]
            fresh[i] = jnp.where(upper, pltpu.roll(high, shift, 1), low)
            fresh[i + step] = jnp.where(upper, high, pltpu.roll(low, lanes - shift, 1))
        values = fresh
        step //= 2
    return values


def edge_kernel(
    one, two, flux_in, taps, wc, lt, fwt,
    edges, tiles, north, send_one, send_two,
    halo, flux, ca, cb, la, lb, oa, ob, asked, ask_one, ask_two, sems,
):
    lats = one.shape[1]
    chans = lt.shape[1]
    columns = taps.shape[1] // lats
    lists = []
    for i, (ref, to) in enumerate(((one, ask_one), (two, ask_two))):
        wanted = ref[pl.ds(chans, ASK), :128].astype(F32).astype(jnp.int32)
        asked[pl.ds(i * ASK, ASK), :] = jnp.clip(wanted, 0, lats // TLAT - 1)
        lists.append(pltpu.make_async_copy(asked.at[pl.ds(i * ASK, 8)], to, sems.at[i]))
        lists[-1].start()
    odd = parity()
    put_shifts(halo, pl.multiple_of(lats * (1 - odd), 128), one[pl.ds(0, chans), :])
    put_shifts(halo, pl.multiple_of(lats * odd, 128), two[pl.ds(0, chans), :])
    sides = [
        [(halo, 0), (taps, 0), (taps, lats)],
        [(taps, (columns - 2) * lats), (taps, (columns - 1) * lats), (halo, lats)],
    ]
    work = []
    full = lats // CHUNK * CHUNK
    for side in range(2):
        for lo in range(0, full, CHUNK):
            work.append([(side, lo, CHUNK)])
    if full < lats:
        work.append([(0, full, lats - full), (1, full, lats - full)])
    bufs = [(ca, la, oa), (cb, lb, ob)]

    def feed(j):
        segments = []
        for side, lo, size in work[j]:
            segments.append([(ref, at + lo) for ref, at in sides[side]] + [size])
        multiply(segments, wc, lt, bufs[j % 2][0], bufs[j % 2][1])

    def finish(j):
        stores = []
        at = 0
        for side, lo, size in work[j]:
            stores.append((edges.at[side], lo, at, at + size))
            at += size
        activate(bufs[j % 2][0], bufs[j % 2][1], bufs[j % 2][2], stores)

    def head(j):
        got = dot(fwt[...], bufs[j % 2][2][...])
        at = 0
        for side, lo, size in work[j]:
            flux[side, :, lo : lo + size] = got[:, at : at + size]
            at += size

    feed(0)
    for j in range(len(work)):
        if j + 1 < len(work):
            feed(j + 1)
        finish(j)
        if j:
            head(j - 1)
    head(len(work) - 1)
    group = 128 // TLAT
    for g in range(lats // 128):
        at = slice(g * 128, g * 128 + 128)
        values = [flux[0, :, at]]
        for i in range(columns - 2):
            values.append(flux_in[:, i * lats + g * 128 : i * lats + g * 128 + 128])
        values.append(flux[1, :, at])
        for a, v in enumerate(swap_blocks(values, 128)):
            tiles[g * group + a] = v.astype(BF16)
            if g == lats // 128 - 1 and a == group - 1:
                north[...] = v.astype(BF16)
                send_one[MAXACT] = v.astype(BF16)
                send_two[MAXACT] = v.astype(BF16)
    for c in lists:
        c.wait()
    for k in range(MAXACT):
        send_one[k] = tiles[ask_one[0, k]]
        send_two[k] = tiles[ask_two[0, k]]


def edge(one, two, flux_in, taps, wc, lt, fwt):
    lats = one.shape[1]
    columns = taps.shape[1] // lats
    width, chans = lt.shape
    fluxes = fwt.shape[0]
    cells = columns * TLAT
    return pl.pallas_call(
        edge_kernel,
        out_shape=(
            jax.ShapeDtypeStruct((2, width, lats), BF16),
            jax.ShapeDtypeStruct((lats // TLAT, fluxes, cells), BF16),
            jax.ShapeDtypeStruct((fluxes, cells), BF16),
            jax.ShapeDtypeStruct((MAXACT + 1, fluxes, cells), BF16),
            jax.ShapeDtypeStruct((MAXACT + 1, fluxes, cells), BF16),
        ),
        in_specs=[VM] * 7,
        out_specs=(VM,) * 5,
        scratch_shapes=[
            pltpu.VMEM((3 * chans, 2 * lats), BF16),
            pltpu.VMEM((2, fluxes, lats), F32),
            pltpu.VMEM((width, CHUNK), F32),
            pltpu.VMEM((width, CHUNK), F32),
            pltpu.VMEM((width, CHUNK), BF16),
            pltpu.VMEM((width, CHUNK), BF16),
            pltpu.VMEM((width, CHUNK), BF16),
            pltpu.VMEM((width, CHUNK), BF16),
            pltpu.VMEM((2 * ASK, 128), jnp.int32),
            pltpu.SMEM((8, 128), jnp.int32),
            pltpu.SMEM((8, 128), jnp.int32),
            pltpu.SemaphoreType.DMA((2,)),
        ],
        compiler_params=pltpu.CompilerParams(vmem_limit_bytes=12 * 2**20),
        cost_estimate=pl.CostEstimate(flops=10**9, bytes_accessed=10**6, transcendentals=3 * 10**5),
        name="edge",
    )(one, two, flux_in, taps, wc, lt, fwt)


def early_kernel(
    hid, edges, pair, mask, tiles, ocean, regrid, ow, cw, mw,
    hid_out, out_hbm, sums, base, cwt, mwt,
    zero, chosen, sems,
):
    count = ocean.shape[0]
    cells = ocean.shape[2]
    columns, _, lats = hid_out.shape
    zero[...] = jnp.zeros(zero.shape, BF16)
    out = [
        pltpu.make_async_copy(edges.at[0], hid_out.at[0], sems.at[0]),
        pltpu.make_async_copy(edges.at[1], hid_out.at[columns - 1], sems.at[1]),
    ]
    for i in range(columns - 2):
        out.append(
            pltpu.make_async_copy(hid.at[:, pl.ds(i * lats, lats)], hid_out.at[i + 1], sems.at[2 + i])
        )
    for c in out:
        c.start()
    list_tiles(mask, chosen, count)
    for t in range(count - FOLDB):

        @pl.when(mask[t] != 1)
        def _():
            pltpu.make_async_copy(zero, out_hbm.at[t], sems.at[columns]).start()

    cwt[...] = cw[...].astype(F32).T.astype(BF16)
    mwt[...] = (0.5 * mw[...].astype(F32)).T.astype(BF16)
    owt = ow[...].astype(F32).T.astype(BF16)
    ones = jnp.ones(tiles.shape[1:], BF16)
    for k in range(MAXACT):
        t = chosen[k]
        at = slice(k * cells, k * cells + cells)
        mine = jnp.concatenate([tiles[pair[1, t]], ones], 0)
        sums[:, at] = dot_t(mine, regrid[t, 1])
        base[:, at] = dot(owt, ocean[t])
    for t in range(count - FOLDB):

        @pl.when(mask[t] != 1)
        def _():
            pltpu.make_async_copy(zero, out_hbm.at[t], sems.at[columns]).wait()

    for c in out:
        c.wait()


def early(hid, edges, pair, mask, tiles, ocean, regrid, ow, cw, mw):
    count, _, cells = ocean.shape
    width = mw.shape[0]
    fluxes = cw.shape[0]
    lats = edges.shape[2]
    columns = hid.shape[1] // lats + 2
    return pl.pallas_call(
        early_kernel,
        out_shape=(
            jax.ShapeDtypeStruct((columns, width, lats), BF16),
            jax.ShapeDtypeStruct((count, width, cells), BF16),
            jax.ShapeDtypeStruct((2 * fluxes, MAXACT * cells), F32),
            jax.ShapeDtypeStruct((width, MAXACT * cells), F32),
            jax.ShapeDtypeStruct((width, fluxes), BF16),
            jax.ShapeDtypeStruct((width, width), BF16),
        ),
        in_specs=[VM, VM, SM, SM, VM, VM, VM, VM, VM, VM],
        out_specs=(HBM, HBM, VM, VM, VM, VM),
        scratch_shapes=[
            pltpu.VMEM((width, cells), BF16),
            pltpu.SMEM((MAXACT + 1,), jnp.int32),
            pltpu.SemaphoreType.DMA((columns + 1,)),
        ],
        compiler_params=pltpu.CompilerParams(vmem_limit_bytes=12 * 2**20),
        cost_estimate=pl.CostEstimate(flops=10**9, bytes_accessed=6 * 10**6, transcendentals=0),
        name="early",
    )(hid, edges, pair, mask, tiles, ocean, regrid, ow, cw, mw)


def late_kernel(
    mask, one, two, fold, regrid_weight, sums, base, cwt, mwt, given_hbm,
    out_hbm,
    state, mixed, out, chosen, sems,
):
    count = out_hbm.shape[0]
    fluxes = fold.shape[0]
    cells = out.shape[2]
    found = list_tiles(mask, chosen, count)
    strip, strips = lax.axis_index("lon"), lax.axis_size("lon")
    odd = lax.rem(strip, 2)
    met = lax.rem(strip + 2 * odd - 1 + strips, strips) == strips - 1 - strip
    odd = odd == 1
    partner = jnp.where(met, two[MAXACT], fold[...])
    ones = jnp.ones(fold.shape, BF16)
    wide = 2 * cells
    totals = []
    for k in range(MAXACT):
        t = chosen[k]
        west = jnp.where(odd, one[k], two[k])
        east = jnp.where(odd, two[k], one[k])
        got = jnp.concatenate([jnp.concatenate([west, ones], 0), jnp.concatenate([east, ones], 0)], 1)
        weights = jnp.concatenate([regrid_weight[t, 0], regrid_weight[t, 2]], 1)
        total = sums[:, k * cells : (k + 1) * cells] + dot_t(got, weights)
        if k < FOLDB:
            total = total + dot_t(jnp.concatenate([partner, ones], 0), regrid_weight[t, 3])
        totals.append(total)
    for p in range(MAXACT // 2):
        at = slice(p * wide, p * wide + wide)
        total = jnp.concatenate(totals[2 * p : 2 * p + 2], 1)
        regrid = (total[:fluxes] / total[fluxes : fluxes + 1]).astype(BF16)
        state[:, at] = (base[:, at] + dot(cwt[...], regrid)).astype(BF16)

    def mix(p):
        mixed[p % 2][...] = dot(mwt[...], state[:, p * wide : p * wide + wide])

    mix(0)
    for p in range(MAXACT // 2):
        if p + 1 < MAXACT // 2:
            mix(p + 1)
        for r in range(0, state.shape[0], STRIP):
            at = slice(r, r + STRIP)
            for side in range(2):
                k = 2 * p + side
                own = state[at, k * cells : (k + 1) * cells].astype(F32)
                half = mixed[p % 2][at, side * cells : (side + 1) * cells]
                out[k, at, :] = (own + gelu_of_half(half)).astype(BF16)
        for side in range(2):
            k = 2 * p + side

            @pl.when(k < found)
            def _():
                pltpu.make_async_copy(out.at[k], out_hbm.at[chosen[k]], sems.at[k]).start()

    for k in range(MAXACT):

        @pl.when(k < found)
        def _():
            pltpu.make_async_copy(out.at[k], out_hbm.at[0], sems.at[k]).wait()


def late(mask, one, two, fold, regrid, sums, base, cwt, mwt, given):
    count, width, cells = given.shape

    def body(*refs):
        head, (state, ma, mb, out, chosen, sems) = refs[:11], refs[11:]
        late_kernel(*head, state, (ma, mb), out, chosen, sems)

    return pl.pallas_call(
        body,
        out_shape=jax.ShapeDtypeStruct((count, width, cells), BF16),
        in_specs=[SM, VM, VM, VM, VM, VM, VM, VM, VM, HBM],
        out_specs=HBM,
        scratch_shapes=[
            pltpu.VMEM((width, MAXACT * cells), BF16),
            pltpu.VMEM((width, 2 * cells), F32),
            pltpu.VMEM((width, 2 * cells), F32),
            pltpu.VMEM((MAXACT, width, cells), BF16),
            pltpu.SMEM((MAXACT + 1,), jnp.int32),
            pltpu.SemaphoreType.DMA((MAXACT,)),
        ],
        input_output_aliases={9: 0},
        compiler_params=pltpu.CompilerParams(vmem_limit_bytes=12 * 2**20),
        cost_estimate=pl.CostEstimate(flops=10**9, bytes_accessed=10**6, transcendentals=3 * 10**5),
        name="late",
    )(mask, one, two, fold, regrid, sums, base, cwt, mwt, given)


def per_device(
    atm_in,
    ocean_in,
    lift_weight,
    conv_weight,
    flux_weight,
    ocean_weight,
    couple_weight,
    mix_weight,
    regrid_weight,
    pair_tile,
    ocean_mask,
):
    strips = lax.axis_size("lon")
    inward = [(i, i ^ 1) for i in range(strips)]
    outward = [(i, (i + 1 if i % 2 else i - 1) % strips) for i in range(strips)]
    met = dict(outward)
    mirror = [(i, strips - 1 - i) for i in range(strips) if met[i] != strips - 1 - i]
    fwt = flux_weight.T
    pair = pair_tile.T
    send_one, send_two = first(atm_in, pair, ocean_mask)
    two = lax.ppermute(send_two, "lon", outward)
    one = lax.ppermute(send_one, "lon", inward)
    hid, flux, taps, wc, lt = interior(atm_in, lift_weight, conv_weight, fwt)
    edges, tiles, north, send_one, send_two = edge(one, two, flux, taps, wc, lt, fwt)
    one = lax.ppermute(send_one, "lon", inward)
    two = lax.ppermute(send_two, "lon", outward)
    fold = lax.ppermute(north, "lon", mirror)
    atm_hidden, given, sums, base, cwt, mwt = early(
        hid, edges, pair, ocean_mask, tiles, ocean_in, regrid_weight,
        ocean_weight, couple_weight, mix_weight,
    )
    ocean_hidden = late(ocean_mask, one, two, fold, regrid_weight, sums, base, cwt, mwt, given)
    return (atm_hidden, ocean_hidden)


def solution(mesh):
    in_specs = (
        P(("groups", "lon"), None, None),
        P(("groups", "lon"), None, None),
        P(),
        P(),
        P(),
        P(),
        P(),
        P(),
        P("lon", None, None, None),
        P("lon", None),
        P("lon"),
    )
    out_specs = (P(("groups", "lon"), None, None), P(("groups", "lon"), None, None))
    return jax.shard_map(
        per_device, mesh=mesh, in_specs=in_specs, out_specs=out_specs, check_vma=False
    )
```

```python
import jax
import jax.numpy as jnp
from jax import lax
from jax.experimental import pallas as pl
from jax.experimental.pallas import tpu as pltpu
from jax.sharding import PartitionSpec as P


TLAT = 16
MAXACT = 8
FOLDB = 2
F32 = jnp.float32
BF16 = jnp.bfloat16
ROOT = 0.7978845608028654
CUBIC = ROOT * 0.044715

CHUNK = 256
STRIP = 32
ASK = 16

HBM = pl.BlockSpec(memory_space=pltpu.HBM)
VM = pl.BlockSpec(memory_space=pltpu.VMEM)
SM = pl.BlockSpec(memory_space=pltpu.SMEM)


def dot(a, b):
    return lax.dot_general(a, b, (((1,), (0,)), ((), ())), preferred_element_type=F32)


def dot_t(a, b):
    return lax.dot_general(a, b, (((1,), (1,)), ((), ())), preferred_element_type=F32)


def gelu_of_half(half):
    return half + half * jnp.tanh(half * (2.0 * ROOT + 8.0 * CUBIC * (half * half)))


def put_shifts(taps, at, column):
    chans, lats = column.shape
    wide = column.astype(F32)
    lane = lax.broadcasted_iota(jnp.int32, wide.shape, 1)
    south = jnp.where(lane == 0, 0.0, pltpu.roll(wide, 1, 1))
    north = jnp.where(lane == lats - 1, 0.0, pltpu.roll(wide, lats - 1, 1))
    taps[:chans, pl.ds(at, lats)] = south.astype(BF16)
    taps[chans : 2 * chans, pl.ds(at, lats)] = column
    taps[2 * chans :, pl.ds(at, lats)] = north.astype(BF16)


def join(parts, axis):
    return parts[0] if len(parts) == 1 else jnp.concatenate(parts, axis)


def multiply(segments, wc, lt, conv, lifted):
    chans = lt.shape[1]
    rows = 3 * chans
    parts = []
    for a in range(3):
        parts.append(join([seg[a][0][:, pl.ds(seg[a][1], seg[3])] for seg in segments], 1))
    parts.append(jnp.zeros((wc.shape[1] - 3 * rows, parts[0].shape[1]), BF16))
    own = join([seg[1][0][chans : 2 * chans, pl.ds(seg[1][1], seg[3])] for seg in segments], 1)
    conv[...] = dot(wc[...], jnp.concatenate(parts, 0))
    lifted[...] = dot(lt[...], own).astype(BF16)


def activate(conv, lifted, out, stores):
    for r in range(0, conv.shape[0], STRIP):
        at = slice(r, r + STRIP)
        fresh = (lifted[at, :].astype(F32) + gelu_of_half(conv[at, :])).astype(BF16)
        out[at, :] = fresh
        for ref, first, lo, hi in stores:
            ref[at, pl.ds(first, hi - lo)] = fresh[:, lo:hi]


def parity():
    return lax.rem(lax.axis_index("lon"), 2)


def list_tiles(mask, chosen, count):
    for k in range(FOLDB):
        chosen[k] = count - FOLDB + k
    for k in range(FOLDB, MAXACT + 1):
        chosen[k] = count - 1
    found = jnp.int32(FOLDB)
    for t in range(count - FOLDB):
        chosen[jnp.minimum(found, MAXACT)] = t
        found = found + jnp.where(mask[t] == 1, 1, 0)
    return jnp.minimum(found, MAXACT)


def first_kernel(x_hbm, pair_hbm, mask_hbm, one, two, pair, mask, chosen, sems):
    odd = parity()
    last = x_hbm.shape[0] - 1
    chans = x_hbm.shape[1]
    copies = [
        pltpu.make_async_copy(mask_hbm, mask, sems.at[0]),
        pltpu.make_async_copy(pair_hbm, pair, sems.at[1]),
        pltpu.make_async_copy(x_hbm.at[last * (1 - odd)], one.at[pl.ds(0, chans)], sems.at[2]),
        pltpu.make_async_copy(x_hbm.at[last * odd], two.at[pl.ds(0, chans)], sems.at[3]),
    ]
    for c in copies:
        c.start()
    copies[0].wait()
    list_tiles(mask, chosen, mask.shape[0])
    copies[1].wait()
    lane = lax.broadcasted_iota(jnp.int32, (ASK, 128), 1)
    for ref, side in ((one, 2 - 2 * odd), (two, 2 * odd)):
        asked = jnp.zeros((ASK, 128), jnp.int32)
        for k in range(MAXACT):
            asked = jnp.where(lane == k, pair[side, chosen[k]], asked)
        ref[pl.ds(chans, ASK), :128] = asked.astype(F32).astype(BF16)
        ref[pl.ds(chans, ASK), 128:] = jnp.zeros((ASK, ref.shape[1] - 128), BF16)
    copies[2].wait()
    copies[3].wait()


def first(x, pair, mask):
    column = jax.ShapeDtypeStruct((x.shape[1] + ASK, x.shape[2]), BF16)
    given = [pltpu.with_memory_space_constraint(v, pltpu.HBM) for v in (x, pair, mask)]
    return pl.pallas_call(
        first_kernel,
        out_shape=(column, column),
        in_specs=[HBM] * 3,
        out_specs=(VM, VM),
        scratch_shapes=[
            pltpu.SMEM(pair.shape, jnp.int32),
            pltpu.SMEM(mask.shape, jnp.int32),
            pltpu.SMEM((MAXACT + 1,), jnp.int32),
            pltpu.SemaphoreType.DMA((4,)),
        ],
        compiler_params=pltpu.CompilerParams(vmem_limit_bytes=4 * 2**20),
        cost_estimate=pl.CostEstimate(flops=4 * 10**9, bytes_accessed=10**6, transcendentals=0),
        name="first",
    )(*given)


def inner_kernel(
    x, lift, conv, fwt,
    hid, flux, taps, wc, lt,
    comp, ca, cb, la, lb, oa, ob,
):
    columns, chans, lats = x.shape
    width = lift.shape[1]
    comp[pl.ds(9 * chans, 2 * width - 9 * chans), :] = jnp.zeros((2 * width - 9 * chans, width), F32)
    half = 0.5 * lift[...]
    for a in range(3):
        for b in range(3):
            comp[pl.ds((3 * a + b) * chans, chans), :] = dot(half, conv[a, b])
    wc[...] = comp[...].T.astype(BF16)
    lt[...] = lift[...].astype(F32).T.astype(BF16)
    for i in range(columns):
        put_shifts(taps, i * lats, x[i])

    def feed(j, conv_to, lifted_to):
        at = [pl.multiple_of(j * CHUNK + a * lats, 128) for a in range(3)]
        multiply([[(taps, p) for p in at] + [CHUNK]], wc, lt, conv_to, lifted_to)

    def finish(j, conv_of, lifted_of, out):
        activate(conv_of, lifted_of, out, [(hid, pl.multiple_of(j * CHUNK, 128), 0, CHUNK)])

    def head(j, out):
        flux[:, pl.ds(pl.multiple_of(j * CHUNK, 128), CHUNK)] = dot(fwt[...], out[...])

    chunks = (columns - 2) * lats // CHUNK
    feed(0, ca, la)

    def two(i, _):
        j = 2 * i
        feed(j + 1, cb, lb)
        finish(j, ca, la, oa)
        head(jnp.maximum(j - 1, 0), ob)

        feed(jnp.minimum(j + 2, chunks - 1), ca, la)
        finish(j + 1, cb, lb, ob)
        head(j, oa)
        return 0

    lax.fori_loop(0, chunks // 2, two, 0)
    head(chunks // 2 * 2 - 1, ob)
    if chunks % 2:
        finish(chunks - 1, ca, la, oa)
        head(chunks - 1, oa)


def interior(x, lift, conv, fwt):
    columns, chans, lats = x.shape
    width = lift.shape[1]
    fluxes = fwt.shape[0]
    inner = (columns - 2) * lats
    return pl.pallas_call(
        inner_kernel,
        out_shape=(
            jax.ShapeDtypeStruct((width, inner), BF16),
            jax.ShapeDtypeStruct((fluxes, inner), F32),
            jax.ShapeDtypeStruct((3 * chans, columns * lats), BF16),
            jax.ShapeDtypeStruct((width, 2 * width), BF16),
            jax.ShapeDtypeStruct((width, chans), BF16),
        ),
        in_specs=[VM] * 4,
        out_specs=(VM,) * 5,
        scratch_shapes=[
            pltpu.VMEM((2 * width, width), F32),
            pltpu.VMEM((width, CHUNK), F32),
            pltpu.VMEM((width, CHUNK), F32),
            pltpu.VMEM((width, CHUNK), BF16),
            pltpu.VMEM((width, CHUNK), BF16),
            pltpu.VMEM((width, CHUNK), BF16),
            pltpu.VMEM((width, CHUNK), BF16),
        ],
        compiler_params=pltpu.CompilerParams(vmem_limit_bytes=12 * 2**20),
        cost_estimate=pl.CostEstimate(flops=4 * 10**9, bytes_accessed=4 * 10**6, transcendentals=10**6),
        name="interior",
    )(x, lift, conv, fwt)


def swap_blocks(values, lanes):
    count = len(values)
    lane = lax.broadcasted_iota(jnp.int32, values[0].shape, 1)
    step = count // 2
    while step:
        shift = step * TLAT
        upper = (lane & shift) != 0
        fresh = list(values)
        for i in range(count):
            if i & step:
                continue
            low, high = values[i], values[i + step]
            fresh[i] = jnp.where(upper, pltpu.roll(high, shift, 1), low)
            fresh[i + step] = jnp.where(upper, high, pltpu.roll(low, lanes - shift, 1))
        values = fresh
        step //= 2
    return values


def edge_kernel(
    one, two, flux_in, taps, wc, lt, fwt,
    edges, tiles, north, send_one, send_two,
    halo, flux, ca, cb, la, lb, oa, ob, asked, ask_one, ask_two, sems,
):
    lats = one.shape[1]
    chans = lt.shape[1]
    columns = taps.shape[1] // lats
    lists = []
    for i, (ref, to) in enumerate(((one, ask_one), (two, ask_two))):
        wanted = ref[pl.ds(chans, ASK), :128].astype(F32).astype(jnp.int32)
        asked[pl.ds(i * ASK, ASK), :] = jnp.clip(wanted, 0, lats // TLAT - 1)
        lists.append(pltpu.make_async_copy(asked.at[pl.ds(i * ASK, 1)], to, sems.at[i]))
        lists[-1].start()
    odd = parity()
    put_shifts(halo, pl.multiple_of(lats * (1 - odd), 128), one[pl.ds(0, chans), :])
    put_shifts(halo, pl.multiple_of(lats * odd, 128), two[pl.ds(0, chans), :])
    sides = [
        [(halo, 0), (taps, 0), (taps, lats)],
        [(taps, (columns - 2) * lats), (taps, (columns - 1) * lats), (halo, lats)],
    ]
    work = []
    full = lats // CHUNK * CHUNK
    for side in range(2):
        for lo in range(0, full, CHUNK):
            work.append([(side, lo, CHUNK)])
    if full < lats:
        work.append([(0, full, lats - full), (1, full, lats - full)])
    bufs = [(ca, la, oa), (cb, lb, ob)]

    def feed(j):
        segments = []
        for side, lo, size in work[j]:
            segments.append([(ref, at + lo) for ref, at in sides[side]] + [size])
        multiply(segments, wc, lt, bufs[j % 2][0], bufs[j % 2][1])

    def finish(j):
        stores = []
        at = 0
        for side, lo, size in work[j]:
            stores.append((edges.at[side], lo, at, at + size))
            at += size
        activate(bufs[j % 2][0], bufs[j % 2][1], bufs[j % 2][2], stores)

    def head(j):
        got = dot(fwt[...], bufs[j % 2][2][...])
        at = 0
        for side, lo, size in work[j]:
            flux[side, :, lo : lo + size] = got[:, at : at + size]
            at += size

    feed(0)
    for j in range(len(work)):
        if j + 1 < len(work):
            feed(j + 1)
        finish(j)
        if j:
            head(j - 1)
    head(len(work) - 1)
    group = 128 // TLAT
    for g in range(lats // 128):
        at = slice(g * 128, g * 128 + 128)
        values = [flux[0, :, at]]
        for i in range(columns - 2):
            values.append(flux_in[:, i * lats + g * 128 : i * lats + g * 128 + 128])
        values.append(flux[1, :, at])
        for a, v in enumerate(swap_blocks(values, 128)):
            tiles[g * group + a] = v.astype(BF16)
            if g == lats // 128 - 1 and a == group - 1:
                north[...] = v.astype(BF16)
                send_one[MAXACT] = v.astype(BF16)
                send_two[MAXACT] = v.astype(BF16)
    for c in lists:
        c.wait()
    for k in range(MAXACT):
        send_one[k] = tiles[ask_one[0, k]]
        send_two[k] = tiles[ask_two[0, k]]


def edge(one, two, flux_in, taps, wc, lt, fwt):
    lats = one.shape[1]
    columns = taps.shape[1] // lats
    width, chans = lt.shape
    fluxes = fwt.shape[0]
    cells = columns * TLAT
    return pl.pallas_call(
        edge_kernel,
        out_shape=(
            jax.ShapeDtypeStruct((2, width, lats), BF16),
            jax.ShapeDtypeStruct((lats // TLAT, fluxes, cells), BF16),
            jax.ShapeDtypeStruct((fluxes, cells), BF16),
            jax.ShapeDtypeStruct((MAXACT + 1, fluxes, cells), BF16),
            jax.ShapeDtypeStruct((MAXACT + 1, fluxes, cells), BF16),
        ),
        in_specs=[VM] * 7,
        out_specs=(VM,) * 5,
        scratch_shapes=[
            pltpu.VMEM((3 * chans, 2 * lats), BF16),
            pltpu.VMEM((2, fluxes, lats), F32),
            pltpu.VMEM((width, CHUNK), F32),
            pltpu.VMEM((width, CHUNK), F32),
            pltpu.VMEM((width, CHUNK), BF16),
            pltpu.VMEM((width, CHUNK), BF16),
            pltpu.VMEM((width, CHUNK), BF16),
            pltpu.VMEM((width, CHUNK), BF16),
            pltpu.VMEM((2 * ASK, 128), jnp.int32),
            pltpu.SMEM((1, 128), jnp.int32),
            pltpu.SMEM((1, 128), jnp.int32),
            pltpu.SemaphoreType.DMA((2,)),
        ],
        compiler_params=pltpu.CompilerParams(vmem_limit_bytes=12 * 2**20),
        cost_estimate=pl.CostEstimate(flops=10**9, bytes_accessed=10**6, transcendentals=3 * 10**5),
        name="edge",
    )(one, two, flux_in, taps, wc, lt, fwt)


def early_kernel(
    hid, edges, pair, mask, tiles, ocean, regrid, ow, cw, mw,
    hid_out, out_hbm, sums, base, cwt, mwt,
    zero, chosen, sems,
):
    count = ocean.shape[0]
    cells = ocean.shape[2]
    columns, _, lats = hid_out.shape
    zero[...] = jnp.zeros(zero.shape, BF16)
    out = [
        pltpu.make_async_copy(edges.at[0], hid_out.at[0], sems.at[0]),
        pltpu.make_async_copy(edges.at[1], hid_out.at[columns - 1], sems.at[1]),
    ]
    for i in range(columns - 2):
        out.append(
            pltpu.make_async_copy(hid.at[:, pl.ds(i * lats, lats)], hid_out.at[i + 1], sems.at[2 + i])
        )
    for c in out:
        c.start()
    list_tiles(mask, chosen, count)
    for t in range(count - FOLDB):

        @pl.when(mask[t] != 1)
        def _():
            pltpu.make_async_copy(zero, out_hbm.at[t], sems.at[columns]).start()

    cwt[...] = cw[...].astype(F32).T.astype(BF16)
    mwt[...] = (0.5 * mw[...].astype(F32)).T.astype(BF16)
    owt = ow[...].astype(F32).T.astype(BF16)
    ones = jnp.ones(tiles.shape[1:], BF16)
    for k in range(MAXACT):
        t = chosen[k]
        at = slice(k * cells, k * cells + cells)
        mine = jnp.concatenate([tiles[pair[1, t]], ones], 0)
        sums[:, at] = dot_t(mine, regrid[t, 1])
        base[:, at] = dot(owt, ocean[t])
    for t in range(count - FOLDB):

        @pl.when(mask[t] != 1)
        def _():
            pltpu.make_async_copy(zero, out_hbm.at[t], sems.at[columns]).wait()

    for c in out:
        c.wait()


def early(hid, edges, pair, mask, tiles, ocean, regrid, ow, cw, mw):
    count, _, cells = ocean.shape
    width = mw.shape[0]
    fluxes = cw.shape[0]
    lats = edges.shape[2]
    columns = hid.shape[1] // lats + 2
    return pl.pallas_call(
        early_kernel,
        out_shape=(
            jax.ShapeDtypeStruct((columns, width, lats), BF16),
            jax.ShapeDtypeStruct((count, width, cells), BF16),
            jax.ShapeDtypeStruct((2 * fluxes, MAXACT * cells), F32),
            jax.ShapeDtypeStruct((width, MAXACT * cells), F32),
            jax.ShapeDtypeStruct((width, fluxes), BF16),
            jax.ShapeDtypeStruct((width, width), BF16),
        ),
        in_specs=[VM, VM, SM, SM, VM, VM, VM, VM, VM, VM],
        out_specs=(HBM, HBM, VM, VM, VM, VM),
        scratch_shapes=[
            pltpu.VMEM((width, cells), BF16),
            pltpu.SMEM((MAXACT + 1,), jnp.int32),
            pltpu.SemaphoreType.DMA((columns + 1,)),
        ],
        compiler_params=pltpu.CompilerParams(vmem_limit_bytes=12 * 2**20),
        cost_estimate=pl.CostEstimate(flops=10**9, bytes_accessed=6 * 10**6, transcendentals=0),
        name="early",
    )(hid, edges, pair, mask, tiles, ocean, regrid, ow, cw, mw)


def late_kernel(
    mask, one, two, fold, regrid_weight, sums, base, cwt, mwt, given_hbm,
    out_hbm,
    state, mixed, out, chosen, sems,
):
    count = out_hbm.shape[0]
    fluxes = fold.shape[0]
    cells = out.shape[2]
    found = list_tiles(mask, chosen, count)
    strip, strips = lax.axis_index("lon"), lax.axis_size("lon")
    odd = lax.rem(strip, 2)
    met = lax.rem(strip + 2 * odd - 1 + strips, strips) == strips - 1 - strip
    odd = odd == 1
    partner = jnp.where(met, two[MAXACT], fold[...])
    ones = jnp.ones(fold.shape, BF16)
    wide = 2 * cells
    totals = []
    for k in range(MAXACT):
        t = chosen[k]
        west = jnp.where(odd, one[k], two[k])
        east = jnp.where(odd, two[k], one[k])
        got = jnp.concatenate([jnp.concatenate([west, ones], 0), jnp.concatenate([east, ones], 0)], 1)
        weights = jnp.concatenate([regrid_weight[t, 0], regrid_weight[t, 2]], 1)
        total = sums[:, k * cells : (k + 1) * cells] + dot_t(got, weights)
        if k < FOLDB:
            total = total + dot_t(jnp.concatenate([partner, ones], 0), regrid_weight[t, 3])
        totals.append(total)
    for p in range(MAXACT // 2):
        at = slice(p * wide, p * wide + wide)
        total = jnp.concatenate(totals[2 * p : 2 * p + 2], 1)
        regrid = (total[:fluxes] / total[fluxes : fluxes + 1]).astype(BF16)
        state[:, at] = (base[:, at] + dot(cwt[...], regrid)).astype(BF16)

    def mix(p):
        mixed[p % 2][...] = dot(mwt[...], state[:, p * wide : p * wide + wide])

    mix(0)
    for p in range(MAXACT // 2):
        if p + 1 < MAXACT // 2:
            mix(p + 1)
        for r in range(0, state.shape[0], STRIP):
            at = slice(r, r + STRIP)
            for side in range(2):
                k = 2 * p + side
                own = state[at, k * cells : (k + 1) * cells].astype(F32)
                half = mixed[p % 2][at, side * cells : (side + 1) * cells]
                out[k, at, :] = (own + gelu_of_half(half)).astype(BF16)
        for side in range(2):
            k = 2 * p + side

            @pl.when(k < found)
            def _():
                pltpu.make_async_copy(out.at[k], out_hbm.at[chosen[k]], sems.at[k]).start()

    for k in range(MAXACT):

        @pl.when(k < found)
        def _():
            pltpu.make_async_copy(out.at[k], out_hbm.at[0], sems.at[k]).wait()


def late(mask, one, two, fold, regrid, sums, base, cwt, mwt, given):
    count, width, cells = given.shape

    def body(*refs):
        head, (state, ma, mb, out, chosen, sems) = refs[:11], refs[11:]
        late_kernel(*head, state, (ma, mb), out, chosen, sems)

    return pl.pallas_call(
        body,
        out_shape=jax.ShapeDtypeStruct((count, width, cells), BF16),
        in_specs=[SM, VM, VM, VM, VM, VM, VM, VM, VM, HBM],
        out_specs=HBM,
        scratch_shapes=[
            pltpu.VMEM((width, MAXACT * cells), BF16),
            pltpu.VMEM((width, 2 * cells), F32),
            pltpu.VMEM((width, 2 * cells), F32),
            pltpu.VMEM((MAXACT, width, cells), BF16),
            pltpu.SMEM((MAXACT + 1,), jnp.int32),
            pltpu.SemaphoreType.DMA((MAXACT,)),
        ],
        input_output_aliases={9: 0},
        compiler_params=pltpu.CompilerParams(vmem_limit_bytes=12 * 2**20),
        cost_estimate=pl.CostEstimate(flops=10**9, bytes_accessed=10**6, transcendentals=3 * 10**5),
        name="late",
    )(mask, one, two, fold, regrid, sums, base, cwt, mwt, given)


def per_device(
    atm_in,
    ocean_in,
    lift_weight,
    conv_weight,
    flux_weight,
    ocean_weight,
    couple_weight,
    mix_weight,
    regrid_weight,
    pair_tile,
    ocean_mask,
):
    strips = lax.axis_size("lon")
    inward = [(i, i ^ 1) for i in range(strips)]
    outward = [(i, (i + 1 if i % 2 else i - 1) % strips) for i in range(strips)]
    met = dict(outward)
    mirror = [(i, strips - 1 - i) for i in range(strips) if met[i] != strips - 1 - i]
    fwt = flux_weight.T
    pair = pair_tile.T
    send_one, send_two = first(atm_in, pair, ocean_mask)
    two = lax.ppermute(send_two, "lon", outward)
    one = lax.ppermute(send_one, "lon", inward)
    hid, flux, taps, wc, lt = interior(atm_in, lift_weight, conv_weight, fwt)
    edges, tiles, north, send_one, send_two = edge(one, two, flux, taps, wc, lt, fwt)
    one = lax.ppermute(send_one, "lon", inward)
    two = lax.ppermute(send_two, "lon", outward)
    fold = lax.ppermute(north, "lon", mirror)
    atm_hidden, given, sums, base, cwt, mwt = early(
        hid, edges, pair, ocean_mask, tiles, ocean_in, regrid_weight,
        ocean_weight, couple_weight, mix_weight,
    )
    ocean_hidden = late(ocean_mask, one, two, fold, regrid_weight, sums, base, cwt, mwt, given)
    return (atm_hidden, ocean_hidden)


def solution(mesh):
    in_specs = (
        P(("groups", "lon"), None, None),
        P(("groups", "lon"), None, None),
        P(),
        P(),
        P(),
        P(),
        P(),
        P(),
        P("lon", None, None, None),
        P("lon", None),
        P("lon"),
    )
    out_specs = (P(("groups", "lon"), None, None), P(("groups", "lon"), None, None))

    return jax.shard_map(
        per_device, mesh=mesh, in_specs=in_specs, out_specs=out_specs, check_vma=False
    )
```

```python
import jax
import jax.numpy as jnp
from jax import lax
from jax.experimental import pallas as pl
from jax.experimental.pallas import tpu as pltpu
from jax.sharding import PartitionSpec as P


TLAT = 16
MAXACT = 8
FOLDB = 2
F32 = jnp.float32
BF16 = jnp.bfloat16
ROOT = 0.7978845608028654
CUBIC = ROOT * 0.044715

CHUNK = 256
STRIP = 32
ASK = 16

HBM = pl.BlockSpec(memory_space=pltpu.HBM)
VM = pl.BlockSpec(memory_space=pltpu.VMEM)
SM = pl.BlockSpec(memory_space=pltpu.SMEM)


def dot(a, b):
    return lax.dot_general(a, b, (((1,), (0,)), ((), ())), preferred_element_type=F32)


def dot_t(a, b):
    return lax.dot_general(a, b, (((1,), (1,)), ((), ())), preferred_element_type=F32)


def gelu_of_half(half):
    return half + half * jnp.tanh(half * (2.0 * ROOT + 8.0 * CUBIC * (half * half)))


def put_shifts(taps, at, column):
    chans, lats = column.shape
    wide = column.astype(F32)
    lane = lax.broadcasted_iota(jnp.int32, wide.shape, 1)
    south = jnp.where(lane == 0, 0.0, pltpu.roll(wide, 1, 1))
    north = jnp.where(lane == lats - 1, 0.0, pltpu.roll(wide, lats - 1, 1))
    taps[:chans, pl.ds(at, lats)] = south.astype(BF16)
    taps[chans : 2 * chans, pl.ds(at, lats)] = column
    taps[2 * chans :, pl.ds(at, lats)] = north.astype(BF16)


def join(parts, axis):
    return parts[0] if len(parts) == 1 else jnp.concatenate(parts, axis)


def multiply(segments, wc, lt, conv, lifted):
    chans = lt.shape[1]
    rows = 3 * chans
    parts = []
    for a in range(3):
        parts.append(join([seg[a][0][:, pl.ds(seg[a][1], seg[3])] for seg in segments], 1))
    parts.append(jnp.zeros((wc.shape[1] - 3 * rows, parts[0].shape[1]), BF16))
    own = join([seg[1][0][chans : 2 * chans, pl.ds(seg[1][1], seg[3])] for seg in segments], 1)
    conv[...] = dot(wc[...], jnp.concatenate(parts, 0))
    lifted[...] = dot(lt[...], own).astype(BF16)


def activate(conv, lifted, out, stores):
    for r in range(0, conv.shape[0], STRIP):
        at = slice(r, r + STRIP)
        fresh = (lifted[at, :].astype(F32) + gelu_of_half(conv[at, :])).astype(BF16)
        out[at, :] = fresh
        for ref, first, lo, hi in stores:
            ref[at, pl.ds(first, hi - lo)] = fresh[:, lo:hi]


def parity():
    return lax.rem(lax.axis_index("lon"), 2)


def list_tiles(mask, chosen, count):
    for k in range(FOLDB):
        chosen[k] = count - FOLDB + k
    for k in range(FOLDB, MAXACT + 1):
        chosen[k] = count - 1
    found = jnp.int32(FOLDB)
    for t in range(count - FOLDB):
        chosen[jnp.minimum(found, MAXACT)] = t
        found = found + jnp.where(mask[t] == 1, 1, 0)
    return jnp.minimum(found, MAXACT)


def first_kernel(x_hbm, pair_hbm, mask_hbm, one, two, pair, mask, chosen, sems):
    odd = parity()
    last = x_hbm.shape[0] - 1
    chans = x_hbm.shape[1]
    copies = [
        pltpu.make_async_copy(mask_hbm, mask, sems.at[0]),
        pltpu.make_async_copy(pair_hbm, pair, sems.at[1]),
        pltpu.make_async_copy(x_hbm.at[last * (1 - odd)], one.at[pl.ds(0, chans)], sems.at[2]),
        pltpu.make_async_copy(x_hbm.at[last * odd], two.at[pl.ds(0, chans)], sems.at[3]),
    ]
    for c in copies:
        c.start()
    copies[0].wait()
    list_tiles(mask, chosen, mask.shape[0])
    copies[1].wait()
    lane = lax.broadcasted_iota(jnp.int32, (ASK, 128), 1)
    for ref, side in ((one, 2 - 2 * odd), (two, 2 * odd)):
        asked = jnp.zeros((ASK, 128), jnp.int32)
        for k in range(MAXACT):
            asked = jnp.where(lane == k, pair[side, chosen[k]], asked)
        ref[pl.ds(chans, ASK), :128] = asked.astype(F32).astype(BF16)
        ref[pl.ds(chans, ASK), 128:] = jnp.zeros((ASK, ref.shape[1] - 128), BF16)
    copies[2].wait()
    copies[3].wait()


def first(x, pair, mask):
    column = jax.ShapeDtypeStruct((x.shape[1] + ASK, x.shape[2]), BF16)
    given = [pltpu.with_memory_space_constraint(v, pltpu.HBM) for v in (x, pair, mask)]
    return pl.pallas_call(
        first_kernel,
        out_shape=(column, column),
        in_specs=[HBM] * 3,
        out_specs=(VM, VM),
        scratch_shapes=[
            pltpu.SMEM(pair.shape, jnp.int32),
            pltpu.SMEM(mask.shape, jnp.int32),
            pltpu.SMEM((MAXACT + 1,), jnp.int32),
            pltpu.SemaphoreType.DMA((4,)),
        ],
        compiler_params=pltpu.CompilerParams(vmem_limit_bytes=4 * 2**20),
        cost_estimate=pl.CostEstimate(flops=4 * 10**9, bytes_accessed=10**6, transcendentals=0),
        name="first",
    )(*given)


def inner_kernel(
    x, lift, conv, fwt,
    hid, flux, taps, wc, lt,
    comp, ca, cb, la, lb, oa, ob,
):
    columns, chans, lats = x.shape
    width = lift.shape[1]
    comp[pl.ds(9 * chans, 2 * width - 9 * chans), :] = jnp.zeros((2 * width - 9 * chans, width), F32)
    half = 0.5 * lift[...]
    for a in range(3):
        for b in range(3):
            comp[pl.ds((3 * a + b) * chans, chans), :] = dot(half, conv[a, b])
    wc[...] = comp[...].T.astype(BF16)
    lt[...] = lift[...].astype(F32).T.astype(BF16)
    for i in range(columns):
        put_shifts(taps, i * lats, x[i])

    def feed(j, conv_to, lifted_to):
        at = [pl.multiple_of(j * CHUNK + a * lats, 128) for a in range(3)]
        multiply([[(taps, p) for p in at] + [CHUNK]], wc, lt, conv_to, lifted_to)

    def finish(j, conv_of, lifted_of, out):
        activate(conv_of, lifted_of, out, [(hid, pl.multiple_of(j * CHUNK, 128), 0, CHUNK)])

    def head(j, out):
        flux[:, pl.ds(pl.multiple_of(j * CHUNK, 128), CHUNK)] = dot(fwt[...], out[...])

    chunks = (columns - 2) * lats // CHUNK
    feed(0, ca, la)

    def two(i, _):
        j = 2 * i
        feed(j + 1, cb, lb)
        finish(j, ca, la, oa)
        head(jnp.maximum(j - 1, 0), ob)

        feed(jnp.minimum(j + 2, chunks - 1), ca, la)
        finish(j + 1, cb, lb, ob)
        head(j, oa)
        return 0

    lax.fori_loop(0, chunks // 2, two, 0)
    head(chunks // 2 * 2 - 1, ob)
    if chunks % 2:
        finish(chunks - 1, ca, la, oa)
        head(chunks - 1, oa)


def interior(x, lift, conv, fwt):
    columns, chans, lats = x.shape
    width = lift.shape[1]
    fluxes = fwt.shape[0]
    inner = (columns - 2) * lats
    return pl.pallas_call(
        inner_kernel,
        out_shape=(
            jax.ShapeDtypeStruct((width, inner), BF16),
            jax.ShapeDtypeStruct((fluxes, inner), F32),
            jax.ShapeDtypeStruct((3 * chans, columns * lats), BF16),
            jax.ShapeDtypeStruct((width, 2 * width), BF16),
            jax.ShapeDtypeStruct((width, chans), BF16),
        ),
        in_specs=[VM] * 4,
        out_specs=(VM,) * 5,
        scratch_shapes=[
            pltpu.VMEM((2 * width, width), F32),
            pltpu.VMEM((width, CHUNK), F32),
            pltpu.VMEM((width, CHUNK), F32),
            pltpu.VMEM((width, CHUNK), BF16),
            pltpu.VMEM((width, CHUNK), BF16),
            pltpu.VMEM((width, CHUNK), BF16),
            pltpu.VMEM((width, CHUNK), BF16),
        ],
        compiler_params=pltpu.CompilerParams(vmem_limit_bytes=12 * 2**20),
        cost_estimate=pl.CostEstimate(flops=4 * 10**9, bytes_accessed=4 * 10**6, transcendentals=10**6),
        name="interior",
    )(x, lift, conv, fwt)


def swap_blocks(values, lanes):
    count = len(values)
    lane = lax.broadcasted_iota(jnp.int32, values[0].shape, 1)
    step = count // 2
    while step:
        shift = step * TLAT
        upper = (lane & shift) != 0
        fresh = list(values)
        for i in range(count):
            if i & step:
                continue
            low, high = values[i], values[i + step]
            fresh[i] = jnp.where(upper, pltpu.roll(high, shift, 1), low)
            fresh[i + step] = jnp.where(upper, high, pltpu.roll(low, lanes - shift, 1))
        values = fresh
        step //= 2
    return values


def edge_kernel(
    one, two, flux_in, taps, wc, lt, fwt,
    edges, tiles, north, send_one, send_two,
    halo, flux, ca, cb, la, lb, oa, ob,
):
    lats = one.shape[1]
    chans = lt.shape[1]
    columns = taps.shape[1] // lats
    lists = []
    for ref in (one, two):
        wanted = ref[pl.ds(chans, ASK), :128].astype(F32).astype(jnp.int32)
        wanted = jnp.clip(wanted, 0, lats // TLAT - 1)
        lists.append([wanted[0, k] for k in range(MAXACT)])
    odd = parity()
    put_shifts(halo, pl.multiple_of(lats * (1 - odd), 128), one[pl.ds(0, chans), :])
    put_shifts(halo, pl.multiple_of(lats * odd, 128), two[pl.ds(0, chans), :])
    sides = [
        [(halo, 0), (taps, 0), (taps, lats)],
        [(taps, (columns - 2) * lats), (taps, (columns - 1) * lats), (halo, lats)],
    ]
    work = []
    full = lats // CHUNK * CHUNK
    for side in range(2):
        for lo in range(0, full, CHUNK):
            work.append([(side, lo, CHUNK)])
    if full < lats:
        work.append([(0, full, lats - full), (1, full, lats - full)])
    bufs = [(ca, la, oa), (cb, lb, ob)]

    def feed(j):
        segments = []
        for side, lo, size in work[j]:
            segments.append([(ref, at + lo) for ref, at in sides[side]] + [size])
        multiply(segments, wc, lt, bufs[j % 2][0], bufs[j % 2][1])

    def finish(j):
        stores = []
        at = 0
        for side, lo, size in work[j]:
            stores.append((edges.at[side], lo, at, at + size))
            at += size
        activate(bufs[j % 2][0], bufs[j % 2][1], bufs[j % 2][2], stores)

    def head(j):
        got = dot(fwt[...], bufs[j % 2][2][...])
        at = 0
        for side, lo, size in work[j]:
            flux[side, :, lo : lo + size] = got[:, at : at + size]
            at += size

    feed(0)
    for j in range(len(work)):
        if j + 1 < len(work):
            feed(j + 1)
        finish(j)
        if j:
            head(j - 1)
    head(len(work) - 1)
    group = 128 // TLAT
    for g in range(lats // 128):
        at = slice(g * 128, g * 128 + 128)
        values = [flux[0, :, at]]
        for i in range(columns - 2):
            values.append(flux_in[:, i * lats + g * 128 : i * lats + g * 128 + 128])
        values.append(flux[1, :, at])
        for a, v in enumerate(swap_blocks(values, 128)):
            tiles[g * group + a] = v.astype(BF16)
            if g == lats // 128 - 1 and a == group - 1:
                north[...] = v.astype(BF16)
                send_one[MAXACT] = v.astype(BF16)
                send_two[MAXACT] = v.astype(BF16)
    for k in range(MAXACT):
        send_one[k] = tiles[lists[0][k]]
        send_two[k] = tiles[lists[1][k]]


def edge(one, two, flux_in, taps, wc, lt, fwt):
    lats = one.shape[1]
    columns = taps.shape[1] // lats
    width, chans = lt.shape
    fluxes = fwt.shape[0]
    cells = columns * TLAT
    return pl.pallas_call(
        edge_kernel,
        out_shape=(
            jax.ShapeDtypeStruct((2, width, lats), BF16),
            jax.ShapeDtypeStruct((lats // TLAT, fluxes, cells), BF16),
            jax.ShapeDtypeStruct((fluxes, cells), BF16),
            jax.ShapeDtypeStruct((MAXACT + 1, fluxes, cells), BF16),
            jax.ShapeDtypeStruct((MAXACT + 1, fluxes, cells), BF16),
        ),
        in_specs=[VM] * 7,
        out_specs=(VM,) * 5,
        scratch_shapes=[
            pltpu.VMEM((3 * chans, 2 * lats), BF16),
            pltpu.VMEM((2, fluxes, lats), F32),
            pltpu.VMEM((width, CHUNK), F32),
            pltpu.VMEM((width, CHUNK), F32),
            pltpu.VMEM((width, CHUNK), BF16),
            pltpu.VMEM((width, CHUNK), BF16),
            pltpu.VMEM((width, CHUNK), BF16),
            pltpu.VMEM((width, CHUNK), BF16),
        ],
        compiler_params=pltpu.CompilerParams(vmem_limit_bytes=12 * 2**20),
        cost_estimate=pl.CostEstimate(flops=10**9, bytes_accessed=10**6, transcendentals=3 * 10**5),
        name="edge",
    )(one, two, flux_in, taps, wc, lt, fwt)


def early_kernel(
    hid, edges, pair, mask, tiles, ocean, regrid, ow, cw, mw,
    hid_out, out_hbm, sums, base, cwt, mwt,
    zero, chosen, sems,
):
    count = ocean.shape[0]
    cells = ocean.shape[2]
    columns, _, lats = hid_out.shape
    zero[...] = jnp.zeros(zero.shape, BF16)
    out = [
        pltpu.make_async_copy(edges.at[0], hid_out.at[0], sems.at[0]),
        pltpu.make_async_copy(edges.at[1], hid_out.at[columns - 1], sems.at[1]),
    ]
    for i in range(columns - 2):
        out.append(
            pltpu.make_async_copy(hid.at[:, pl.ds(i * lats, lats)], hid_out.at[i + 1], sems.at[2 + i])
        )
    for c in out:
        c.start()
    list_tiles(mask, chosen, count)
    for t in range(count - FOLDB):

        @pl.when(mask[t] != 1)
        def _():
            pltpu.make_async_copy(zero, out_hbm.at[t], sems.at[columns]).start()

    cwt[...] = cw[...].astype(F32).T.astype(BF16)
    mwt[...] = (0.5 * mw[...].astype(F32)).T.astype(BF16)
    owt = ow[...].astype(F32).T.astype(BF16)
    ones = jnp.ones(tiles.shape[1:], BF16)
    for k in range(MAXACT):
        t = chosen[k]
        at = slice(k * cells, k * cells + cells)
        mine = jnp.concatenate([tiles[pair[1, t]], ones], 0)
        sums[:, at] = dot_t(mine, regrid[t, 1])
        base[:, at] = dot(owt, ocean[t])
    for t in range(count - FOLDB):

        @pl.when(mask[t] != 1)
        def _():
            pltpu.make_async_copy(zero, out_hbm.at[t], sems.at[columns]).wait()

    for c in out:
        c.wait()


def early(hid, edges, pair, mask, tiles, ocean, regrid, ow, cw, mw):
    count, _, cells = ocean.shape
    width = mw.shape[0]
    fluxes = cw.shape[0]
    lats = edges.shape[2]
    columns = hid.shape[1] // lats + 2
    return pl.pallas_call(
        early_kernel,
        out_shape=(
            jax.ShapeDtypeStruct((columns, width, lats), BF16),
            jax.ShapeDtypeStruct((count, width, cells), BF16),
            jax.ShapeDtypeStruct((2 * fluxes, MAXACT * cells), F32),
            jax.ShapeDtypeStruct((width, MAXACT * cells), F32),
            jax.ShapeDtypeStruct((width, fluxes), BF16),
            jax.ShapeDtypeStruct((width, width), BF16),
        ),
        in_specs=[VM, VM, SM, SM, VM, VM, VM, VM, VM, VM],
        out_specs=(HBM, HBM, VM, VM, VM, VM),
        scratch_shapes=[
            pltpu.VMEM((width, cells), BF16),
            pltpu.SMEM((MAXACT + 1,), jnp.int32),
            pltpu.SemaphoreType.DMA((columns + 1,)),
        ],
        compiler_params=pltpu.CompilerParams(vmem_limit_bytes=12 * 2**20),
        cost_estimate=pl.CostEstimate(flops=10**9, bytes_accessed=6 * 10**6, transcendentals=0),
        name="early",
    )(hid, edges, pair, mask, tiles, ocean, regrid, ow, cw, mw)


def late_kernel(
    mask, one, two, fold, regrid_weight, sums, base, cwt, mwt, given_hbm,
    out_hbm,
    state, mixed, out, chosen, sems,
):
    count = out_hbm.shape[0]
    fluxes = fold.shape[0]
    cells = out.shape[2]
    found = list_tiles(mask, chosen, count)
    strip, strips = lax.axis_index("lon"), lax.axis_size("lon")
    odd = lax.rem(strip, 2)
    met = lax.rem(strip + 2 * odd - 1 + strips, strips) == strips - 1 - strip
    odd = odd == 1
    partner = jnp.where(met, two[MAXACT], fold[...])
    ones = jnp.ones(fold.shape, BF16)
    wide = 2 * cells
    totals = []
    for k in range(MAXACT):
        t = chosen[k]
        west = jnp.where(odd, one[k], two[k])
        east = jnp.where(odd, two[k], one[k])
        got = jnp.concatenate([jnp.concatenate([west, ones], 0), jnp.concatenate([east, ones], 0)], 1)
        weights = jnp.concatenate([regrid_weight[t, 0], regrid_weight[t, 2]], 1)
        total = sums[:, k * cells : (k + 1) * cells] + dot_t(got, weights)
        if k < FOLDB:
            total = total + dot_t(jnp.concatenate([partner, ones], 0), regrid_weight[t, 3])
        totals.append(total)
    for p in range(MAXACT // 2):
        at = slice(p * wide, p * wide + wide)
        total = jnp.concatenate(totals[2 * p : 2 * p + 2], 1)
        regrid = (total[:fluxes] / total[fluxes : fluxes + 1]).astype(BF16)
        state[:, at] = (base[:, at] + dot(cwt[...], regrid)).astype(BF16)

    def mix(p):
        mixed[p % 2][...] = dot(mwt[...], state[:, p * wide : p * wide + wide])

    mix(0)
    for p in range(MAXACT // 2):
        if p + 1 < MAXACT // 2:
            mix(p + 1)
        for r in range(0, state.shape[0], STRIP):
            at = slice(r, r + STRIP)
            for side in range(2):
                k = 2 * p + side
                own = state[at, k * cells : (k + 1) * cells].astype(F32)
                half = mixed[p % 2][at, side * cells : (side + 1) * cells]
                out[k, at, :] = (own + gelu_of_half(half)).astype(BF16)
        for side in range(2):
            k = 2 * p + side

            @pl.when(k < found)
            def _():
                pltpu.make_async_copy(out.at[k], out_hbm.at[chosen[k]], sems.at[k]).start()

    for k in range(MAXACT):

        @pl.when(k < found)
        def _():
            pltpu.make_async_copy(out.at[k], out_hbm.at[0], sems.at[k]).wait()


def late(mask, one, two, fold, regrid, sums, base, cwt, mwt, given):
    count, width, cells = given.shape

    def body(*refs):
        head, (state, ma, mb, out, chosen, sems) = refs[:11], refs[11:]
        late_kernel(*head, state, (ma, mb), out, chosen, sems)

    return pl.pallas_call(
        body,
        out_shape=jax.ShapeDtypeStruct((count, width, cells), BF16),
        in_specs=[SM, VM, VM, VM, VM, VM, VM, VM, VM, HBM],
        out_specs=HBM,
        scratch_shapes=[
            pltpu.VMEM((width, MAXACT * cells), BF16),
            pltpu.VMEM((width, 2 * cells), F32),
            pltpu.VMEM((width, 2 * cells), F32),
            pltpu.VMEM((MAXACT, width, cells), BF16),
            pltpu.SMEM((MAXACT + 1,), jnp.int32),
            pltpu.SemaphoreType.DMA((MAXACT,)),
        ],
        input_output_aliases={9: 0},
        compiler_params=pltpu.CompilerParams(vmem_limit_bytes=12 * 2**20),
        cost_estimate=pl.CostEstimate(flops=10**9, bytes_accessed=10**6, transcendentals=3 * 10**5),
        name="late",
    )(mask, one, two, fold, regrid, sums, base, cwt, mwt, given)


def per_device(
    atm_in,
    ocean_in,
    lift_weight,
    conv_weight,
    flux_weight,
    ocean_weight,
    couple_weight,
    mix_weight,
    regrid_weight,
    pair_tile,
    ocean_mask,
):
    strips = lax.axis_size("lon")
    inward = [(i, i ^ 1) for i in range(strips)]
    outward = [(i, (i + 1 if i % 2 else i - 1) % strips) for i in range(strips)]
    met = dict(outward)
    mirror = [
        (i, (i + strips // 2) % strips if met[i] == strips - 1 - i else strips - 1 - i)
        for i in range(strips)
    ]
    fwt = flux_weight.T
    pair = pair_tile.T
    send_one, send_two = first(atm_in, pair, ocean_mask)
    two = lax.ppermute(send_two, "lon", outward)
    one = lax.ppermute(send_one, "lon", inward)
    hid, flux, taps, wc, lt = interior(atm_in, lift_weight, conv_weight, fwt)
    edges, tiles, north, send_one, send_two = edge(one, two, flux, taps, wc, lt, fwt)
    one = lax.ppermute(send_one, "lon", inward)
    two = lax.ppermute(send_two, "lon", outward)
    fold = lax.ppermute(north, "lon", mirror)
    atm_hidden, given, sums, base, cwt, mwt = early(
        hid, edges, pair, ocean_mask, tiles, ocean_in, regrid_weight,
        ocean_weight, couple_weight, mix_weight,
    )
    ocean_hidden = late(ocean_mask, one, two, fold, regrid_weight, sums, base, cwt, mwt, given)
    return (atm_hidden, ocean_hidden)


def solution(mesh):
    in_specs = (
        P(("groups", "lon"), None, None),
        P(("groups", "lon"), None, None),
        P(),
        P(),
        P(),
        P(),
        P(),
        P(),
        P("lon", None, None, None),
        P("lon", None),
        P("lon"),
    )
    out_specs = (P(("groups", "lon"), None, None), P(("groups", "lon"), None, None))

    return jax.shard_map(
        per_device, mesh=mesh, in_specs=in_specs, out_specs=out_specs, check_vma=False
    )
```

```python
import jax
import jax.numpy as jnp
from jax import lax
from jax.experimental import pallas as pl
from jax.experimental.pallas import tpu as pltpu
from jax.sharding import PartitionSpec as P


TLAT = 16
MAXACT = 8
FOLDB = 2
F32 = jnp.float32
BF16 = jnp.bfloat16
ROOT = 0.7978845608028654
CUBIC = ROOT * 0.044715

CHUNK = 256
STRIP = 32
ASK = 8

HBM = pl.BlockSpec(memory_space=pltpu.HBM)
VM = pl.BlockSpec(memory_space=pltpu.VMEM)
SM = pl.BlockSpec(memory_space=pltpu.SMEM)


def dot(a, b):
    return lax.dot_general(a, b, (((1,), (0,)), ((), ())), preferred_element_type=F32)


def dot_t(a, b):
    return lax.dot_general(a, b, (((1,), (1,)), ((), ())), preferred_element_type=F32)


def gelu_of_half(half):
    return half + half * jnp.tanh(half * (2.0 * ROOT + 8.0 * CUBIC * (half * half)))


def put_shifts(taps, at, column):
    chans, lats = column.shape
    wide = column.astype(F32)
    lane = lax.broadcasted_iota(jnp.int32, wide.shape, 1)
    south = jnp.where(lane == 0, 0.0, pltpu.roll(wide, 1, 1))
    north = jnp.where(lane == lats - 1, 0.0, pltpu.roll(wide, lats - 1, 1))
    taps[:chans, pl.ds(at, lats)] = south.astype(BF16)
    taps[chans : 2 * chans, pl.ds(at, lats)] = column
    taps[2 * chans :, pl.ds(at, lats)] = north.astype(BF16)


def join(parts, axis):
    return parts[0] if len(parts) == 1 else jnp.concatenate(parts, axis)


def multiply(segments, wc, lt, conv, lifted):
    deep = wc.shape[1] // 2
    chans = lt.shape[1]
    rows = 3 * chans
    width = sum(seg[3] for seg in segments)

    def side(a):
        parts = []
        for seg in segments:
            if seg[a] is None:
                parts.append(jnp.zeros((rows, seg[3]), BF16))
            else:
                parts.append(seg[a][0][:, pl.ds(seg[a][1], seg[3])])
        return join(parts, 1)

    def blank(count):
        return jnp.zeros((count, width), BF16)

    absent = [all(seg[a] is None for seg in segments) for a in range(3)]
    if absent[1] and absent[2]:
        conv[...] = dot(wc[:, :deep], jnp.concatenate([side(0), blank(deep - rows)], 0))
    elif absent[0] and absent[1]:
        before = 2 * rows - deep
        conv[...] = dot(
            wc[:, deep:], jnp.concatenate([blank(before), side(2), blank(deep - before - rows)], 0)
        )
    else:
        parts = [side(0), side(1), side(2), blank(2 * deep - 3 * rows)]
        conv[...] = dot(wc[...], jnp.concatenate(parts, 0))
    if lifted is not None:
        own = join([seg[1][0][chans : 2 * chans, pl.ds(seg[1][1], seg[3])] for seg in segments], 1)
        lifted[...] = dot(lt[...], own).astype(BF16)


def edge_lanes(lats):
    half = -(-lats // CHUNK)
    return half, 2 * half * CHUNK - lats


def edge_work(lats):
    work = []
    full = lats // CHUNK * CHUNK
    for lo in range(0, full, CHUNK):
        for side in range(2):
            work.append([(side, lo, CHUNK)])
    if full < lats:
        work.append([(0, full, lats - full), (1, full, lats - full)])
    return work


def activate(conv, lifted, out, stores, rest=None):
    for r in range(0, conv.shape[0], STRIP):
        at = slice(r, r + STRIP)
        half = conv[at, :] if rest is None else conv[at, :] + rest(at)
        fresh = (lifted(at).astype(F32) + gelu_of_half(half)).astype(BF16)
        out[at, :] = fresh
        for ref, first, lo, hi in stores:
            ref[at, pl.ds(first, hi - lo)] = fresh[:, lo:hi]


def parity():
    return lax.rem(lax.axis_index("lon"), 2)


def list_tiles(mask, chosen, count):
    for k in range(FOLDB):
        chosen[k] = count - FOLDB + k
    for k in range(FOLDB, MAXACT + 1):
        chosen[k] = count - 1
    found = jnp.int32(FOLDB)
    for t in range(count - FOLDB):
        chosen[jnp.minimum(found, MAXACT)] = t
        found = found + jnp.where(mask[t] == 1, 1, 0)
    return jnp.minimum(found, MAXACT)


def first_kernel(x_hbm, pair_hbm, mask_hbm, one, two, pair, mask, chosen, sems):
    odd = parity()
    last = x_hbm.shape[0] - 1
    chans = x_hbm.shape[1]
    copies = [
        pltpu.make_async_copy(mask_hbm, mask, sems.at[0]),
        pltpu.make_async_copy(pair_hbm, pair, sems.at[1]),
        pltpu.make_async_copy(x_hbm.at[last * (1 - odd)], one.at[pl.ds(0, chans)], sems.at[2]),
        pltpu.make_async_copy(x_hbm.at[last * odd], two.at[pl.ds(0, chans)], sems.at[3]),
    ]
    for c in copies:
        c.start()
    copies[0].wait()
    list_tiles(mask, chosen, mask.shape[0])
    copies[1].wait()
    lane = lax.broadcasted_iota(jnp.int32, (ASK, 128), 1)
    for ref, side in ((one, 2 - 2 * odd), (two, 2 * odd)):
        asked = jnp.zeros((ASK, 128), jnp.int32)
        for k in range(MAXACT):
            asked = jnp.where(lane == k, pair[side, chosen[k]], asked)
        ref[pl.ds(chans, ASK), :128] = asked.astype(F32).astype(BF16)
        ref[pl.ds(chans, ASK), 128:] = jnp.zeros((ASK, ref.shape[1] - 128), BF16)
    copies[2].wait()
    copies[3].wait()


def first(x, pair, mask):
    column = jax.ShapeDtypeStruct((x.shape[1] + ASK, x.shape[2]), BF16)
    given = [pltpu.with_memory_space_constraint(v, pltpu.HBM) for v in (x, pair, mask)]
    return pl.pallas_call(
        first_kernel,
        out_shape=(column, column),
        in_specs=[HBM] * 3,
        out_specs=(VM, VM),
        scratch_shapes=[
            pltpu.SMEM(pair.shape, jnp.int32),
            pltpu.SMEM(mask.shape, jnp.int32),
            pltpu.SMEM((MAXACT + 1,), jnp.int32),
            pltpu.SemaphoreType.DMA((4,)),
        ],
        compiler_params=pltpu.CompilerParams(vmem_limit_bytes=4 * 2**20),
        cost_estimate=pl.CostEstimate(flops=4 * 10**9, bytes_accessed=10**6, transcendentals=0),
        name="first",
    )(*given)


def inner_kernel(
    x, lift, conv, fwt,
    hid, flux, wc, rest, lifted,
    taps, lt, comp, ca, cb, la, lb, oa, ob,
):
    columns, chans, lats = x.shape
    width = lift.shape[1]
    comp[pl.ds(9 * chans, 2 * width - 9 * chans), :] = jnp.zeros((2 * width - 9 * chans, width), F32)
    half = 0.5 * lift[...]
    for a in range(3):
        for b in range(3):
            comp[pl.ds((3 * a + b) * chans, chans), :] = dot(half, conv[a, b])
    wc[...] = comp[...].T.astype(BF16)
    lt[...] = lift[...].astype(F32).T.astype(BF16)
    for i in (0, columns + 1):
        taps[:, i * lats : (i + 1) * lats] = jnp.zeros((3 * chans, lats), BF16)
    for i in range(columns):
        put_shifts(taps, (i + 1) * lats, x[i])

    def window(first, conv_to, lifted_to):
        at = [pl.multiple_of(first + a * lats, 128) for a in range(3)]
        multiply([[(taps, p) for p in at] + [CHUNK]], wc, lt, conv_to, lifted_to)

    def feed(j, conv_to, lifted_to):
        window(lats + j * CHUNK, conv_to, lifted_to)

    def finish(j, conv_of, lifted_of, out):
        store = (hid, pl.multiple_of(j * CHUNK, 128), 0, CHUNK)
        activate(conv_of, lambda at: lifted_of[at, :], out, [store])

    def near_edge(k):
        half, _ = edge_lanes(lats)
        k = jnp.minimum(k, 2 * half - 1)
        first = jnp.where(k < half, k * CHUNK, columns * lats + (k - 2 * half) * CHUNK)
        to = pl.ds(pl.multiple_of(k * CHUNK, 128), CHUNK)
        window(first, rest.at[:, to], lifted.at[:, to])

    def head(j, out):
        flux[:, pl.ds(pl.multiple_of(j * CHUNK, 128), CHUNK)] = dot(fwt[...], out[...])

    chunks = (columns - 2) * lats // CHUNK
    feed(0, ca, la)

    def two(i, _):
        j = 2 * i
        feed(j + 1, cb, lb)
        near_edge(i)
        finish(j, ca, la, oa)
        head(jnp.maximum(j - 1, 0), ob)

        feed(jnp.minimum(j + 2, chunks - 1), ca, la)
        finish(j + 1, cb, lb, ob)
        head(j, oa)
        return 0

    lax.fori_loop(0, chunks // 2, two, 0)
    head(chunks // 2 * 2 - 1, ob)
    if chunks % 2:
        finish(chunks - 1, ca, la, oa)
        head(chunks - 1, oa)
    for k in range(chunks // 2, 2 * edge_lanes(lats)[0]):
        near_edge(k)


def interior(x, lift, conv, fwt):
    columns, chans, lats = x.shape
    width = lift.shape[1]
    fluxes = fwt.shape[0]
    inner = (columns - 2) * lats
    pieces = 2 * edge_lanes(lats)[0] * CHUNK
    return pl.pallas_call(
        inner_kernel,
        out_shape=(
            jax.ShapeDtypeStruct((width, inner), BF16),
            jax.ShapeDtypeStruct((fluxes, inner), F32),
            jax.ShapeDtypeStruct((width, 2 * width), BF16),
            jax.ShapeDtypeStruct((width, pieces), F32),
            jax.ShapeDtypeStruct((width, pieces), BF16),
        ),
        in_specs=[VM] * 4,
        out_specs=(VM,) * 5,
        scratch_shapes=[
            pltpu.VMEM((3 * chans, (columns + 2) * lats), BF16),
            pltpu.VMEM((width, chans), BF16),
            pltpu.VMEM((2 * width, width), F32),
            pltpu.VMEM((width, CHUNK), F32),
            pltpu.VMEM((width, CHUNK), F32),
            pltpu.VMEM((width, CHUNK), BF16),
            pltpu.VMEM((width, CHUNK), BF16),
            pltpu.VMEM((width, CHUNK), BF16),
            pltpu.VMEM((width, CHUNK), BF16),
        ],
        compiler_params=pltpu.CompilerParams(vmem_limit_bytes=12 * 2**20),
        cost_estimate=pl.CostEstimate(flops=4 * 10**9, bytes_accessed=4 * 10**6, transcendentals=10**6),
        name="interior",
    )(x, lift, conv, fwt)


def swap_blocks(values, lanes):
    count = len(values)
    lane = lax.broadcasted_iota(jnp.int32, values[0].shape, 1)
    step = count // 2
    while step:
        shift = step * TLAT
        upper = (lane & shift) != 0
        fresh = list(values)
        for i in range(count):
            if i & step:
                continue
            low, high = values[i], values[i + step]
            fresh[i] = jnp.where(upper, pltpu.roll(high, shift, 1), low)
            fresh[i + step] = jnp.where(upper, high, pltpu.roll(low, lanes - shift, 1))
        values = fresh
        step //= 2
    return values


def edge_kernel(
    one, two, flux_in, wc, rest, lifted, fwt,
    edges, tiles, north, send_one, send_two,
    halo, flux, ca, cb, oa, ob,
):
    lats = one.shape[1]
    chans = one.shape[0] - ASK
    columns = flux_in.shape[1] // lats + 2
    lists = []
    for ref in (one, two):
        wanted = ref[pl.ds(chans, ASK), :128].astype(F32).astype(jnp.int32)
        wanted = jnp.clip(wanted, 0, lats // TLAT - 1)
        lists.append([wanted[0, k] for k in range(MAXACT)])
    odd = parity()
    put_shifts(halo, pl.multiple_of(lats * (1 - odd), 128), one[pl.ds(0, chans), :])
    put_shifts(halo, pl.multiple_of(lats * odd, 128), two[pl.ds(0, chans), :])
    sides = [[(halo, 0), None, None], [None, None, (halo, lats)]]
    work = edge_work(lats)
    bufs = [(ca, oa), (cb, ob)]

    def feed(j):
        segments = []
        for side, lo, size in work[j]:
            segments.append([c and (c[0], c[1] + lo) for c in sides[side]] + [size])
        multiply(segments, wc, fwt[:, :chans], bufs[j % 2][0], None)

    def finish(j):
        stores, lanes = [], []
        at = 0
        for side, lo, size in work[j]:
            stores.append((edges.at[side], lo, at, at + size))
            first = lo + side * edge_lanes(lats)[1]
            lanes.append(slice(first, first + size))
            at += size

        def read(ref):
            return lambda rows: join([ref[rows, at] for at in lanes], 1)

        activate(bufs[j % 2][0], read(lifted), bufs[j % 2][1], stores, read(rest))

    def head(j):
        got = dot(fwt[...], bufs[j % 2][1][...])
        at = 0
        for side, lo, size in work[j]:
            flux[side, :, lo : lo + size] = got[:, at : at + size]
            at += size

    group = 128 // TLAT
    north_tile = lats // TLAT - 1

    def swap(g):
        at = slice(g * 128, g * 128 + 128)
        values = [flux[0, :, at]]
        for i in range(columns - 2):
            values.append(flux_in[:, i * lats + g * 128 : i * lats + g * 128 + 128])
        values.append(flux[1, :, at])
        for a, v in enumerate(swap_blocks(values, 128)):
            tiles[g * group + a] = v.astype(BF16)
            if g * group + a == north_tile:
                for ref in (north, send_one.at[MAXACT], send_two.at[MAXACT]):
                    ref[...] = v.astype(BF16)

    ready, seen = [], [0, 0]
    for pieces in work:
        for side, lo, size in pieces:
            seen[side] = lo + size
        ready.append(min(seen) // 128)
    feed(0)
    swapped = 0
    for j in range(len(work)):
        if j + 1 < len(work):
            feed(j + 1)
        finish(j)
        if j:
            head(j - 1)
            for g in range(swapped, ready[j - 1]):
                swap(g)
            swapped = ready[j - 1]
    head(len(work) - 1)
    for g in range(swapped, lats // 128):
        swap(g)
    for k in range(MAXACT):
        send_one[k] = tiles[lists[0][k]]
        send_two[k] = tiles[lists[1][k]]


def edge(one, two, flux_in, wc, rest, lifted, fwt):
    lats = one.shape[1]
    chans = one.shape[0] - ASK
    columns = flux_in.shape[1] // lats + 2
    fluxes, width = fwt.shape
    cells = columns * TLAT
    return pl.pallas_call(
        edge_kernel,
        out_shape=(
            jax.ShapeDtypeStruct((2, width, lats), BF16),
            jax.ShapeDtypeStruct((lats // TLAT, fluxes, cells), BF16),
            jax.ShapeDtypeStruct((fluxes, cells), BF16),
            jax.ShapeDtypeStruct((MAXACT + 1, fluxes, cells), BF16),
            jax.ShapeDtypeStruct((MAXACT + 1, fluxes, cells), BF16),
        ),
        in_specs=[VM] * 7,
        out_specs=(VM,) * 5,
        scratch_shapes=[
            pltpu.VMEM((3 * chans, 2 * lats), BF16),
            pltpu.VMEM((2, fluxes, lats), F32),
            pltpu.VMEM((width, CHUNK), F32),
            pltpu.VMEM((width, CHUNK), F32),
            pltpu.VMEM((width, CHUNK), BF16),
            pltpu.VMEM((width, CHUNK), BF16),
        ],
        compiler_params=pltpu.CompilerParams(vmem_limit_bytes=12 * 2**20),
        cost_estimate=pl.CostEstimate(flops=10**9, bytes_accessed=10**6, transcendentals=3 * 10**5),
        name="edge",
    )(one, two, flux_in, wc, rest, lifted, fwt)


def early_kernel(
    hid, edges, pair, mask, tiles, ocean, regrid, ow, cw, mw,
    hid_out, out_hbm, sums, base, cwt, mwt, blocks, folds,
    zero, chosen, sems,
):
    count = ocean.shape[0]
    cells = ocean.shape[2]
    columns, _, lats = hid_out.shape
    zero[...] = jnp.zeros(zero.shape, BF16)
    out = [
        pltpu.make_async_copy(edges.at[0], hid_out.at[0], sems.at[0]),
        pltpu.make_async_copy(edges.at[1], hid_out.at[columns - 1], sems.at[1]),
    ]
    for i in range(columns - 2):
        out.append(
            pltpu.make_async_copy(hid.at[:, pl.ds(i * lats, lats)], hid_out.at[i + 1], sems.at[2 + i])
        )
    for c in out:
        c.start()
    list_tiles(mask, chosen, count)
    for t in range(count - FOLDB):

        @pl.when(mask[t] != 1)
        def _():
            pltpu.make_async_copy(zero, out_hbm.at[t], sems.at[columns]).start()

    cwt[...] = cw[...].astype(F32).T.astype(BF16)
    mwt[...] = (0.5 * mw[...].astype(F32)).T.astype(BF16)
    owt = ow[...].astype(F32).T.astype(BF16)
    ones = jnp.ones(tiles.shape[1:], BF16)
    for k in range(MAXACT):
        t = chosen[k]
        at = slice(k * cells, k * cells + cells)
        mine = jnp.concatenate([tiles[pair[1, t]], ones], 0)
        sums[:, at] = dot_t(mine, regrid[t, 1])
        base[:, at] = dot(owt, ocean[t])
        for side in range(2):
            blocks[at, side * cells : (side + 1) * cells] = regrid[t, 2 * side]
        if k < FOLDB:
            folds[at, :] = regrid[t, 3]
    for t in range(count - FOLDB):

        @pl.when(mask[t] != 1)
        def _():
            pltpu.make_async_copy(zero, out_hbm.at[t], sems.at[columns]).wait()

    for c in out:
        c.wait()


def early(hid, edges, pair, mask, tiles, ocean, regrid, ow, cw, mw):
    count, _, cells = ocean.shape
    width = mw.shape[0]
    fluxes = cw.shape[0]
    lats = edges.shape[2]
    columns = hid.shape[1] // lats + 2
    return pl.pallas_call(
        early_kernel,
        out_shape=(
            jax.ShapeDtypeStruct((columns, width, lats), BF16),
            jax.ShapeDtypeStruct((count, width, cells), BF16),
            jax.ShapeDtypeStruct((2 * fluxes, MAXACT * cells), F32),
            jax.ShapeDtypeStruct((width, MAXACT * cells), F32),
            jax.ShapeDtypeStruct((width, fluxes), BF16),
            jax.ShapeDtypeStruct((width, width), BF16),
            jax.ShapeDtypeStruct((MAXACT * cells, 2 * cells), BF16),
            jax.ShapeDtypeStruct((FOLDB * cells, cells), BF16),
        ),
        in_specs=[VM, VM, SM, SM, VM, VM, VM, VM, VM, VM],
        out_specs=(HBM, HBM) + (VM,) * 6,
        scratch_shapes=[
            pltpu.VMEM((width, cells), BF16),
            pltpu.SMEM((MAXACT + 1,), jnp.int32),
            pltpu.SemaphoreType.DMA((columns + 1,)),
        ],
        compiler_params=pltpu.CompilerParams(vmem_limit_bytes=12 * 2**20),
        cost_estimate=pl.CostEstimate(flops=10**9, bytes_accessed=6 * 10**6, transcendentals=0),
        name="early",
    )(hid, edges, pair, mask, tiles, ocean, regrid, ow, cw, mw)


def late_kernel(
    mask, one, two, fold, sums, base, cwt, mwt, blocks, folds, given_hbm,
    out_hbm,
    state, mixed_even, mixed_odd, out, chosen, sems,
):
    fluxes = fold.shape[0]
    cells = out.shape[2]
    pairs = MAXACT // 2
    wide = 2 * cells
    strip, strips = lax.axis_index("lon"), lax.axis_size("lon")
    odd = lax.rem(strip, 2)
    met = lax.rem(strip + 2 * odd - 1 + strips, strips) == strips - 1 - strip
    odd = odd == 1
    partner = jnp.where(met, two[MAXACT], fold[...])
    ones = jnp.ones(fold.shape, BF16)

    def got(k):
        west = jnp.where(odd, one[k], two[k])
        east = jnp.where(odd, two[k], one[k])
        return [jnp.concatenate([west, east], 1), jnp.concatenate([ones, ones], 1)]

    half = 2 * fluxes
    totals = []
    for p in range(pairs):
        at = slice(p * wide, p * wide + wide)
        product = dot_t(jnp.concatenate(got(2 * p) + got(2 * p + 1), 0), blocks[at, :])
        total = jnp.concatenate([product[:half, :cells], product[half:, cells:]], 1) + sums[:, at]
        if 2 * p < FOLDB:
            total = total + dot_t(jnp.concatenate([partner, ones], 0), folds[at, :])
        totals.append(total)
    for p in range(pairs):
        at = slice(p * wide, p * wide + wide)
        regrid = (totals[p][:fluxes] / totals[p][fluxes : fluxes + 1]).astype(BF16)
        state[:, at] = (base[:, at] + dot(cwt[...], regrid)).astype(BF16)

    mixed = (mixed_even, mixed_odd)

    def mix(p):
        mixed[p % 2][...] = dot(mwt[...], state[:, p * wide : p * wide + wide])

    def finish(p):
        for r in range(0, state.shape[0], STRIP):
            at = slice(r, r + STRIP)
            for side in range(2):
                k = 2 * p + side
                own = state[at, k * cells : (k + 1) * cells].astype(F32)
                half = mixed[p % 2][at, side * cells : (side + 1) * cells]
                out[k, at, :] = (own + gelu_of_half(half)).astype(BF16)

    found = list_tiles(mask, chosen, out_hbm.shape[0])
    mix(0)
    for p in range(pairs):
        if p + 1 < pairs:
            mix(p + 1)
        finish(p)
        for k in (2 * p, 2 * p + 1):

            @pl.when(k < found)
            def _():
                pltpu.make_async_copy(out.at[k], out_hbm.at[chosen[k]], sems.at[k]).start()

    for k in range(MAXACT):

        @pl.when(k < found)
        def _():
            pltpu.make_async_copy(out.at[k], out_hbm.at[0], sems.at[k]).wait()


def late(mask, one, two, fold, sums, base, cwt, mwt, blocks, folds, given):
    count, width, cells = given.shape
    return pl.pallas_call(
        late_kernel,
        out_shape=jax.ShapeDtypeStruct((count, width, cells), BF16),
        in_specs=[SM] + [VM] * 9 + [HBM],
        out_specs=HBM,
        scratch_shapes=[
            pltpu.VMEM((width, MAXACT * cells), BF16),
            pltpu.VMEM((width, 2 * cells), F32),
            pltpu.VMEM((width, 2 * cells), F32),
            pltpu.VMEM((MAXACT, width, cells), BF16),
            pltpu.SMEM((MAXACT + 1,), jnp.int32),
            pltpu.SemaphoreType.DMA((MAXACT,)),
        ],
        input_output_aliases={10: 0},
        compiler_params=pltpu.CompilerParams(vmem_limit_bytes=12 * 2**20),
        cost_estimate=pl.CostEstimate(flops=10**9, bytes_accessed=10**6, transcendentals=3 * 10**5),
        name="late",
    )(mask, one, two, fold, sums, base, cwt, mwt, blocks, folds, given)


def per_device(
    atm_in,
    ocean_in,
    lift_weight,
    conv_weight,
    flux_weight,
    ocean_weight,
    couple_weight,
    mix_weight,
    regrid_weight,
    pair_tile,
    ocean_mask,
):
    strips = lax.axis_size("lon")
    inward = [(i, i ^ 1) for i in range(strips)]
    outward = [(i, (i + 1 if i % 2 else i - 1) % strips) for i in range(strips)]
    met = dict(outward)
    mirror = [
        (i, (i + strips // 2) % strips if met[i] == strips - 1 - i else strips - 1 - i)
        for i in range(strips)
    ]
    fwt = flux_weight.T
    pair = pair_tile.T
    send_one, send_two = first(atm_in, pair, ocean_mask)
    two = lax.ppermute(send_two, "lon", outward)
    one = lax.ppermute(send_one, "lon", inward)
    hid, flux, wc, rest, lifted = interior(atm_in, lift_weight, conv_weight, fwt)
    edges, tiles, north, send_one, send_two = edge(one, two, flux, wc, rest, lifted, fwt)
    one = lax.ppermute(send_one, "lon", inward)
    two = lax.ppermute(send_two, "lon", outward)
    fold = lax.ppermute(north, "lon", mirror)
    atm_hidden, given, sums, base, cwt, mwt, blocks, folds = early(
        hid, edges, pair, ocean_mask, tiles, ocean_in, regrid_weight,
        ocean_weight, couple_weight, mix_weight,
    )
    ocean_hidden = late(
        ocean_mask, one, two, fold, sums, base, cwt, mwt, blocks, folds, given
    )
    return (atm_hidden, ocean_hidden)


def solution(mesh):
    in_specs = (
        P(("groups", "lon"), None, None),
        P(("groups", "lon"), None, None),
        P(),
        P(),
        P(),
        P(),
        P(),
        P(),
        P("lon", None, None, None),
        P("lon", None),
        P("lon"),
    )
    out_specs = (P(("groups", "lon"), None, None), P(("groups", "lon"), None, None))

    return jax.shard_map(
        per_device, mesh=mesh, in_specs=in_specs, out_specs=out_specs, check_vma=False
    )
```

```python
import jax
import jax.numpy as jnp
from jax import lax
from jax.experimental import pallas as pl
from jax.experimental.pallas import tpu as pltpu
from jax.sharding import PartitionSpec as P


TLAT = 16
MAXACT = 8
FOLDB = 2
F32 = jnp.float32
BF16 = jnp.bfloat16
ROOT = 0.7978845608028654
CUBIC = ROOT * 0.044715

CHUNK = 256
STRIP = 32
ASK = 8

HBM = pl.BlockSpec(memory_space=pltpu.HBM)
VM = pl.BlockSpec(memory_space=pltpu.VMEM)
SM = pl.BlockSpec(memory_space=pltpu.SMEM)


def dot(a, b):
    return lax.dot_general(a, b, (((1,), (0,)), ((), ())), preferred_element_type=F32)


def dot_t(a, b):
    return lax.dot_general(a, b, (((1,), (1,)), ((), ())), preferred_element_type=F32)


def gelu_of_half(half):
    return half + half * jnp.tanh(half * (2.0 * ROOT + 8.0 * CUBIC * (half * half)))


def put_shifts(taps, at, column):
    chans, lats = column.shape
    lane = lax.broadcasted_iota(jnp.int32, column.shape, 1)
    zero = jnp.zeros(column.shape, BF16)
    taps[:chans, pl.ds(at, lats)] = jnp.where(lane == 0, zero, pltpu.roll(column, 1, 1))
    taps[chans : 2 * chans, pl.ds(at, lats)] = column
    taps[2 * chans :, pl.ds(at, lats)] = jnp.where(
        lane == lats - 1, zero, pltpu.roll(column, lats - 1, 1)
    )


def join(parts, axis):
    return parts[0] if len(parts) == 1 else jnp.concatenate(parts, axis)


def multiply(segments, wc, lt, conv, lifted):
    chans = lt.shape[1]
    rows = 3 * chans
    parts = []
    for a in range(3):
        parts.append(join([seg[a][0][:, pl.ds(seg[a][1], seg[3])] for seg in segments], 1))
    parts.append(jnp.zeros((wc.shape[1] - 3 * rows, parts[0].shape[1]), BF16))
    own = join([seg[1][0][chans : 2 * chans, pl.ds(seg[1][1], seg[3])] for seg in segments], 1)
    conv[...] = dot(wc[...], jnp.concatenate(parts, 0))
    lifted[...] = dot(lt[...], own).astype(BF16)


def activate(conv, lifted, out, stores):
    for r in range(0, conv.shape[0], STRIP):
        at = slice(r, r + STRIP)
        fresh = (lifted[at, :].astype(F32) + gelu_of_half(conv[at, :])).astype(BF16)
        out[at, :] = fresh
        for ref, first, lo, hi in stores:
            ref[at, pl.ds(first, hi - lo)] = fresh[:, lo:hi]


def parity():
    return lax.rem(lax.axis_index("lon"), 2)


def list_tiles(mask, chosen, count):
    for k in range(FOLDB):
        chosen[k] = count - FOLDB + k
    for k in range(FOLDB, MAXACT + 1):
        chosen[k] = count - 1
    found = jnp.int32(FOLDB)
    for t in range(count - FOLDB):
        chosen[jnp.minimum(found, MAXACT)] = t
        found = found + jnp.where(mask[t] == 1, 1, 0)
    return jnp.minimum(found, MAXACT)


def first_kernel(x_hbm, pair_hbm, mask_hbm, one, two, pair, mask, chosen, sems):
    odd = parity()
    last = x_hbm.shape[0] - 1
    chans = x_hbm.shape[1]
    copies = [
        pltpu.make_async_copy(mask_hbm, mask, sems.at[0]),
        pltpu.make_async_copy(pair_hbm, pair, sems.at[1]),
        pltpu.make_async_copy(x_hbm.at[last * (1 - odd)], one.at[pl.ds(0, chans)], sems.at[2]),
        pltpu.make_async_copy(x_hbm.at[last * odd], two.at[pl.ds(0, chans)], sems.at[3]),
    ]
    for c in copies:
        c.start()
    copies[0].wait()
    list_tiles(mask, chosen, mask.shape[0])
    copies[1].wait()
    lane = lax.broadcasted_iota(jnp.int32, (ASK, 128), 1)
    for ref, side in ((one, 2 - 2 * odd), (two, 2 * odd)):
        asked = jnp.zeros((ASK, 128), jnp.int32)
        for k in range(MAXACT):
            asked = jnp.where(lane == k, pair[side, chosen[k]], asked)
        ref[pl.ds(chans, ASK), :128] = asked.astype(F32).astype(BF16)
        ref[pl.ds(chans, ASK), 128:] = jnp.zeros((ASK, ref.shape[1] - 128), BF16)
    copies[2].wait()
    copies[3].wait()


def first(x, pair, mask):
    column = jax.ShapeDtypeStruct((x.shape[1] + ASK, x.shape[2]), BF16)
    given = [pltpu.with_memory_space_constraint(v, pltpu.HBM) for v in (x, pair, mask)]
    return pl.pallas_call(
        first_kernel,
        out_shape=(column, column),
        in_specs=[HBM] * 3,
        out_specs=(VM, VM),
        scratch_shapes=[
            pltpu.SMEM(pair.shape, jnp.int32),
            pltpu.SMEM(mask.shape, jnp.int32),
            pltpu.SMEM((MAXACT + 1,), jnp.int32),
            pltpu.SemaphoreType.DMA((4,)),
        ],
        compiler_params=pltpu.CompilerParams(vmem_limit_bytes=4 * 2**20),
        cost_estimate=pl.CostEstimate(flops=4 * 10**9, bytes_accessed=10**6, transcendentals=0),
        name="first",
    )(*given)


def inner_kernel(
    x, lift, conv, fwt,
    hid, flux, taps, wc, lt,
    comp, ca, cb, la, lb, oa, ob,
):
    columns, chans, lats = x.shape
    width = lift.shape[1]
    comp[pl.ds(9 * chans, 2 * width - 9 * chans), :] = jnp.zeros((2 * width - 9 * chans, width), F32)
    half = 0.5 * lift[...]
    for a in range(3):
        for b in range(3):
            comp[pl.ds((3 * a + b) * chans, chans), :] = dot(half, conv[a, b])
    for side in range(2):
        at = slice(side * width, side * width + width)
        wc[:, at] = comp[at, :].T.astype(BF16)
    lt[...] = lift[...].astype(F32).T.astype(BF16)
    for i in range(columns):
        put_shifts(taps, i * lats, x[i])

    def feed(j, conv_to, lifted_to):
        at = [pl.multiple_of(j * CHUNK + a * lats, 128) for a in range(3)]
        multiply([[(taps, p) for p in at] + [CHUNK]], wc, lt, conv_to, lifted_to)

    def finish(j, conv_of, lifted_of, out):
        activate(conv_of, lifted_of, out, [(hid, pl.multiple_of(j * CHUNK, 128), 0, CHUNK)])

    def head(j, out):
        flux[:, pl.ds(pl.multiple_of(j * CHUNK, 128), CHUNK)] = dot(fwt[...], out[...])

    chunks = (columns - 2) * lats // CHUNK
    feed(0, ca, la)

    def two(i, _):
        j = 2 * i
        feed(j + 1, cb, lb)
        finish(j, ca, la, oa)
        head(jnp.maximum(j - 1, 0), ob)

        feed(jnp.minimum(j + 2, chunks - 1), ca, la)
        finish(j + 1, cb, lb, ob)
        head(j, oa)
        return 0

    lax.fori_loop(0, chunks // 2, two, 0)
    head(chunks // 2 * 2 - 1, ob)
    if chunks % 2:
        finish(chunks - 1, ca, la, oa)
        head(chunks - 1, oa)


def interior(x, lift, conv, fwt):
    columns, chans, lats = x.shape
    width = lift.shape[1]
    fluxes = fwt.shape[0]
    inner = (columns - 2) * lats
    return pl.pallas_call(
        inner_kernel,
        out_shape=(
            jax.ShapeDtypeStruct((width, inner), BF16),
            jax.ShapeDtypeStruct((fluxes, inner), F32),
            jax.ShapeDtypeStruct((3 * chans, columns * lats), BF16),
            jax.ShapeDtypeStruct((width, 2 * width), BF16),
            jax.ShapeDtypeStruct((width, chans), BF16),
        ),
        in_specs=[VM] * 4,
        out_specs=(VM,) * 5,
        scratch_shapes=[
            pltpu.VMEM((2 * width, width), F32),
            pltpu.VMEM((width, CHUNK), F32),
            pltpu.VMEM((width, CHUNK), F32),
            pltpu.VMEM((width, CHUNK), BF16),
            pltpu.VMEM((width, CHUNK), BF16),
            pltpu.VMEM((width, CHUNK), BF16),
            pltpu.VMEM((width, CHUNK), BF16),
        ],
        compiler_params=pltpu.CompilerParams(vmem_limit_bytes=12 * 2**20),
        cost_estimate=pl.CostEstimate(flops=4 * 10**9, bytes_accessed=4 * 10**6, transcendentals=10**6),
        name="interior",
    )(x, lift, conv, fwt)


def swap_blocks(values, lanes):
    count = len(values)
    lane = lax.broadcasted_iota(jnp.int32, values[0].shape, 1)
    step = count // 2
    while step:
        shift = step * TLAT
        upper = (lane & shift) != 0
        fresh = list(values)
        for i in range(count):
            if i & step:
                continue
            low, high = values[i], values[i + step]
            fresh[i] = jnp.where(upper, pltpu.roll(high, shift, 1), low)
            fresh[i + step] = jnp.where(upper, high, pltpu.roll(low, lanes - shift, 1))
        values = fresh
        step //= 2
    return values


def edge_kernel(
    one, two, flux_in, taps, wc, lt, fwt,
    edges, tiles, north, send_one, send_two,
    halo, flux, ca, cb, la, lb, oa, ob,
):
    lats = one.shape[1]
    chans = lt.shape[1]
    columns = taps.shape[1] // lats
    lists = []
    for ref in (one, two):
        wanted = ref[pl.ds(chans, ASK), :128].astype(F32).astype(jnp.int32)
        wanted = jnp.clip(wanted, 0, lats // TLAT - 1)
        lists.append([wanted[0, k] for k in range(MAXACT)])
    odd = parity()
    put_shifts(halo, pl.multiple_of(lats * (1 - odd), 128), one[pl.ds(0, chans), :])
    put_shifts(halo, pl.multiple_of(lats * odd, 128), two[pl.ds(0, chans), :])
    sides = [
        [(halo, 0), (taps, 0), (taps, lats)],
        [(taps, (columns - 2) * lats), (taps, (columns - 1) * lats), (halo, lats)],
    ]
    work = []
    full = lats // CHUNK * CHUNK
    for lo in range(0, full, CHUNK):
        for side in range(2):
            work.append([(side, lo, CHUNK)])
    if full < lats:
        work.append([(0, full, lats - full), (1, full, lats - full)])
    bufs = [(ca, la, oa), (cb, lb, ob)]

    def feed(j):
        segments = []
        for side, lo, size in work[j]:
            segments.append([(ref, at + lo) for ref, at in sides[side]] + [size])
        multiply(segments, wc, lt, bufs[j % 2][0], bufs[j % 2][1])

    def finish(j):
        stores = []
        at = 0
        for side, lo, size in work[j]:
            stores.append((edges.at[side], lo, at, at + size))
            at += size
        activate(bufs[j % 2][0], bufs[j % 2][1], bufs[j % 2][2], stores)

    def head(j):
        got = dot(fwt[...], bufs[j % 2][2][...])
        at = 0
        for side, lo, size in work[j]:
            flux[side, :, lo : lo + size] = got[:, at : at + size]
            at += size

    group = 128 // TLAT
    north_tile = lats // TLAT - 1

    def swap(g):
        at = slice(g * 128, g * 128 + 128)
        values = [flux[0, :, at]]
        for i in range(columns - 2):
            values.append(flux_in[:, i * lats + g * 128 : i * lats + g * 128 + 128])
        values.append(flux[1, :, at])
        for a, v in enumerate(swap_blocks(values, 128)):
            tiles[g * group + a] = v.astype(BF16)
            if g * group + a == north_tile:
                for ref in (north, send_one.at[MAXACT], send_two.at[MAXACT]):
                    ref[...] = v.astype(BF16)

    ready, seen = [], [0, 0]
    for pieces in work:
        for side, lo, size in pieces:
            seen[side] = lo + size
        ready.append(min(seen) // 128)
    feed(0)
    swapped = 0
    for j in range(len(work)):
        if j + 1 < len(work):
            feed(j + 1)
        finish(j)
        if j:
            head(j - 1)
            for g in range(swapped, ready[j - 1]):
                swap(g)
            swapped = ready[j - 1]
    head(len(work) - 1)
    for g in range(swapped, lats // 128):
        swap(g)
    for k in range(MAXACT):
        send_one[k] = tiles[lists[0][k]]
        send_two[k] = tiles[lists[1][k]]


def edge(one, two, flux_in, taps, wc, lt, fwt):
    lats = one.shape[1]
    columns = taps.shape[1] // lats
    width, chans = lt.shape
    fluxes = fwt.shape[0]
    cells = columns * TLAT
    return pl.pallas_call(
        edge_kernel,
        out_shape=(
            jax.ShapeDtypeStruct((2, width, lats), BF16),
            jax.ShapeDtypeStruct((lats // TLAT, fluxes, cells), BF16),
            jax.ShapeDtypeStruct((fluxes, cells), BF16),
            jax.ShapeDtypeStruct((MAXACT + 1, fluxes, cells), BF16),
            jax.ShapeDtypeStruct((MAXACT + 1, fluxes, cells), BF16),
        ),
        in_specs=[VM] * 7,
        out_specs=(VM,) * 5,
        scratch_shapes=[
            pltpu.VMEM((3 * chans, 2 * lats), BF16),
            pltpu.VMEM((2, fluxes, lats), F32),
            pltpu.VMEM((width, CHUNK), F32),
            pltpu.VMEM((width, CHUNK), F32),
            pltpu.VMEM((width, CHUNK), BF16),
            pltpu.VMEM((width, CHUNK), BF16),
            pltpu.VMEM((width, CHUNK), BF16),
            pltpu.VMEM((width, CHUNK), BF16),
        ],
        compiler_params=pltpu.CompilerParams(vmem_limit_bytes=12 * 2**20),
        cost_estimate=pl.CostEstimate(flops=10**9, bytes_accessed=10**6, transcendentals=3 * 10**5),
        name="edge",
    )(one, two, flux_in, taps, wc, lt, fwt)


def early_kernel(
    hid, edges, pair, mask, tiles, ocean, regrid, ow, cw, mw,
    hid_out, out_hbm, sums, base, cwt, mwt, blocks, folds,
    zero, chosen, sems,
):
    count = ocean.shape[0]
    cells = ocean.shape[2]
    columns, _, lats = hid_out.shape
    zero[...] = jnp.zeros(zero.shape, BF16)
    out = [
        pltpu.make_async_copy(edges.at[0], hid_out.at[0], sems.at[0]),
        pltpu.make_async_copy(edges.at[1], hid_out.at[columns - 1], sems.at[1]),
    ]
    for i in range(columns - 2):
        out.append(
            pltpu.make_async_copy(hid.at[:, pl.ds(i * lats, lats)], hid_out.at[i + 1], sems.at[2 + i])
        )
    for c in out:
        c.start()
    list_tiles(mask, chosen, count)
    for t in range(count - FOLDB):

        @pl.when(mask[t] != 1)
        def _():
            pltpu.make_async_copy(zero, out_hbm.at[t], sems.at[columns]).start()

    cwt[...] = cw[...].astype(F32).T.astype(BF16)
    mwt[...] = (0.5 * mw[...].astype(F32)).T.astype(BF16)
    owt = ow[...].astype(F32).T.astype(BF16)
    ones = jnp.ones(tiles.shape[1:], BF16)
    for k in range(MAXACT):
        t = chosen[k]
        at = slice(k * cells, k * cells + cells)
        mine = jnp.concatenate([tiles[pair[1, t]], ones], 0)
        sums[:, at] = dot_t(mine, regrid[t, 1])
        base[:, at] = dot(owt, ocean[t])
        for side in range(2):
            blocks[at, side * cells : (side + 1) * cells] = regrid[t, 2 * side]
        if k < FOLDB:
            folds[at, :] = regrid[t, 3]
    for t in range(count - FOLDB):

        @pl.when(mask[t] != 1)
        def _():
            pltpu.make_async_copy(zero, out_hbm.at[t], sems.at[columns]).wait()

    for c in out:
        c.wait()


def early(hid, edges, pair, mask, tiles, ocean, regrid, ow, cw, mw):
    count, _, cells = ocean.shape
    width = mw.shape[0]
    fluxes = cw.shape[0]
    lats = edges.shape[2]
    columns = hid.shape[1] // lats + 2
    return pl.pallas_call(
        early_kernel,
        out_shape=(
            jax.ShapeDtypeStruct((columns, width, lats), BF16),
            jax.ShapeDtypeStruct((count, width, cells), BF16),
            jax.ShapeDtypeStruct((2 * fluxes, MAXACT * cells), F32),
            jax.ShapeDtypeStruct((width, MAXACT * cells), F32),
            jax.ShapeDtypeStruct((width, fluxes), BF16),
            jax.ShapeDtypeStruct((width, width), BF16),
            jax.ShapeDtypeStruct((MAXACT * cells, 2 * cells), BF16),
            jax.ShapeDtypeStruct((FOLDB * cells, cells), BF16),
        ),
        in_specs=[VM, VM, SM, SM, VM, VM, VM, VM, VM, VM],
        out_specs=(HBM, HBM) + (VM,) * 6,
        scratch_shapes=[
            pltpu.VMEM((width, cells), BF16),
            pltpu.SMEM((MAXACT + 1,), jnp.int32),
            pltpu.SemaphoreType.DMA((columns + 1,)),
        ],
        compiler_params=pltpu.CompilerParams(vmem_limit_bytes=12 * 2**20),
        cost_estimate=pl.CostEstimate(flops=10**9, bytes_accessed=6 * 10**6, transcendentals=0),
        name="early",
    )(hid, edges, pair, mask, tiles, ocean, regrid, ow, cw, mw)


def late_kernel(
    mask, one, two, fold, sums, base, cwt, mwt, blocks, folds, given_hbm,
    out_hbm,
    state, mixed_even, mixed_odd, out, chosen, sems,
):
    fluxes = fold.shape[0]
    cells = out.shape[2]
    pairs = MAXACT // 2
    wide = 2 * cells
    strip, strips = lax.axis_index("lon"), lax.axis_size("lon")
    odd = lax.rem(strip, 2)
    met = lax.rem(strip + 2 * odd - 1 + strips, strips) == strips - 1 - strip
    odd = odd == 1
    partner = jnp.where(met, two[MAXACT], fold[...])
    ones = jnp.ones(fold.shape, BF16)

    def got(k):
        west = jnp.where(odd, one[k], two[k])
        east = jnp.where(odd, two[k], one[k])
        return [jnp.concatenate([west, east], 1), jnp.concatenate([ones, ones], 1)]

    half = 2 * fluxes
    totals = []
    for p in range(pairs):
        at = slice(p * wide, p * wide + wide)
        product = dot_t(jnp.concatenate(got(2 * p) + got(2 * p + 1), 0), blocks[at, :])
        total = jnp.concatenate([product[:half, :cells], product[half:, cells:]], 1) + sums[:, at]
        if 2 * p < FOLDB:
            total = total + dot_t(jnp.concatenate([partner, ones], 0), folds[at, :])
        totals.append(total)
    for p in range(pairs):
        at = slice(p * wide, p * wide + wide)
        regrid = (totals[p][:fluxes] / totals[p][fluxes : fluxes + 1]).astype(BF16)
        state[:, at] = (base[:, at] + dot(cwt[...], regrid)).astype(BF16)

    mixed = (mixed_even, mixed_odd)

    def mix(p):
        mixed[p % 2][...] = dot(mwt[...], state[:, p * wide : p * wide + wide])

    def finish(p):
        for r in range(0, state.shape[0], STRIP):
            at = slice(r, r + STRIP)
            for side in range(2):
                k = 2 * p + side
                own = state[at, k * cells : (k + 1) * cells].astype(F32)
                half = mixed[p % 2][at, side * cells : (side + 1) * cells]
                out[k, at, :] = (own + gelu_of_half(half)).astype(BF16)

    found = list_tiles(mask, chosen, out_hbm.shape[0])
    mix(0)
    for p in range(pairs):
        if p + 1 < pairs:
            mix(p + 1)
        finish(p)
        for k in (2 * p, 2 * p + 1):

            @pl.when(k < found)
            def _():
                pltpu.make_async_copy(out.at[k], out_hbm.at[chosen[k]], sems.at[k]).start()

    for k in range(MAXACT):

        @pl.when(k < found)
        def _():
            pltpu.make_async_copy(out.at[k], out_hbm.at[0], sems.at[k]).wait()


def late(mask, one, two, fold, sums, base, cwt, mwt, blocks, folds, given):
    count, width, cells = given.shape
    return pl.pallas_call(
        late_kernel,
        out_shape=jax.ShapeDtypeStruct((count, width, cells), BF16),
        in_specs=[SM] + [VM] * 9 + [HBM],
        out_specs=HBM,
        scratch_shapes=[
            pltpu.VMEM((width, MAXACT * cells), BF16),
            pltpu.VMEM((width, 2 * cells), F32),
            pltpu.VMEM((width, 2 * cells), F32),
            pltpu.VMEM((MAXACT, width, cells), BF16),
            pltpu.SMEM((MAXACT + 1,), jnp.int32),
            pltpu.SemaphoreType.DMA((MAXACT,)),
        ],
        input_output_aliases={10: 0},
        compiler_params=pltpu.CompilerParams(vmem_limit_bytes=12 * 2**20),
        cost_estimate=pl.CostEstimate(flops=10**9, bytes_accessed=10**6, transcendentals=3 * 10**5),
        name="late",
    )(mask, one, two, fold, sums, base, cwt, mwt, blocks, folds, given)


def per_device(
    atm_in,
    ocean_in,
    lift_weight,
    conv_weight,
    flux_weight,
    ocean_weight,
    couple_weight,
    mix_weight,
    regrid_weight,
    pair_tile,
    ocean_mask,
):
    strips = lax.axis_size("lon")
    inward = [(i, i ^ 1) for i in range(strips)]
    outward = [(i, (i + 1 if i % 2 else i - 1) % strips) for i in range(strips)]
    met = dict(outward)
    mirror = [
        (i, (i + strips // 2) % strips if met[i] == strips - 1 - i else strips - 1 - i)
        for i in range(strips)
    ]
    fwt = flux_weight.T
    pair = pair_tile.T
    send_one, send_two = first(atm_in, pair, ocean_mask)
    two = lax.ppermute(send_two, "lon", outward)
    one = lax.ppermute(send_one, "lon", inward)
    hid, flux, taps, wc, lt = interior(atm_in, lift_weight, conv_weight, fwt)
    edges, tiles, north, send_one, send_two = edge(one, two, flux, taps, wc, lt, fwt)
    one = lax.ppermute(send_one, "lon", inward)
    two = lax.ppermute(send_two, "lon", outward)
    fold = lax.ppermute(north, "lon", mirror)
    atm_hidden, given, sums, base, cwt, mwt, blocks, folds = early(
        hid, edges, pair, ocean_mask, tiles, ocean_in, regrid_weight,
        ocean_weight, couple_weight, mix_weight,
    )
    ocean_hidden = late(
        ocean_mask, one, two, fold, sums, base, cwt, mwt, blocks, folds, given
    )
    return (atm_hidden, ocean_hidden)


def solution(mesh):
    in_specs = (
        P(("groups", "lon"), None, None),
        P(("groups", "lon"), None, None),
        P(),
        P(),
        P(),
        P(),
        P(),
        P(),
        P("lon", None, None, None),
        P("lon", None),
        P("lon"),
    )
    out_specs = (P(("groups", "lon"), None, None), P(("groups", "lon"), None, None))

    return jax.shard_map(
        per_device, mesh=mesh, in_specs=in_specs, out_specs=out_specs, check_vma=False
    )
```

```python
import jax
import jax.numpy as jnp
from jax import lax
from jax.experimental import pallas as pl
from jax.experimental.pallas import tpu as pltpu
from jax.sharding import PartitionSpec as P


TLAT = 16
MAXACT = 8
FOLDB = 2
F32 = jnp.float32
BF16 = jnp.bfloat16
ROOT = 0.7978845608028654
CUBIC = ROOT * 0.044715

CHUNK = 256
STRIP = 32
BUFS = 2
AHEAD = 1
ASK = 8

HBM = pl.BlockSpec(memory_space=pltpu.HBM)
VM = pl.BlockSpec(memory_space=pltpu.VMEM)
SM = pl.BlockSpec(memory_space=pltpu.SMEM)


def dot(a, b):
    return lax.dot_general(a, b, (((1,), (0,)), ((), ())), preferred_element_type=F32)


def dot_t(a, b):
    return lax.dot_general(a, b, (((1,), (1,)), ((), ())), preferred_element_type=F32)


def gelu_of_half(half):
    return half + half * jnp.tanh(half * (2.0 * ROOT + 8.0 * CUBIC * (half * half)))


def put_shifts(taps, at, column):
    chans, lats = column.shape
    lane = lax.broadcasted_iota(jnp.int32, column.shape, 1)
    zero = jnp.zeros(column.shape, BF16)
    taps[:chans, pl.ds(at, lats)] = jnp.where(lane == 0, zero, pltpu.roll(column, 1, 1))
    taps[chans : 2 * chans, pl.ds(at, lats)] = column
    taps[2 * chans :, pl.ds(at, lats)] = jnp.where(
        lane == lats - 1, zero, pltpu.roll(column, lats - 1, 1)
    )


def join(parts, axis):
    return parts[0] if len(parts) == 1 else jnp.concatenate(parts, axis)


def multiply(segments, wc, lt, conv, lifted):
    chans = lt.shape[1]
    rows = 3 * chans
    parts = []
    for a in range(3):
        parts.append(join([seg[a][0][:, pl.ds(seg[a][1], seg[3])] for seg in segments], 1))
    parts.append(jnp.zeros((wc.shape[1] - 3 * rows, parts[0].shape[1]), BF16))
    own = join([seg[1][0][chans : 2 * chans, pl.ds(seg[1][1], seg[3])] for seg in segments], 1)
    conv[...] = dot(wc[...], jnp.concatenate(parts, 0))
    lifted[...] = dot(lt[...], own).astype(BF16)


def activate(conv, lifted, out, stores):
    for r in range(0, conv.shape[0], STRIP):
        at = slice(r, r + STRIP)
        fresh = (lifted[at, :].astype(F32) + gelu_of_half(conv[at, :])).astype(BF16)
        out[at, :] = fresh
        for ref, first, lo, hi in stores:
            ref[at, pl.ds(first, hi - lo)] = fresh[:, lo:hi]


def parity():
    return lax.rem(lax.axis_index("lon"), 2)


def list_tiles(mask, chosen, count):
    for k in range(FOLDB):
        chosen[k] = count - FOLDB + k
    for k in range(FOLDB, MAXACT + 1):
        chosen[k] = count - 1
    found = jnp.int32(FOLDB)
    for t in range(count - FOLDB):
        chosen[jnp.minimum(found, MAXACT)] = t
        found = found + jnp.where(mask[t] == 1, 1, 0)
    return jnp.minimum(found, MAXACT)


def first_kernel(x_hbm, pair_hbm, mask_hbm, one, two, pair, mask, chosen, sems):
    odd = parity()
    last = x_hbm.shape[0] - 1
    chans = x_hbm.shape[1]
    copies = [
        pltpu.make_async_copy(mask_hbm, mask, sems.at[0]),
        pltpu.make_async_copy(pair_hbm, pair, sems.at[1]),
        pltpu.make_async_copy(x_hbm.at[last * (1 - odd)], one.at[pl.ds(0, chans)], sems.at[2]),
        pltpu.make_async_copy(x_hbm.at[last * odd], two.at[pl.ds(0, chans)], sems.at[3]),
    ]
    for c in copies:
        c.start()
    copies[0].wait()
    list_tiles(mask, chosen, mask.shape[0])
    copies[1].wait()
    lane = lax.broadcasted_iota(jnp.int32, (ASK, 128), 1)
    for ref, side in ((one, 2 - 2 * odd), (two, 2 * odd)):
        asked = jnp.zeros((ASK, 128), jnp.int32)
        for k in range(MAXACT):
            asked = jnp.where(lane == k, pair[side, chosen[k]], asked)
        ref[pl.ds(chans, ASK), :128] = asked.astype(F32).astype(BF16)
        ref[pl.ds(chans, ASK), 128:] = jnp.zeros((ASK, ref.shape[1] - 128), BF16)
    copies[2].wait()
    copies[3].wait()


def first(x, pair, mask):
    column = jax.ShapeDtypeStruct((x.shape[1] + ASK, x.shape[2]), BF16)
    given = [pltpu.with_memory_space_constraint(v, pltpu.HBM) for v in (x, pair, mask)]
    return pl.pallas_call(
        first_kernel,
        out_shape=(column, column),
        in_specs=[HBM] * 3,
        out_specs=(VM, VM),
        scratch_shapes=[
            pltpu.SMEM(pair.shape, jnp.int32),
            pltpu.SMEM(mask.shape, jnp.int32),
            pltpu.SMEM((MAXACT + 1,), jnp.int32),
            pltpu.SemaphoreType.DMA((4,)),
        ],
        compiler_params=pltpu.CompilerParams(vmem_limit_bytes=4 * 2**20),
        cost_estimate=pl.CostEstimate(flops=4 * 10**9, bytes_accessed=10**6, transcendentals=0),
        name="first",
    )(*given)


def inner_kernel(
    x, lift, conv, fwt,
    hid, flux, taps, wc, lt,
    comp, *bufs,
):
    columns, chans, lats = x.shape
    convs, lifts, outs = bufs[:BUFS], bufs[BUFS : 2 * BUFS], bufs[2 * BUFS :]
    width = lift.shape[1]
    comp[pl.ds(9 * chans, 2 * width - 9 * chans), :] = jnp.zeros((2 * width - 9 * chans, width), F32)
    half = 0.5 * lift[...]
    for a in range(3):
        for b in range(3):
            comp[pl.ds((3 * a + b) * chans, chans), :] = dot(half, conv[a, b])
    for side in range(2):
        at = slice(side * width, side * width + width)
        wc[:, at] = comp[at, :].T.astype(BF16)
    lt[...] = lift[...].astype(F32).T.astype(BF16)
    for i in range(columns):
        put_shifts(taps, i * lats, x[i])

    def feed(j):
        at = [j * CHUNK + a * lats for a in range(3)]
        multiply([[(taps, p) for p in at] + [CHUNK]], wc, lt, convs[j % BUFS], lifts[j % BUFS])

    def finish(j):
        activate(convs[j % BUFS], lifts[j % BUFS], outs[j % 2], [(hid, j * CHUNK, 0, CHUNK)])

    def head(j):
        flux[:, j * CHUNK : (j + 1) * CHUNK] = dot(fwt[...], outs[j % 2][...])

    chunks = (columns - 2) * lats // CHUNK
    for j in range(AHEAD):
        feed(j)
    for j in range(chunks):
        if j + AHEAD < chunks:
            feed(j + AHEAD)
        finish(j)
        if j:
            head(j - 1)
    head(chunks - 1)


def interior(x, lift, conv, fwt):
    columns, chans, lats = x.shape
    width = lift.shape[1]
    fluxes = fwt.shape[0]
    inner = (columns - 2) * lats
    return pl.pallas_call(
        inner_kernel,
        out_shape=(
            jax.ShapeDtypeStruct((width, inner), BF16),
            jax.ShapeDtypeStruct((fluxes, inner), F32),
            jax.ShapeDtypeStruct((3 * chans, columns * lats), BF16),
            jax.ShapeDtypeStruct((width, 2 * width), BF16),
            jax.ShapeDtypeStruct((width, chans), BF16),
        ),
        in_specs=[VM] * 4,
        out_specs=(VM,) * 5,
        scratch_shapes=[
            pltpu.VMEM((2 * width, width), F32),
        ]
        + [pltpu.VMEM((width, CHUNK), F32)] * BUFS
        + [pltpu.VMEM((width, CHUNK), BF16)] * (BUFS + 2),
        compiler_params=pltpu.CompilerParams(vmem_limit_bytes=12 * 2**20),
        cost_estimate=pl.CostEstimate(flops=4 * 10**9, bytes_accessed=4 * 10**6, transcendentals=10**6),
        name="interior",
    )(x, lift, conv, fwt)


def swap_blocks(values, lanes):
    count = len(values)
    lane = lax.broadcasted_iota(jnp.int32, values[0].shape, 1)
    step = count // 2
    while step:
        shift = step * TLAT
        upper = (lane & shift) != 0
        fresh = list(values)
        for i in range(count):
            if i & step:
                continue
            low, high = values[i], values[i + step]
            fresh[i] = jnp.where(upper, pltpu.roll(high, shift, 1), low)
            fresh[i + step] = jnp.where(upper, high, pltpu.roll(low, lanes - shift, 1))
        values = fresh
        step //= 2
    return values


def edge_kernel(
    one, two, flux_in, taps, wc, lt, fwt,
    edges, tiles, north, send_one, send_two,
    halo, flux, ca, cb, la, lb, oa, ob,
):
    lats = one.shape[1]
    chans = lt.shape[1]
    columns = taps.shape[1] // lats
    lists = []
    for ref in (one, two):
        wanted = ref[pl.ds(chans, ASK), :128].astype(F32).astype(jnp.int32)
        wanted = jnp.clip(wanted, 0, lats // TLAT - 1)
        lists.append([wanted[0, k] for k in range(MAXACT)])
    odd = parity()
    put_shifts(halo, pl.multiple_of(lats * (1 - odd), 128), one[pl.ds(0, chans), :])
    put_shifts(halo, pl.multiple_of(lats * odd, 128), two[pl.ds(0, chans), :])
    sides = [
        [(halo, 0), (taps, 0), (taps, lats)],
        [(taps, (columns - 2) * lats), (taps, (columns - 1) * lats), (halo, lats)],
    ]
    work = []
    full = lats // CHUNK * CHUNK
    for lo in range(0, full, CHUNK):
        for side in range(2):
            work.append([(side, lo, CHUNK)])
    if full < lats:
        work.append([(0, full, lats - full), (1, full, lats - full)])
    bufs = [(ca, la, oa), (cb, lb, ob)]

    def feed(j):
        segments = []
        for side, lo, size in work[j]:
            segments.append([(ref, at + lo) for ref, at in sides[side]] + [size])
        multiply(segments, wc, lt, bufs[j % 2][0], bufs[j % 2][1])

    def finish(j):
        stores = []
        at = 0
        for side, lo, size in work[j]:
            stores.append((edges.at[side], lo, at, at + size))
            at += size
        activate(bufs[j % 2][0], bufs[j % 2][1], bufs[j % 2][2], stores)

    def head(j):
        got = dot(fwt[...], bufs[j % 2][2][...])
        at = 0
        for side, lo, size in work[j]:
            flux[side, :, lo : lo + size] = got[:, at : at + size]
            at += size

    group = 128 // TLAT
    north_tile = lats // TLAT - 1

    def swap(g):
        at = slice(g * 128, g * 128 + 128)
        values = [flux[0, :, at]]
        for i in range(columns - 2):
            values.append(flux_in[:, i * lats + g * 128 : i * lats + g * 128 + 128])
        values.append(flux[1, :, at])
        for a, v in enumerate(swap_blocks(values, 128)):
            tiles[g * group + a] = v.astype(BF16)
            if g * group + a == north_tile:
                for ref in (north, send_one.at[MAXACT], send_two.at[MAXACT]):
                    ref[...] = v.astype(BF16)

    ready, seen = [], [0, 0]
    for pieces in work:
        for side, lo, size in pieces:
            seen[side] = lo + size
        ready.append(min(seen) // 128)
    feed(0)
    swapped = 0
    for j in range(len(work)):
        if j + 1 < len(work):
            feed(j + 1)
        finish(j)
        if j:
            head(j - 1)
            for g in range(swapped, ready[j - 1]):
                swap(g)
            swapped = ready[j - 1]
    head(len(work) - 1)
    for g in range(swapped, lats // 128):
        swap(g)
    for k in range(MAXACT):
        send_one[k] = tiles[lists[0][k]]
        send_two[k] = tiles[lists[1][k]]


def edge(one, two, flux_in, taps, wc, lt, fwt):
    lats = one.shape[1]
    columns = taps.shape[1] // lats
    width, chans = lt.shape
    fluxes = fwt.shape[0]
    cells = columns * TLAT
    return pl.pallas_call(
        edge_kernel,
        out_shape=(
            jax.ShapeDtypeStruct((2, width, lats), BF16),
            jax.ShapeDtypeStruct((lats // TLAT, fluxes, cells), BF16),
            jax.ShapeDtypeStruct((fluxes, cells), BF16),
            jax.ShapeDtypeStruct((MAXACT + 1, fluxes, cells), BF16),
            jax.ShapeDtypeStruct((MAXACT + 1, fluxes, cells), BF16),
        ),
        in_specs=[VM] * 7,
        out_specs=(VM,) * 5,
        scratch_shapes=[
            pltpu.VMEM((3 * chans, 2 * lats), BF16),
            pltpu.VMEM((2, fluxes, lats), F32),
            pltpu.VMEM((width, CHUNK), F32),
            pltpu.VMEM((width, CHUNK), F32),
            pltpu.VMEM((width, CHUNK), BF16),
            pltpu.VMEM((width, CHUNK), BF16),
            pltpu.VMEM((width, CHUNK), BF16),
            pltpu.VMEM((width, CHUNK), BF16),
        ],
        compiler_params=pltpu.CompilerParams(vmem_limit_bytes=12 * 2**20),
        cost_estimate=pl.CostEstimate(flops=10**9, bytes_accessed=10**6, transcendentals=3 * 10**5),
        name="edge",
    )(one, two, flux_in, taps, wc, lt, fwt)


def early_kernel(
    hid, edges, pair, mask, tiles, ocean, regrid, ow, cw, mw,
    hid_out, out_hbm, sums, base, cwt, mwt, blocks, folds,
    zero, chosen, sems,
):
    count = ocean.shape[0]
    cells = ocean.shape[2]
    columns, _, lats = hid_out.shape
    zero[...] = jnp.zeros(zero.shape, BF16)
    out = [
        pltpu.make_async_copy(edges.at[0], hid_out.at[0], sems.at[0]),
        pltpu.make_async_copy(edges.at[1], hid_out.at[columns - 1], sems.at[1]),
    ]
    for i in range(columns - 2):
        out.append(
            pltpu.make_async_copy(hid.at[:, pl.ds(i * lats, lats)], hid_out.at[i + 1], sems.at[2 + i])
        )
    for c in out:
        c.start()
    list_tiles(mask, chosen, count)
    for t in range(count - FOLDB):

        @pl.when(mask[t] != 1)
        def _():
            pltpu.make_async_copy(zero, out_hbm.at[t], sems.at[columns]).start()

    cwt[...] = cw[...].astype(F32).T.astype(BF16)
    mwt[...] = (0.5 * mw[...].astype(F32)).T.astype(BF16)
    owt = ow[...].astype(F32).T.astype(BF16)
    ones = jnp.ones(tiles.shape[1:], BF16)
    for k in range(MAXACT):
        t = chosen[k]
        at = slice(k * cells, k * cells + cells)
        mine = jnp.concatenate([tiles[pair[1, t]], ones], 0)
        sums[:, at] = dot_t(mine, regrid[t, 1])
        base[:, at] = dot(owt, ocean[t])
        for side in range(2):
            blocks[at, side * cells : (side + 1) * cells] = regrid[t, 2 * side]
        if k < FOLDB:
            folds[at, :] = regrid[t, 3]
    for t in range(count - FOLDB):

        @pl.when(mask[t] != 1)
        def _():
            pltpu.make_async_copy(zero, out_hbm.at[t], sems.at[columns]).wait()

    for c in out:
        c.wait()


def early(hid, edges, pair, mask, tiles, ocean, regrid, ow, cw, mw):
    count, _, cells = ocean.shape
    width = mw.shape[0]
    fluxes = cw.shape[0]
    lats = edges.shape[2]
    columns = hid.shape[1] // lats + 2
    return pl.pallas_call(
        early_kernel,
        out_shape=(
            jax.ShapeDtypeStruct((columns, width, lats), BF16),
            jax.ShapeDtypeStruct((count, width, cells), BF16),
            jax.ShapeDtypeStruct((2 * fluxes, MAXACT * cells), F32),
            jax.ShapeDtypeStruct((width, MAXACT * cells), F32),
            jax.ShapeDtypeStruct((width, fluxes), BF16),
            jax.ShapeDtypeStruct((width, width), BF16),
            jax.ShapeDtypeStruct((MAXACT * cells, 2 * cells), BF16),
            jax.ShapeDtypeStruct((FOLDB * cells, cells), BF16),
        ),
        in_specs=[VM, VM, SM, SM, VM, VM, VM, VM, VM, VM],
        out_specs=(HBM, HBM) + (VM,) * 6,
        scratch_shapes=[
            pltpu.VMEM((width, cells), BF16),
            pltpu.SMEM((MAXACT + 1,), jnp.int32),
            pltpu.SemaphoreType.DMA((columns + 1,)),
        ],
        compiler_params=pltpu.CompilerParams(vmem_limit_bytes=12 * 2**20),
        cost_estimate=pl.CostEstimate(flops=10**9, bytes_accessed=6 * 10**6, transcendentals=0),
        name="early",
    )(hid, edges, pair, mask, tiles, ocean, regrid, ow, cw, mw)


def late_kernel(
    mask, one, two, fold, sums, base, cwt, mwt, blocks, folds, given_hbm,
    out_hbm,
    state, mixed_even, mixed_odd, out, chosen, sems,
):
    fluxes = fold.shape[0]
    cells = out.shape[2]
    pairs = MAXACT // 2
    wide = 2 * cells
    strip, strips = lax.axis_index("lon"), lax.axis_size("lon")
    odd = lax.rem(strip, 2)
    met = lax.rem(strip + 2 * odd - 1 + strips, strips) == strips - 1 - strip
    odd = odd == 1
    partner = jnp.where(met, two[MAXACT], fold[...])
    ones = jnp.ones(fold.shape, BF16)

    def got(k):
        west = jnp.where(odd, one[k], two[k])
        east = jnp.where(odd, two[k], one[k])
        return [jnp.concatenate([west, east], 1), jnp.concatenate([ones, ones], 1)]

    half = 2 * fluxes
    totals = []
    for p in range(pairs):
        at = slice(p * wide, p * wide + wide)
        product = dot_t(jnp.concatenate(got(2 * p) + got(2 * p + 1), 0), blocks[at, :])
        total = jnp.concatenate([product[:half, :cells], product[half:, cells:]], 1) + sums[:, at]
        if 2 * p < FOLDB:
            total = total + dot_t(jnp.concatenate([partner, ones], 0), folds[at, :])
        totals.append(total)
    for p in range(pairs):
        at = slice(p * wide, p * wide + wide)
        regrid = (totals[p][:fluxes] / totals[p][fluxes : fluxes + 1]).astype(BF16)
        state[:, at] = (base[:, at] + dot(cwt[...], regrid)).astype(BF16)

    mixed = (mixed_even, mixed_odd)

    def mix(p):
        mixed[p % 2][...] = dot(mwt[...], state[:, p * wide : p * wide + wide])

    def finish(p):
        for r in range(0, state.shape[0], STRIP):
            at = slice(r, r + STRIP)
            for side in range(2):
                k = 2 * p + side
                own = state[at, k * cells : (k + 1) * cells].astype(F32)
                half = mixed[p % 2][at, side * cells : (side + 1) * cells]
                out[k, at, :] = (own + gelu_of_half(half)).astype(BF16)

    found = list_tiles(mask, chosen, out_hbm.shape[0])
    mix(0)
    for p in range(pairs):
        if p + 1 < pairs:
            mix(p + 1)
        finish(p)
        for k in (2 * p, 2 * p + 1):

            @pl.when(k < found)
            def _():
                pltpu.make_async_copy(out.at[k], out_hbm.at[chosen[k]], sems.at[k]).start()

    for k in range(MAXACT):

        @pl.when(k < found)
        def _():
            pltpu.make_async_copy(out.at[k], out_hbm.at[0], sems.at[k]).wait()


def late(mask, one, two, fold, sums, base, cwt, mwt, blocks, folds, given):
    count, width, cells = given.shape
    return pl.pallas_call(
        late_kernel,
        out_shape=jax.ShapeDtypeStruct((count, width, cells), BF16),
        in_specs=[SM] + [VM] * 9 + [HBM],
        out_specs=HBM,
        scratch_shapes=[
            pltpu.VMEM((width, MAXACT * cells), BF16),
            pltpu.VMEM((width, 2 * cells), F32),
            pltpu.VMEM((width, 2 * cells), F32),
            pltpu.VMEM((MAXACT, width, cells), BF16),
            pltpu.SMEM((MAXACT + 1,), jnp.int32),
            pltpu.SemaphoreType.DMA((MAXACT,)),
        ],
        input_output_aliases={10: 0},
        compiler_params=pltpu.CompilerParams(vmem_limit_bytes=12 * 2**20),
        cost_estimate=pl.CostEstimate(flops=10**9, bytes_accessed=10**6, transcendentals=3 * 10**5),
        name="late",
    )(mask, one, two, fold, sums, base, cwt, mwt, blocks, folds, given)


def per_device(
    atm_in,
    ocean_in,
    lift_weight,
    conv_weight,
    flux_weight,
    ocean_weight,
    couple_weight,
    mix_weight,
    regrid_weight,
    pair_tile,
    ocean_mask,
):
    strips = lax.axis_size("lon")
    inward = [(i, i ^ 1) for i in range(strips)]
    outward = [(i, (i + 1 if i % 2 else i - 1) % strips) for i in range(strips)]
    met = dict(outward)
    mirror = [
        (i, (i + strips // 2) % strips if met[i] == strips - 1 - i else strips - 1 - i)
        for i in range(strips)
    ]
    fwt = flux_weight.T
    pair = pair_tile.T
    send_one, send_two = first(atm_in, pair, ocean_mask)
    two = lax.ppermute(send_two, "lon", outward)
    one = lax.ppermute(send_one, "lon", inward)
    hid, flux, taps, wc, lt = interior(atm_in, lift_weight, conv_weight, fwt)
    edges, tiles, north, send_one, send_two = edge(one, two, flux, taps, wc, lt, fwt)
    one = lax.ppermute(send_one, "lon", inward)
    two = lax.ppermute(send_two, "lon", outward)
    fold = lax.ppermute(north, "lon", mirror)
    atm_hidden, given, sums, base, cwt, mwt, blocks, folds = early(
        hid, edges, pair, ocean_mask, tiles, ocean_in, regrid_weight,
        ocean_weight, couple_weight, mix_weight,
    )
    ocean_hidden = late(
        ocean_mask, one, two, fold, sums, base, cwt, mwt, blocks, folds, given
    )
    return (atm_hidden, ocean_hidden)


def solution(mesh):
    in_specs = (
        P(("groups", "lon"), None, None),
        P(("groups", "lon"), None, None),
        P(),
        P(),
        P(),
        P(),
        P(),
        P(),
        P("lon", None, None, None),
        P("lon", None),
        P("lon"),
    )
    out_specs = (P(("groups", "lon"), None, None), P(("groups", "lon"), None, None))

    return jax.shard_map(
        per_device, mesh=mesh, in_specs=in_specs, out_specs=out_specs, check_vma=False
    )
```

```python
import jax
import jax.numpy as jnp
from jax import lax
from jax.experimental import pallas as pl
from jax.experimental.pallas import tpu as pltpu
from jax.sharding import PartitionSpec as P


TLAT = 16
MAXACT = 8
FOLDB = 2
F32 = jnp.float32
BF16 = jnp.bfloat16
ROOT = 0.7978845608028654
CUBIC = ROOT * 0.044715

CHUNK = 256
STRIP = 32
BUFS = 2
AHEAD = 1
ASK = 8
TILE, OWN, WATER, COUNT = range(4)

HBM = pl.BlockSpec(memory_space=pltpu.HBM)
VM = pl.BlockSpec(memory_space=pltpu.VMEM)


def dot(a, b):
    return lax.dot_general(a, b, (((1,), (0,)), ((), ())), preferred_element_type=F32)


def dot_t(a, b):
    return lax.dot_general(a, b, (((1,), (1,)), ((), ())), preferred_element_type=F32)


def gelu_of_half(half):
    return half + half * jnp.tanh(half * (2.0 * ROOT + 8.0 * CUBIC * (half * half)))


def put_shifts(taps, at, column):
    chans, lats = column.shape
    lane = lax.broadcasted_iota(jnp.int32, column.shape, 1)
    zero = jnp.zeros(column.shape, BF16)
    taps[:chans, pl.ds(at, lats)] = jnp.where(lane == 0, zero, pltpu.roll(column, 1, 1))
    taps[chans : 2 * chans, pl.ds(at, lats)] = column
    taps[2 * chans :, pl.ds(at, lats)] = jnp.where(
        lane == lats - 1, zero, pltpu.roll(column, lats - 1, 1)
    )


def join(parts, axis):
    return parts[0] if len(parts) == 1 else jnp.concatenate(parts, axis)


def multiply(segments, wc, lt, conv, lifted):
    chans = lt.shape[1]
    rows = 3 * chans
    parts = []
    for a in range(3):
        parts.append(join([seg[a][0][:, pl.ds(seg[a][1], seg[3])] for seg in segments], 1))
    parts.append(jnp.zeros((wc.shape[1] - 3 * rows, parts[0].shape[1]), BF16))
    own = join([seg[1][0][chans : 2 * chans, pl.ds(seg[1][1], seg[3])] for seg in segments], 1)
    conv[...] = dot(wc[...], jnp.concatenate(parts, 0))
    lifted[...] = dot(lt[...], own).astype(BF16)


def activate(conv, lifted, out, stores):
    for r in range(0, conv.shape[0], STRIP):
        at = slice(r, r + STRIP)
        fresh = (lifted[at, :].astype(F32) + gelu_of_half(conv[at, :])).astype(BF16)
        out[at, :] = fresh
        for ref, first, lo, hi in stores:
            ref[at, pl.ds(first, hi - lo)] = fresh[:, lo:hi]


def parity():
    return lax.rem(lax.axis_index("lon"), 2)


def list_tiles(mask, chosen, count):
    for k in range(FOLDB):
        chosen[k] = count - FOLDB + k
    for k in range(FOLDB, MAXACT + 1):
        chosen[k] = count - 1
    found = jnp.int32(FOLDB)
    for t in range(count - FOLDB):
        chosen[jnp.minimum(found, MAXACT)] = t
        found = found + jnp.where(mask[t] == 1, 1, 0)
    return jnp.minimum(found, MAXACT)


def first_kernel(x_hbm, pair_hbm, mask_hbm, one, two, plan, pair, mask, chosen, sems):
    odd = parity()
    last = x_hbm.shape[0] - 1
    chans = x_hbm.shape[1]
    copies = [
        pltpu.make_async_copy(mask_hbm, mask, sems.at[0]),
        pltpu.make_async_copy(pair_hbm, pair, sems.at[1]),
        pltpu.make_async_copy(x_hbm.at[last * (1 - odd)], one.at[pl.ds(0, chans)], sems.at[2]),
        pltpu.make_async_copy(x_hbm.at[last * odd], two.at[pl.ds(0, chans)], sems.at[3]),
    ]
    for c in copies:
        c.start()
    copies[0].wait()
    found = list_tiles(mask, chosen, mask.shape[0])
    copies[1].wait()
    row = lax.broadcasted_iota(jnp.int32, plan.shape, 0)
    spot = lax.broadcasted_iota(jnp.int32, plan.shape, 1)
    facts = jnp.where(row == COUNT, found, jnp.zeros(plan.shape, jnp.int32))
    for k in range(MAXACT):
        facts = jnp.where((row == TILE) & (spot == k), chosen[k], facts)
        facts = jnp.where((row == OWN) & (spot == k), pair[1, chosen[k]], facts)
    for t in range(mask.shape[0]):
        facts = jnp.where((row == WATER) & (spot == t), mask[t], facts)
    plan[...] = facts
    lane = lax.broadcasted_iota(jnp.int32, (ASK, 128), 1)
    for ref, side in ((one, 2 - 2 * odd), (two, 2 * odd)):
        asked = jnp.zeros((ASK, 128), jnp.int32)
        for k in range(MAXACT):
            asked = jnp.where(lane == k, pair[side, chosen[k]], asked)
        ref[pl.ds(chans, ASK), :128] = asked.astype(F32).astype(BF16)
        ref[pl.ds(chans, ASK), 128:] = jnp.zeros((ASK, ref.shape[1] - 128), BF16)
    copies[2].wait()
    copies[3].wait()


def first(x, pair, mask):
    column = jax.ShapeDtypeStruct((x.shape[1] + ASK, x.shape[2]), BF16)
    given = [pltpu.with_memory_space_constraint(v, pltpu.HBM) for v in (x, pair, mask)]
    return pl.pallas_call(
        first_kernel,
        out_shape=(column, column, jax.ShapeDtypeStruct((8, 128), jnp.int32)),
        in_specs=[HBM] * 3,
        out_specs=(VM,) * 3,
        scratch_shapes=[
            pltpu.SMEM(pair.shape, jnp.int32),
            pltpu.SMEM(mask.shape, jnp.int32),
            pltpu.SMEM((MAXACT + 1,), jnp.int32),
            pltpu.SemaphoreType.DMA((4,)),
        ],
        compiler_params=pltpu.CompilerParams(vmem_limit_bytes=4 * 2**20),
        cost_estimate=pl.CostEstimate(flops=4 * 10**9, bytes_accessed=10**6, transcendentals=0),
        name="first",
    )(*given)


def inner_kernel(
    x, lift, conv, fwt,
    hid, flux, taps, wc, lt,
    comp, *bufs,
):
    columns, chans, lats = x.shape
    convs, lifts, outs = bufs[:BUFS], bufs[BUFS : 2 * BUFS], bufs[2 * BUFS :]
    width = lift.shape[1]
    comp[pl.ds(9 * chans, 2 * width - 9 * chans), :] = jnp.zeros((2 * width - 9 * chans, width), F32)
    half = 0.5 * lift[...]
    for a in range(3):
        for b in range(3):
            comp[pl.ds((3 * a + b) * chans, chans), :] = dot(half, conv[a, b])
    for side in range(2):
        at = slice(side * width, side * width + width)
        wc[:, at] = comp[at, :].T.astype(BF16)
    lt[...] = lift[...].astype(F32).T.astype(BF16)
    for i in range(columns):
        put_shifts(taps, i * lats, x[i])

    def feed(j):
        at = [j * CHUNK + a * lats for a in range(3)]
        multiply([[(taps, p) for p in at] + [CHUNK]], wc, lt, convs[j % BUFS], lifts[j % BUFS])

    def finish(j):
        activate(convs[j % BUFS], lifts[j % BUFS], outs[j % 2], [(hid, j * CHUNK, 0, CHUNK)])

    def head(j):
        flux[:, j * CHUNK : (j + 1) * CHUNK] = dot(fwt[...], outs[j % 2][...])

    chunks = (columns - 2) * lats // CHUNK
    for j in range(AHEAD):
        feed(j)
    for j in range(chunks):
        if j + AHEAD < chunks:
            feed(j + AHEAD)
        finish(j)
        if j:
            head(j - 1)
    head(chunks - 1)


def interior(x, lift, conv, fwt):
    columns, chans, lats = x.shape
    width = lift.shape[1]
    fluxes = fwt.shape[0]
    inner = (columns - 2) * lats
    return pl.pallas_call(
        inner_kernel,
        out_shape=(
            jax.ShapeDtypeStruct((width, inner), BF16),
            jax.ShapeDtypeStruct((fluxes, inner), F32),
            jax.ShapeDtypeStruct((3 * chans, columns * lats), BF16),
            jax.ShapeDtypeStruct((width, 2 * width), BF16),
            jax.ShapeDtypeStruct((width, chans), BF16),
        ),
        in_specs=[VM] * 4,
        out_specs=(VM,) * 5,
        scratch_shapes=[
            pltpu.VMEM((2 * width, width), F32),
        ]
        + [pltpu.VMEM((width, CHUNK), F32)] * BUFS
        + [pltpu.VMEM((width, CHUNK), BF16)] * (BUFS + 2),
        compiler_params=pltpu.CompilerParams(vmem_limit_bytes=12 * 2**20),
        cost_estimate=pl.CostEstimate(flops=4 * 10**9, bytes_accessed=4 * 10**6, transcendentals=10**6),
        name="interior",
    )(x, lift, conv, fwt)


def swap_blocks(values, lanes):
    count = len(values)
    lane = lax.broadcasted_iota(jnp.int32, values[0].shape, 1)
    step = count // 2
    while step:
        shift = step * TLAT
        upper = (lane & shift) != 0
        fresh = list(values)
        for i in range(count):
            if i & step:
                continue
            low, high = values[i], values[i + step]
            fresh[i] = jnp.where(upper, pltpu.roll(high, shift, 1), low)
            fresh[i + step] = jnp.where(upper, high, pltpu.roll(low, lanes - shift, 1))
        values = fresh
        step //= 2
    return values


def edge_kernel(
    one, two, flux_in, taps, wc, lt, fwt,
    edges, tiles, north, send_one, send_two,
    halo, flux, ca, cb, la, lb, oa, ob,
):
    lats = one.shape[1]
    chans = lt.shape[1]
    columns = taps.shape[1] // lats
    lists = []
    for ref in (one, two):
        wanted = ref[pl.ds(chans, ASK), :128].astype(F32).astype(jnp.int32)
        wanted = jnp.clip(wanted, 0, lats // TLAT - 1)
        lists.append([wanted[0, k] for k in range(MAXACT)])
    odd = parity()
    put_shifts(halo, pl.multiple_of(lats * (1 - odd), 128), one[pl.ds(0, chans), :])
    put_shifts(halo, pl.multiple_of(lats * odd, 128), two[pl.ds(0, chans), :])
    sides = [
        [(halo, 0), (taps, 0), (taps, lats)],
        [(taps, (columns - 2) * lats), (taps, (columns - 1) * lats), (halo, lats)],
    ]
    work = []
    full = lats // CHUNK * CHUNK
    for lo in range(0, full, CHUNK):
        for side in range(2):
            work.append([(side, lo, CHUNK)])
    if full < lats:
        work.append([(0, full, lats - full), (1, full, lats - full)])
    bufs = [(ca, la, oa), (cb, lb, ob)]

    def feed(j):
        segments = []
        for side, lo, size in work[j]:
            segments.append([(ref, at + lo) for ref, at in sides[side]] + [size])
        multiply(segments, wc, lt, bufs[j % 2][0], bufs[j % 2][1])

    def finish(j):
        stores = []
        at = 0
        for side, lo, size in work[j]:
            stores.append((edges.at[side], lo, at, at + size))
            at += size
        activate(bufs[j % 2][0], bufs[j % 2][1], bufs[j % 2][2], stores)

    def head(j):
        got = dot(fwt[...], bufs[j % 2][2][...])
        at = 0
        for side, lo, size in work[j]:
            flux[side, :, lo : lo + size] = got[:, at : at + size]
            at += size

    group = 128 // TLAT
    north_tile = lats // TLAT - 1

    def swap(g):
        at = slice(g * 128, g * 128 + 128)
        values = [flux[0, :, at]]
        for i in range(columns - 2):
            values.append(flux_in[:, i * lats + g * 128 : i * lats + g * 128 + 128])
        values.append(flux[1, :, at])
        for a, v in enumerate(swap_blocks(values, 128)):
            tiles[g * group + a] = v.astype(BF16)
            if g * group + a == north_tile:
                for ref in (north, send_one.at[MAXACT], send_two.at[MAXACT]):
                    ref[...] = v.astype(BF16)

    ready, seen = [], [0, 0]
    for pieces in work:
        for side, lo, size in pieces:
            seen[side] = lo + size
        ready.append(min(seen) // 128)
    feed(0)
    swapped = 0
    for j in range(len(work)):
        if j + 1 < len(work):
            feed(j + 1)
        finish(j)
        if j:
            head(j - 1)
            for g in range(swapped, ready[j - 1]):
                swap(g)
            swapped = ready[j - 1]
    head(len(work) - 1)
    for g in range(swapped, lats // 128):
        swap(g)
    for k in range(MAXACT):
        send_one[k] = tiles[lists[0][k]]
        send_two[k] = tiles[lists[1][k]]


def edge(one, two, flux_in, taps, wc, lt, fwt):
    lats = one.shape[1]
    columns = taps.shape[1] // lats
    width, chans = lt.shape
    fluxes = fwt.shape[0]
    cells = columns * TLAT
    return pl.pallas_call(
        edge_kernel,
        out_shape=(
            jax.ShapeDtypeStruct((2, width, lats), BF16),
            jax.ShapeDtypeStruct((lats // TLAT, fluxes, cells), BF16),
            jax.ShapeDtypeStruct((fluxes, cells), BF16),
            jax.ShapeDtypeStruct((MAXACT + 1, fluxes, cells), BF16),
            jax.ShapeDtypeStruct((MAXACT + 1, fluxes, cells), BF16),
        ),
        in_specs=[VM] * 7,
        out_specs=(VM,) * 5,
        scratch_shapes=[
            pltpu.VMEM((3 * chans, 2 * lats), BF16),
            pltpu.VMEM((2, fluxes, lats), F32),
            pltpu.VMEM((width, CHUNK), F32),
            pltpu.VMEM((width, CHUNK), F32),
            pltpu.VMEM((width, CHUNK), BF16),
            pltpu.VMEM((width, CHUNK), BF16),
            pltpu.VMEM((width, CHUNK), BF16),
            pltpu.VMEM((width, CHUNK), BF16),
        ],
        compiler_params=pltpu.CompilerParams(vmem_limit_bytes=12 * 2**20),
        cost_estimate=pl.CostEstimate(flops=10**9, bytes_accessed=10**6, transcendentals=3 * 10**5),
        name="edge",
    )(one, two, flux_in, taps, wc, lt, fwt)


def early_kernel(
    hid, edges, plan, tiles, ocean, regrid, ow, cw, mw,
    hid_out, out_hbm, sums, base, cwt, mwt, blocks, folds,
    zero, sems,
):
    count = ocean.shape[0]
    cells = ocean.shape[2]
    columns, _, lats = hid_out.shape
    zero[...] = jnp.zeros(zero.shape, BF16)
    out = [
        pltpu.make_async_copy(edges.at[0], hid_out.at[0], sems.at[0]),
        pltpu.make_async_copy(edges.at[1], hid_out.at[columns - 1], sems.at[1]),
    ]
    for i in range(columns - 2):
        out.append(
            pltpu.make_async_copy(hid.at[:, pl.ds(i * lats, lats)], hid_out.at[i + 1], sems.at[2 + i])
        )
    for c in out:
        c.start()
    facts = plan[...]
    water = [facts[WATER, t] == 1 for t in range(count - FOLDB)]
    for t in range(count - FOLDB):

        @pl.when(jnp.logical_not(water[t]))
        def _():
            pltpu.make_async_copy(zero, out_hbm.at[t], sems.at[columns]).start()

    cwt[...] = cw[...].astype(F32).T.astype(BF16)
    mwt[...] = (0.5 * mw[...].astype(F32)).T.astype(BF16)
    owt = ow[...].astype(F32).T.astype(BF16)
    ones = jnp.ones(tiles.shape[1:], BF16)
    for k in range(MAXACT):
        t = facts[TILE, k]
        at = slice(k * cells, k * cells + cells)
        mine = jnp.concatenate([tiles[facts[OWN, k]], ones], 0)
        sums[:, at] = dot_t(mine, regrid[t, 1])
        base[:, at] = dot(owt, ocean[t])
        for side in range(2):
            blocks[at, side * cells : (side + 1) * cells] = regrid[t, 2 * side]
        if k < FOLDB:
            folds[at, :] = regrid[t, 3]
    for t in range(count - FOLDB):

        @pl.when(jnp.logical_not(water[t]))
        def _():
            pltpu.make_async_copy(zero, out_hbm.at[t], sems.at[columns]).wait()

    for c in out:
        c.wait()


def early(hid, edges, plan, tiles, ocean, regrid, ow, cw, mw):
    count, _, cells = ocean.shape
    width = mw.shape[0]
    fluxes = cw.shape[0]
    lats = edges.shape[2]
    columns = hid.shape[1] // lats + 2
    return pl.pallas_call(
        early_kernel,
        out_shape=(
            jax.ShapeDtypeStruct((columns, width, lats), BF16),
            jax.ShapeDtypeStruct((count, width, cells), BF16),
            jax.ShapeDtypeStruct((2 * fluxes, MAXACT * cells), F32),
            jax.ShapeDtypeStruct((width, MAXACT * cells), F32),
            jax.ShapeDtypeStruct((width, fluxes), BF16),
            jax.ShapeDtypeStruct((width, width), BF16),
            jax.ShapeDtypeStruct((MAXACT * cells, 2 * cells), BF16),
            jax.ShapeDtypeStruct((FOLDB * cells, cells), BF16),
        ),
        in_specs=[VM] * 9,
        out_specs=(HBM, HBM) + (VM,) * 6,
        scratch_shapes=[
            pltpu.VMEM((width, cells), BF16),
            pltpu.SemaphoreType.DMA((columns + 1,)),
        ],
        compiler_params=pltpu.CompilerParams(vmem_limit_bytes=12 * 2**20),
        cost_estimate=pl.CostEstimate(flops=10**9, bytes_accessed=6 * 10**6, transcendentals=0),
        name="early",
    )(hid, edges, plan, tiles, ocean, regrid, ow, cw, mw)


def late_kernel(
    plan, one, two, fold, sums, base, cwt, mwt, blocks, folds, given_hbm,
    out_hbm,
    state, mixed_even, mixed_odd, out, sems,
):
    fluxes = fold.shape[0]
    cells = out.shape[2]
    pairs = MAXACT // 2
    wide = 2 * cells
    strip, strips = lax.axis_index("lon"), lax.axis_size("lon")
    odd = lax.rem(strip, 2)
    met = lax.rem(strip + 2 * odd - 1 + strips, strips) == strips - 1 - strip
    odd = odd == 1
    partner = jnp.where(met, two[MAXACT], fold[...])
    ones = jnp.ones(fold.shape, BF16)

    def got(k):
        west = jnp.where(odd, one[k], two[k])
        east = jnp.where(odd, two[k], one[k])
        return [jnp.concatenate([west, east], 1), jnp.concatenate([ones, ones], 1)]

    half = 2 * fluxes
    totals = []
    for p in range(pairs):
        at = slice(p * wide, p * wide + wide)
        product = dot_t(jnp.concatenate(got(2 * p) + got(2 * p + 1), 0), blocks[at, :])
        total = jnp.concatenate([product[:half, :cells], product[half:, cells:]], 1) + sums[:, at]
        if 2 * p < FOLDB:
            total = total + dot_t(jnp.concatenate([partner, ones], 0), folds[at, :])
        totals.append(total)
    for p in range(pairs):
        at = slice(p * wide, p * wide + wide)
        regrid = (totals[p][:fluxes] / totals[p][fluxes : fluxes + 1]).astype(BF16)
        state[:, at] = (base[:, at] + dot(cwt[...], regrid)).astype(BF16)

    mixed = (mixed_even, mixed_odd)

    def mix(p):
        mixed[p % 2][...] = dot(mwt[...], state[:, p * wide : p * wide + wide])

    def finish(p):
        for r in range(0, state.shape[0], STRIP):
            at = slice(r, r + STRIP)
            for side in range(2):
                k = 2 * p + side
                own = state[at, k * cells : (k + 1) * cells].astype(F32)
                half = mixed[p % 2][at, side * cells : (side + 1) * cells]
                out[k, at, :] = (own + gelu_of_half(half)).astype(BF16)

    facts = plan[...]
    found = facts[COUNT, 0]
    chosen = [facts[TILE, k] for k in range(MAXACT)]
    mix(0)
    for p in range(pairs):
        if p + 1 < pairs:
            mix(p + 1)
        finish(p)
        for k in (2 * p, 2 * p + 1):

            @pl.when(k < found)
            def _():
                pltpu.make_async_copy(out.at[k], out_hbm.at[chosen[k]], sems.at[k]).start()

    for k in range(MAXACT):

        @pl.when(k < found)
        def _():
            pltpu.make_async_copy(out.at[k], out_hbm.at[0], sems.at[k]).wait()


def late(plan, one, two, fold, sums, base, cwt, mwt, blocks, folds, given):
    count, width, cells = given.shape
    return pl.pallas_call(
        late_kernel,
        out_shape=jax.ShapeDtypeStruct((count, width, cells), BF16),
        in_specs=[VM] * 10 + [HBM],
        out_specs=HBM,
        scratch_shapes=[
            pltpu.VMEM((width, MAXACT * cells), BF16),
            pltpu.VMEM((width, 2 * cells), F32),
            pltpu.VMEM((width, 2 * cells), F32),
            pltpu.VMEM((MAXACT, width, cells), BF16),
            pltpu.SemaphoreType.DMA((MAXACT,)),
        ],
        input_output_aliases={10: 0},
        compiler_params=pltpu.CompilerParams(vmem_limit_bytes=12 * 2**20),
        cost_estimate=pl.CostEstimate(flops=10**9, bytes_accessed=10**6, transcendentals=3 * 10**5),
        name="late",
    )(plan, one, two, fold, sums, base, cwt, mwt, blocks, folds, given)


def per_device(
    atm_in,
    ocean_in,
    lift_weight,
    conv_weight,
    flux_weight,
    ocean_weight,
    couple_weight,
    mix_weight,
    regrid_weight,
    pair_tile,
    ocean_mask,
):
    strips = lax.axis_size("lon")
    inward = [(i, i ^ 1) for i in range(strips)]
    outward = [(i, (i + 1 if i % 2 else i - 1) % strips) for i in range(strips)]
    met = dict(outward)
    mirror = [
        (i, (i + strips // 2) % strips if met[i] == strips - 1 - i else strips - 1 - i)
        for i in range(strips)
    ]
    fwt = flux_weight.T
    send_one, send_two, plan = first(atm_in, pair_tile.T, ocean_mask)
    two = lax.ppermute(send_two, "lon", outward)
    one = lax.ppermute(send_one, "lon", inward)
    hid, flux, taps, wc, lt = interior(atm_in, lift_weight, conv_weight, fwt)
    edges, tiles, north, send_one, send_two = edge(one, two, flux, taps, wc, lt, fwt)
    one = lax.ppermute(send_one, "lon", inward)
    two = lax.ppermute(send_two, "lon", outward)
    fold = lax.ppermute(north, "lon", mirror)
    atm_hidden, given, sums, base, cwt, mwt, blocks, folds = early(
        hid, edges, plan, tiles, ocean_in, regrid_weight,
        ocean_weight, couple_weight, mix_weight,
    )
    ocean_hidden = late(
        plan, one, two, fold, sums, base, cwt, mwt, blocks, folds, given
    )
    return (atm_hidden, ocean_hidden)


def solution(mesh):
    in_specs = (
        P(("groups", "lon"), None, None),
        P(("groups", "lon"), None, None),
        P(),
        P(),
        P(),
        P(),
        P(),
        P(),
        P("lon", None, None, None),
        P("lon", None),
        P("lon"),
    )
    out_specs = (P(("groups", "lon"), None, None), P(("groups", "lon"), None, None))

    return jax.shard_map(
        per_device, mesh=mesh, in_specs=in_specs, out_specs=out_specs, check_vma=False
    )
```

```python
import jax
import jax.numpy as jnp
from jax import lax
from jax.experimental import pallas as pl
from jax.experimental.pallas import tpu as pltpu
from jax.sharding import PartitionSpec as P


TLAT = 16
MAXACT = 8
FOLDB = 2
F32 = jnp.float32
BF16 = jnp.bfloat16
ROOT = 0.7978845608028654
CUBIC = ROOT * 0.044715

CHUNK = 256
STRIP = 32
BUFS = 2
AHEAD = 1
ASK = 8
TILE, OWN, WATER, COUNT = range(4)

HBM = pl.BlockSpec(memory_space=pltpu.HBM)
VM = pl.BlockSpec(memory_space=pltpu.VMEM)


def dot(a, b):
    return lax.dot_general(a, b, (((1,), (0,)), ((), ())), preferred_element_type=F32)


def dot_t(a, b):
    return lax.dot_general(a, b, (((1,), (1,)), ((), ())), preferred_element_type=F32)


def gelu_of_half(half):
    return half + half * jnp.tanh(half * (2.0 * ROOT + 8.0 * CUBIC * (half * half)))


def put_shifts(taps, at, column):
    chans, lats = column.shape
    lane = lax.broadcasted_iota(jnp.int32, column.shape, 1)
    zero = jnp.zeros(column.shape, BF16)
    taps[:chans, pl.ds(at, lats)] = jnp.where(lane == 0, zero, pltpu.roll(column, 1, 1))
    taps[chans : 2 * chans, pl.ds(at, lats)] = column
    taps[2 * chans :, pl.ds(at, lats)] = jnp.where(
        lane == lats - 1, zero, pltpu.roll(column, lats - 1, 1)
    )


def join(parts, axis):
    return parts[0] if len(parts) == 1 else jnp.concatenate(parts, axis)


def multiply(segments, wc, lt, conv, lifted):
    chans = lt.shape[1]
    rows = 3 * chans
    parts = []
    for a in range(3):
        parts.append(join([seg[a][0][:, pl.ds(seg[a][1], seg[3])] for seg in segments], 1))
    parts.append(jnp.zeros((wc.shape[1] - 3 * rows, parts[0].shape[1]), BF16))
    own = join([seg[1][0][chans : 2 * chans, pl.ds(seg[1][1], seg[3])] for seg in segments], 1)
    conv[...] = dot(wc[...], jnp.concatenate(parts, 0))
    lifted[...] = dot(lt[...], own).astype(BF16)


def activate(conv, lifted, out, stores):
    for r in range(0, conv.shape[0], STRIP):
        at = slice(r, r + STRIP)
        fresh = (lifted[at, :].astype(F32) + gelu_of_half(conv[at, :])).astype(BF16)
        out[at, :] = fresh
        for ref, first, lo, hi in stores:
            ref[at, pl.ds(first, hi - lo)] = fresh[:, lo:hi]


def parity():
    return lax.rem(lax.axis_index("lon"), 2)


def list_tiles(mask, chosen, count):
    for k in range(FOLDB):
        chosen[k] = count - FOLDB + k
    for k in range(FOLDB, MAXACT + 1):
        chosen[k] = count - 1
    found = jnp.int32(FOLDB)
    for t in range(count - FOLDB):
        chosen[jnp.minimum(found, MAXACT)] = t
        found = found + jnp.where(mask[t] == 1, 1, 0)
    return jnp.minimum(found, MAXACT)


def first_kernel(x_hbm, pair_hbm, mask_hbm, one, two, plan, pair, mask, chosen, sems):
    odd = parity()
    last = x_hbm.shape[0] - 1
    chans = x_hbm.shape[1]
    copies = [
        pltpu.make_async_copy(mask_hbm, mask, sems.at[0]),
        pltpu.make_async_copy(pair_hbm, pair, sems.at[1]),
        pltpu.make_async_copy(x_hbm.at[last * (1 - odd)], one.at[pl.ds(0, chans)], sems.at[2]),
        pltpu.make_async_copy(x_hbm.at[last * odd], two.at[pl.ds(0, chans)], sems.at[3]),
    ]
    for c in copies:
        c.start()
    copies[0].wait()
    found = list_tiles(mask, chosen, mask.shape[0])
    copies[1].wait()
    row = lax.broadcasted_iota(jnp.int32, plan.shape, 0)
    spot = lax.broadcasted_iota(jnp.int32, plan.shape, 1)
    facts = jnp.where(row == COUNT, found, jnp.zeros(plan.shape, jnp.int32))
    for k in range(MAXACT):
        facts = jnp.where((row == TILE) & (spot == k), chosen[k], facts)
        facts = jnp.where((row == OWN) & (spot == k), pair[1, chosen[k]], facts)
    for t in range(mask.shape[0]):
        facts = jnp.where((row == WATER) & (spot == t), mask[t], facts)
    plan[...] = facts
    lane = lax.broadcasted_iota(jnp.int32, (ASK, 128), 1)
    for ref, side in ((one, 2 - 2 * odd), (two, 2 * odd)):
        asked = jnp.zeros((ASK, 128), jnp.int32)
        for k in range(MAXACT):
            asked = jnp.where(lane == k, pair[side, chosen[k]], asked)
        ref[pl.ds(chans, ASK), :128] = asked.astype(F32).astype(BF16)
        ref[pl.ds(chans, ASK), 128:] = jnp.zeros((ASK, ref.shape[1] - 128), BF16)
    copies[2].wait()
    copies[3].wait()


def first(x, pair, mask):
    column = jax.ShapeDtypeStruct((x.shape[1] + ASK, x.shape[2]), BF16)
    given = [pltpu.with_memory_space_constraint(v, pltpu.HBM) for v in (x, pair, mask)]
    return pl.pallas_call(
        first_kernel,
        out_shape=(column, column, jax.ShapeDtypeStruct((8, 128), jnp.int32)),
        in_specs=[HBM] * 3,
        out_specs=(VM,) * 3,
        scratch_shapes=[
            pltpu.SMEM(pair.shape, jnp.int32),
            pltpu.SMEM(mask.shape, jnp.int32),
            pltpu.SMEM((MAXACT + 1,), jnp.int32),
            pltpu.SemaphoreType.DMA((4,)),
        ],
        compiler_params=pltpu.CompilerParams(vmem_limit_bytes=4 * 2**20),
        cost_estimate=pl.CostEstimate(flops=4 * 10**9, bytes_accessed=10**6, transcendentals=0),
        name="first",
    )(*given)


def inner_kernel(
    x, lift, conv, fwt,
    hid, flux, taps, wc, lt,
    comp, *bufs,
):
    columns, chans, lats = x.shape
    convs, lifts, outs = bufs[:BUFS], bufs[BUFS : 2 * BUFS], bufs[2 * BUFS :]
    width = lift.shape[1]
    comp[pl.ds(9 * chans, 2 * width - 9 * chans), :] = jnp.zeros((2 * width - 9 * chans, width), F32)
    half = 0.5 * lift[...]
    for a in range(3):
        for b in range(3):
            comp[pl.ds((3 * a + b) * chans, chans), :] = dot(half, conv[a, b])
    for side in range(2):
        at = slice(side * width, side * width + width)
        wc[:, at] = comp[at, :].T.astype(BF16)
    lt[...] = lift[...].astype(F32).T.astype(BF16)
    for i in range(columns):
        put_shifts(taps, i * lats, x[i])

    def feed(j):
        at = [j * CHUNK + a * lats for a in range(3)]
        multiply([[(taps, p) for p in at] + [CHUNK]], wc, lt, convs[j % BUFS], lifts[j % BUFS])

    def finish(j):
        activate(convs[j % BUFS], lifts[j % BUFS], outs[j % 2], [(hid, j * CHUNK, 0, CHUNK)])

    def head(j):
        flux[:, j * CHUNK : (j + 1) * CHUNK] = dot(fwt[...], outs[j % 2][...])

    chunks = (columns - 2) * lats // CHUNK
    for j in range(AHEAD):
        feed(j)
    for j in range(chunks):
        if j + AHEAD < chunks:
            feed(j + AHEAD)
        finish(j)
        if j:
            head(j - 1)
    head(chunks - 1)


def interior(x, lift, conv, fwt):
    columns, chans, lats = x.shape
    width = lift.shape[1]
    fluxes = fwt.shape[0]
    inner = (columns - 2) * lats
    return pl.pallas_call(
        inner_kernel,
        out_shape=(
            jax.ShapeDtypeStruct((width, inner), BF16),
            jax.ShapeDtypeStruct((fluxes, inner), F32),
            jax.ShapeDtypeStruct((3 * chans, columns * lats), BF16),
            jax.ShapeDtypeStruct((width, 2 * width), BF16),
            jax.ShapeDtypeStruct((width, chans), BF16),
        ),
        in_specs=[VM] * 4,
        out_specs=(VM,) * 5,
        scratch_shapes=[
            pltpu.VMEM((2 * width, width), F32),
        ]
        + [pltpu.VMEM((width, CHUNK), F32)] * BUFS
        + [pltpu.VMEM((width, CHUNK), BF16)] * (BUFS + 2),
        compiler_params=pltpu.CompilerParams(vmem_limit_bytes=12 * 2**20),
        cost_estimate=pl.CostEstimate(flops=4 * 10**9, bytes_accessed=4 * 10**6, transcendentals=10**6),
        name="interior",
    )(x, lift, conv, fwt)


def swap_blocks(values, lanes):
    count = len(values)
    lane = lax.broadcasted_iota(jnp.int32, values[0].shape, 1)
    step = count // 2
    while step:
        shift = step * TLAT
        upper = (lane & shift) != 0
        fresh = list(values)
        for i in range(count):
            if i & step:
                continue
            low, high = values[i], values[i + step]
            fresh[i] = jnp.where(upper, pltpu.roll(high, shift, 1), low)
            fresh[i + step] = jnp.where(upper, high, pltpu.roll(low, lanes - shift, 1))
        values = fresh
        step //= 2
    return values


def edge_kernel(
    one, two, flux_in, taps, wc, lt, fwt,
    edges, tiles, north, send_one, send_two,
    halo, flux, ca, cb, la, lb, oa, ob,
):
    lats = one.shape[1]
    chans = lt.shape[1]
    columns = taps.shape[1] // lats
    lists = []
    for ref in (one, two):
        wanted = ref[pl.ds(chans, ASK), :128].astype(F32).astype(jnp.int32)
        wanted = jnp.clip(wanted, 0, lats // TLAT - 1)
        lists.append([wanted[0, k] for k in range(MAXACT)])
    odd = parity()
    put_shifts(halo, pl.multiple_of(lats * (1 - odd), 128), one[pl.ds(0, chans), :])
    put_shifts(halo, pl.multiple_of(lats * odd, 128), two[pl.ds(0, chans), :])
    sides = [
        [(halo, 0), (taps, 0), (taps, lats)],
        [(taps, (columns - 2) * lats), (taps, (columns - 1) * lats), (halo, lats)],
    ]
    work = []
    full = lats // CHUNK * CHUNK
    for lo in range(0, full, CHUNK):
        for side in range(2):
            work.append([(side, lo, CHUNK)])
    if full < lats:
        work.append([(0, full, lats - full), (1, full, lats - full)])
    bufs = [(ca, la, oa), (cb, lb, ob)]

    def feed(j):
        segments = []
        for side, lo, size in work[j]:
            segments.append([(ref, at + lo) for ref, at in sides[side]] + [size])
        multiply(segments, wc, lt, bufs[j % 2][0], bufs[j % 2][1])

    def finish(j):
        stores = []
        at = 0
        for side, lo, size in work[j]:
            stores.append((edges.at[side], lo, at, at + size))
            at += size
        activate(bufs[j % 2][0], bufs[j % 2][1], bufs[j % 2][2], stores)

    def head(j):
        got = dot(fwt[...], bufs[j % 2][2][...])
        at = 0
        for side, lo, size in work[j]:
            flux[side, :, lo : lo + size] = got[:, at : at + size]
            at += size

    group = 128 // TLAT
    north_tile = lats // TLAT - 1

    def swap(g):
        at = slice(g * 128, g * 128 + 128)
        values = [flux[0, :, at]]
        for i in range(columns - 2):
            values.append(flux_in[:, i * lats + g * 128 : i * lats + g * 128 + 128])
        values.append(flux[1, :, at])
        for a, v in enumerate(swap_blocks(values, 128)):
            tiles[g * group + a] = v.astype(BF16)
            if g * group + a == north_tile:
                for ref in (north, send_one.at[MAXACT], send_two.at[MAXACT]):
                    ref[...] = v.astype(BF16)

    ready, seen = [], [0, 0]
    for pieces in work:
        for side, lo, size in pieces:
            seen[side] = lo + size
        ready.append(min(seen) // 128)
    feed(0)
    swapped = 0
    for j in range(len(work)):
        if j + 1 < len(work):
            feed(j + 1)
        finish(j)
        if j:
            head(j - 1)
            for g in range(swapped, ready[j - 1]):
                swap(g)
            swapped = ready[j - 1]
    head(len(work) - 1)
    for g in range(swapped, lats // 128):
        swap(g)
    for k in range(MAXACT):
        send_one[k] = tiles[lists[0][k]]
        send_two[k] = tiles[lists[1][k]]


def edge(one, two, flux_in, taps, wc, lt, fwt):
    lats = one.shape[1]
    columns = taps.shape[1] // lats
    width, chans = lt.shape
    fluxes = fwt.shape[0]
    cells = columns * TLAT
    return pl.pallas_call(
        edge_kernel,
        out_shape=(
            jax.ShapeDtypeStruct((2, width, lats), BF16),
            jax.ShapeDtypeStruct((lats // TLAT, fluxes, cells), BF16),
            jax.ShapeDtypeStruct((fluxes, cells), BF16),
            jax.ShapeDtypeStruct((MAXACT + 1, fluxes, cells), BF16),
            jax.ShapeDtypeStruct((MAXACT + 1, fluxes, cells), BF16),
        ),
        in_specs=[VM] * 7,
        out_specs=(VM,) * 5,
        scratch_shapes=[
            pltpu.VMEM((3 * chans, 2 * lats), BF16),
            pltpu.VMEM((2, fluxes, lats), F32),
            pltpu.VMEM((width, CHUNK), F32),
            pltpu.VMEM((width, CHUNK), F32),
            pltpu.VMEM((width, CHUNK), BF16),
            pltpu.VMEM((width, CHUNK), BF16),
            pltpu.VMEM((width, CHUNK), BF16),
            pltpu.VMEM((width, CHUNK), BF16),
        ],
        compiler_params=pltpu.CompilerParams(vmem_limit_bytes=12 * 2**20),
        cost_estimate=pl.CostEstimate(flops=10**9, bytes_accessed=10**6, transcendentals=3 * 10**5),
        name="edge",
    )(one, two, flux_in, taps, wc, lt, fwt)


def early_kernel(
    hid, edges, plan, tiles, ocean, regrid, ow, cw, mw,
    hid_out, out_hbm, sums, base, cwt, mwt, blocks, folds,
    zero, sems,
):
    count = ocean.shape[0]
    cells = ocean.shape[2]
    columns, _, lats = hid_out.shape
    zero[...] = jnp.zeros(zero.shape, BF16)
    out = [
        pltpu.make_async_copy(edges.at[0], hid_out.at[0], sems.at[0]),
        pltpu.make_async_copy(edges.at[1], hid_out.at[columns - 1], sems.at[1]),
    ]
    for i in range(columns - 2):
        out.append(
            pltpu.make_async_copy(hid.at[:, pl.ds(i * lats, lats)], hid_out.at[i + 1], sems.at[2 + i])
        )
    for c in out:
        c.start()
    facts = plan[...]
    water = [facts[WATER, t] == 1 for t in range(count - FOLDB)]
    for t in range(count - FOLDB):

        @pl.when(jnp.logical_not(water[t]))
        def _():
            pltpu.make_async_copy(zero, out_hbm.at[t], sems.at[columns]).start()

    cwt[...] = cw[...].astype(F32).T.astype(BF16)
    mwt[...] = (0.5 * mw[...].astype(F32)).T.astype(BF16)
    owt = ow[...].astype(F32).T.astype(BF16)
    ones = jnp.ones(tiles.shape[1:], BF16)
    for k in range(MAXACT):
        t = facts[TILE, k]
        at = slice(k * cells, k * cells + cells)
        mine = jnp.concatenate([tiles[facts[OWN, k]], ones], 0)
        sums[:, at] = dot_t(mine, regrid[t, 1])
        base[:, at] = dot(owt, ocean[t])
        for side in range(2):
            blocks[at, side * cells : (side + 1) * cells] = regrid[t, 2 * side]
        if k < FOLDB:
            folds[at, :] = regrid[t, 3]
    for t in range(count - FOLDB):

        @pl.when(jnp.logical_not(water[t]))
        def _():
            pltpu.make_async_copy(zero, out_hbm.at[t], sems.at[columns]).wait()

    for c in out:
        c.wait()


def early(hid, edges, plan, tiles, ocean, regrid, ow, cw, mw):
    count, _, cells = ocean.shape
    width = mw.shape[0]
    fluxes = cw.shape[0]
    lats = edges.shape[2]
    columns = hid.shape[1] // lats + 2
    return pl.pallas_call(
        early_kernel,
        out_shape=(
            jax.ShapeDtypeStruct((columns, width, lats), BF16),
            jax.ShapeDtypeStruct((count, width, cells), BF16),
            jax.ShapeDtypeStruct((2 * fluxes, MAXACT * cells), F32),
            jax.ShapeDtypeStruct((width, MAXACT * cells), F32),
            jax.ShapeDtypeStruct((width, fluxes), BF16),
            jax.ShapeDtypeStruct((width, width), BF16),
            jax.ShapeDtypeStruct((MAXACT * cells, 2 * cells), BF16),
            jax.ShapeDtypeStruct((FOLDB * cells, cells), BF16),
        ),
        in_specs=[VM] * 9,
        out_specs=(HBM, HBM) + (VM,) * 6,
        scratch_shapes=[
            pltpu.VMEM((width, cells), BF16),
            pltpu.SemaphoreType.DMA((columns + 1,)),
        ],
        compiler_params=pltpu.CompilerParams(vmem_limit_bytes=12 * 2**20),
        cost_estimate=pl.CostEstimate(flops=10**9, bytes_accessed=6 * 10**6, transcendentals=0),
        name="early",
    )(hid, edges, plan, tiles, ocean, regrid, ow, cw, mw)


def late_kernel(
    plan, one, two, fold, sums, base, cwt, mwt, blocks, folds, given_hbm,
    out_hbm,
    state, mixed_even, mixed_odd, out, sems,
):
    fluxes = fold.shape[0]
    cells = out.shape[2]
    pairs = MAXACT // 2
    wide = 2 * cells
    strip, strips = lax.axis_index("lon"), lax.axis_size("lon")
    odd = lax.rem(strip, 2)
    met = lax.rem(strip + 2 * odd - 1 + strips, strips) == strips - 1 - strip
    odd = odd == 1
    partner = jnp.where(met, two[MAXACT], fold[...])
    ones = jnp.ones(fold.shape, BF16)

    def got(k):
        west = jnp.where(odd, one[k], two[k])
        east = jnp.where(odd, two[k], one[k])
        return [jnp.concatenate([west, east], 1), jnp.concatenate([ones, ones], 1)]

    half = 2 * fluxes

    def settle(group):
        totals = []
        for p in group:
            at = slice(p * wide, p * wide + wide)
            product = dot_t(jnp.concatenate(got(2 * p) + got(2 * p + 1), 0), blocks[at, :])
            total = jnp.concatenate([product[:half, :cells], product[half:, cells:]], 1) + sums[:, at]
            if 2 * p < FOLDB:
                total = total + dot_t(jnp.concatenate([partner, ones], 0), folds[at, :])
            totals.append(total)
        for p, total in zip(group, totals):
            at = slice(p * wide, p * wide + wide)
            regrid = (total[:fluxes] / total[fluxes : fluxes + 1]).astype(BF16)
            state[:, at] = (base[:, at] + dot(cwt[...], regrid)).astype(BF16)

    mixed = (mixed_even, mixed_odd)

    def mix(p):
        mixed[p % 2][...] = dot(mwt[...], state[:, p * wide : p * wide + wide])

    def finish(p):
        for r in range(0, state.shape[0], STRIP):
            at = slice(r, r + STRIP)
            for side in range(2):
                k = 2 * p + side
                own = state[at, k * cells : (k + 1) * cells].astype(F32)
                gate = mixed[p % 2][at, side * cells : (side + 1) * cells]
                out[k, at, :] = (own + gelu_of_half(gate)).astype(BF16)

    facts = plan[...]
    found = facts[COUNT, 0]
    chosen = [facts[TILE, k] for k in range(MAXACT)]

    def send(k):
        return pltpu.make_async_copy(out.at[k], out_hbm.at[chosen[k]], sems.at[k])

    def run(group):
        settle(group)
        mix(group[0])
        for p in group:
            if p + 1 in group:
                mix(p + 1)
            finish(p)
            for k in (2 * p, 2 * p + 1):
                if k < FOLDB:
                    send(k).start()
                else:
                    pl.when(k < found)(lambda k=k: send(k).start())

    run(range(pairs // 2))

    @pl.when(found > pairs // 2 * 2)
    def _():
        run(range(pairs // 2, pairs))

    for k in range(MAXACT):
        if k < FOLDB:
            send(k).wait()
        else:
            pl.when(k < found)(lambda k=k: send(k).wait())


def late(plan, one, two, fold, sums, base, cwt, mwt, blocks, folds, given):
    count, width, cells = given.shape
    return pl.pallas_call(
        late_kernel,
        out_shape=jax.ShapeDtypeStruct((count, width, cells), BF16),
        in_specs=[VM] * 10 + [HBM],
        out_specs=HBM,
        scratch_shapes=[
            pltpu.VMEM((width, MAXACT * cells), BF16),
            pltpu.VMEM((width, 2 * cells), F32),
            pltpu.VMEM((width, 2 * cells), F32),
            pltpu.VMEM((MAXACT, width, cells), BF16),
            pltpu.SemaphoreType.DMA((MAXACT,)),
        ],
        input_output_aliases={10: 0},
        compiler_params=pltpu.CompilerParams(vmem_limit_bytes=12 * 2**20),
        cost_estimate=pl.CostEstimate(flops=10**9, bytes_accessed=10**6, transcendentals=3 * 10**5),
        name="late",
    )(plan, one, two, fold, sums, base, cwt, mwt, blocks, folds, given)


def per_device(
    atm_in,
    ocean_in,
    lift_weight,
    conv_weight,
    flux_weight,
    ocean_weight,
    couple_weight,
    mix_weight,
    regrid_weight,
    pair_tile,
    ocean_mask,
):
    strips = lax.axis_size("lon")
    inward = [(i, i ^ 1) for i in range(strips)]
    outward = [(i, (i + 1 if i % 2 else i - 1) % strips) for i in range(strips)]
    met = dict(outward)
    mirror = [
        (i, (i + strips // 2) % strips if met[i] == strips - 1 - i else strips - 1 - i)
        for i in range(strips)
    ]
    fwt = flux_weight.T
    send_one, send_two, plan = first(atm_in, pair_tile.T, ocean_mask)
    two = lax.ppermute(send_two, "lon", outward)
    one = lax.ppermute(send_one, "lon", inward)
    hid, flux, taps, wc, lt = interior(atm_in, lift_weight, conv_weight, fwt)
    edges, tiles, north, send_one, send_two = edge(one, two, flux, taps, wc, lt, fwt)
    one = lax.ppermute(send_one, "lon", inward)
    two = lax.ppermute(send_two, "lon", outward)
    fold = lax.ppermute(north, "lon", mirror)
    atm_hidden, given, sums, base, cwt, mwt, blocks, folds = early(
        hid, edges, plan, tiles, ocean_in, regrid_weight,
        ocean_weight, couple_weight, mix_weight,
    )
    ocean_hidden = late(
        plan, one, two, fold, sums, base, cwt, mwt, blocks, folds, given
    )
    return (atm_hidden, ocean_hidden)


def solution(mesh):
    in_specs = (
        P(("groups", "lon"), None, None),
        P(("groups", "lon"), None, None),
        P(),
        P(),
        P(),
        P(),
        P(),
        P(),
        P("lon", None, None, None),
        P("lon", None),
        P("lon"),
    )
    out_specs = (P(("groups", "lon"), None, None), P(("groups", "lon"), None, None))

    return jax.shard_map(
        per_device, mesh=mesh, in_specs=in_specs, out_specs=out_specs, check_vma=False
    )
```

```python
import jax
import jax.numpy as jnp
from jax import lax
from jax.experimental import pallas as pl
from jax.experimental.pallas import tpu as pltpu
from jax.sharding import PartitionSpec as P


TLAT = 16
MAXACT = 8
FOLDB = 2
F32 = jnp.float32
BF16 = jnp.bfloat16
ROOT = 0.7978845608028654
CUBIC = ROOT * 0.044715

CHUNK = 256
STRIP = 32
BUFS = 2
AHEAD = 1
ASK = 8
TILE, OWN, WATER, COUNT = range(4)

HBM = pl.BlockSpec(memory_space=pltpu.HBM)
VM = pl.BlockSpec(memory_space=pltpu.VMEM)


def dot(a, b):
    return lax.dot_general(a, b, (((1,), (0,)), ((), ())), preferred_element_type=F32)


def dot_t(a, b):
    return lax.dot_general(a, b, (((1,), (1,)), ((), ())), preferred_element_type=F32)


def gelu_of_half(half):
    return half + half * jnp.tanh(half * (2.0 * ROOT + 8.0 * CUBIC * (half * half)))


def put_shifts(taps, at, column):
    chans, lats = column.shape
    lane = lax.broadcasted_iota(jnp.int32, column.shape, 1)
    zero = jnp.zeros(column.shape, BF16)
    taps[:chans, pl.ds(at, lats)] = jnp.where(lane == 0, zero, pltpu.roll(column, 1, 1))
    taps[chans : 2 * chans, pl.ds(at, lats)] = column
    taps[2 * chans :, pl.ds(at, lats)] = jnp.where(
        lane == lats - 1, zero, pltpu.roll(column, lats - 1, 1)
    )


def join(parts, axis):
    return parts[0] if len(parts) == 1 else jnp.concatenate(parts, axis)


def multiply(segments, wc, lt, conv, lifted):
    chans = lt.shape[1]
    rows = 3 * chans
    parts = []
    for a in range(3):
        parts.append(join([seg[a][0][:, pl.ds(seg[a][1], seg[3])] for seg in segments], 1))
    parts.append(jnp.zeros((wc.shape[1] - 3 * rows, parts[0].shape[1]), BF16))
    own = join([seg[1][0][chans : 2 * chans, pl.ds(seg[1][1], seg[3])] for seg in segments], 1)
    conv[...] = dot(wc[...], jnp.concatenate(parts, 0))
    lifted[...] = dot(lt[...], own).astype(BF16)


def activate(conv, lifted, out, stores):
    for r in range(0, conv.shape[0], STRIP):
        at = slice(r, r + STRIP)
        fresh = (lifted[at, :].astype(F32) + gelu_of_half(conv[at, :])).astype(BF16)
        out[at, :] = fresh
        for ref, first, lo, hi in stores:
            ref[at, pl.ds(first, hi - lo)] = fresh[:, lo:hi]


def parity():
    return lax.rem(lax.axis_index("lon"), 2)


def list_tiles(mask, chosen, count):
    for k in range(FOLDB):
        chosen[k] = count - FOLDB + k
    for k in range(FOLDB, MAXACT + 1):
        chosen[k] = count - 1
    found = jnp.int32(FOLDB)
    for t in range(count - FOLDB):
        chosen[jnp.minimum(found, MAXACT)] = t
        found = found + jnp.where(mask[t] == 1, 1, 0)
    return jnp.minimum(found, MAXACT)


def first_kernel(x_hbm, pair_hbm, mask_hbm, one, two, plan, pair, mask, chosen, sems):
    odd = parity()
    last = x_hbm.shape[0] - 1
    chans = x_hbm.shape[1]
    copies = [
        pltpu.make_async_copy(mask_hbm, mask, sems.at[0]),
        pltpu.make_async_copy(pair_hbm, pair, sems.at[1]),
        pltpu.make_async_copy(x_hbm.at[last * (1 - odd)], one.at[pl.ds(0, chans)], sems.at[2]),
        pltpu.make_async_copy(x_hbm.at[last * odd], two.at[pl.ds(0, chans)], sems.at[3]),
    ]
    for c in copies:
        c.start()
    copies[0].wait()
    found = list_tiles(mask, chosen, mask.shape[0])
    copies[1].wait()
    row = lax.broadcasted_iota(jnp.int32, plan.shape, 0)
    spot = lax.broadcasted_iota(jnp.int32, plan.shape, 1)
    facts = jnp.where(row == COUNT, found, jnp.zeros(plan.shape, jnp.int32))
    for k in range(MAXACT):
        facts = jnp.where((row == TILE) & (spot == k), chosen[k], facts)
        facts = jnp.where((row == OWN) & (spot == k), pair[1, chosen[k]], facts)
    for t in range(mask.shape[0]):
        facts = jnp.where((row == WATER) & (spot == t), mask[t], facts)
    plan[...] = facts
    lane = lax.broadcasted_iota(jnp.int32, (ASK, 128), 1)
    for ref, side in ((one, 2 - 2 * odd), (two, 2 * odd)):
        asked = jnp.zeros((ASK, 128), jnp.int32)
        for k in range(MAXACT):
            asked = jnp.where(lane == k, pair[side, chosen[k]], asked)
        ref[pl.ds(chans, ASK), :128] = asked.astype(F32).astype(BF16)
        ref[pl.ds(chans, ASK), 128:] = jnp.zeros((ASK, ref.shape[1] - 128), BF16)
    copies[2].wait()
    copies[3].wait()


def first(x, pair, mask):
    column = jax.ShapeDtypeStruct((x.shape[1] + ASK, x.shape[2]), BF16)
    given = [pltpu.with_memory_space_constraint(v, pltpu.HBM) for v in (x, pair, mask)]
    return pl.pallas_call(
        first_kernel,
        out_shape=(column, column, jax.ShapeDtypeStruct((8, 128), jnp.int32)),
        in_specs=[HBM] * 3,
        out_specs=(VM,) * 3,
        scratch_shapes=[
            pltpu.SMEM(pair.shape, jnp.int32),
            pltpu.SMEM(mask.shape, jnp.int32),
            pltpu.SMEM((MAXACT + 1,), jnp.int32),
            pltpu.SemaphoreType.DMA((4,)),
        ],
        compiler_params=pltpu.CompilerParams(vmem_limit_bytes=4 * 2**20),
        cost_estimate=pl.CostEstimate(flops=4 * 10**9, bytes_accessed=10**6, transcendentals=0),
        name="first",
    )(*given)


def inner_kernel(
    x, lift, conv, fwt,
    hid, flux, taps, wc, lt,
    comp, *bufs,
):
    columns, chans, lats = x.shape
    convs, lifts, outs = bufs[:BUFS], bufs[BUFS : 2 * BUFS], bufs[2 * BUFS :]
    width = lift.shape[1]
    comp[pl.ds(9 * chans, 2 * width - 9 * chans), :] = jnp.zeros((2 * width - 9 * chans, width), F32)
    half = 0.5 * lift[...]
    for a in range(3):
        for b in range(3):
            comp[pl.ds((3 * a + b) * chans, chans), :] = dot(half, conv[a, b])
    for side in range(2):
        at = slice(side * width, side * width + width)
        wc[:, at] = comp[at, :].T.astype(BF16)
    lt[...] = lift[...].astype(F32).T.astype(BF16)
    for i in range(columns):
        put_shifts(taps, i * lats, x[i])

    def feed(j):
        at = [j * CHUNK + a * lats for a in range(3)]
        multiply([[(taps, p) for p in at] + [CHUNK]], wc, lt, convs[j % BUFS], lifts[j % BUFS])

    def finish(j):
        activate(convs[j % BUFS], lifts[j % BUFS], outs[j % 2], [(hid, j * CHUNK, 0, CHUNK)])

    def head(j):
        flux[:, j * CHUNK : (j + 1) * CHUNK] = dot(fwt[...], outs[j % 2][...])

    chunks = (columns - 2) * lats // CHUNK
    for j in range(AHEAD):
        feed(j)
    for j in range(chunks):
        if j + AHEAD < chunks:
            feed(j + AHEAD)
        finish(j)
        if j:
            head(j - 1)
    head(chunks - 1)


def interior(x, lift, conv, fwt):
    columns, chans, lats = x.shape
    width = lift.shape[1]
    fluxes = fwt.shape[0]
    inner = (columns - 2) * lats
    return pl.pallas_call(
        inner_kernel,
        out_shape=(
            jax.ShapeDtypeStruct((width, inner), BF16),
            jax.ShapeDtypeStruct((fluxes, inner), F32),
            jax.ShapeDtypeStruct((3 * chans, columns * lats), BF16),
            jax.ShapeDtypeStruct((width, 2 * width), BF16),
            jax.ShapeDtypeStruct((width, chans), BF16),
        ),
        in_specs=[VM] * 4,
        out_specs=(VM,) * 5,
        scratch_shapes=[
            pltpu.VMEM((2 * width, width), F32),
        ]
        + [pltpu.VMEM((width, CHUNK), F32)] * BUFS
        + [pltpu.VMEM((width, CHUNK), BF16)] * (BUFS + 2),
        compiler_params=pltpu.CompilerParams(vmem_limit_bytes=12 * 2**20),
        cost_estimate=pl.CostEstimate(flops=4 * 10**9, bytes_accessed=4 * 10**6, transcendentals=10**6),
        name="interior",
    )(x, lift, conv, fwt)


def swap_blocks(values, lanes):
    count = len(values)
    lane = lax.broadcasted_iota(jnp.int32, values[0].shape, 1)
    step = count // 2
    while step:
        shift = step * TLAT
        upper = (lane & shift) != 0
        fresh = list(values)
        for i in range(count):
            if i & step:
                continue
            low, high = values[i], values[i + step]
            fresh[i] = jnp.where(upper, pltpu.roll(high, shift, 1), low)
            fresh[i + step] = jnp.where(upper, high, pltpu.roll(low, lanes - shift, 1))
        values = fresh
        step //= 2
    return values


def edge_kernel(
    one, two, flux_in, taps, wc, lt, fwt,
    edges, tiles, north, send_one, send_two,
    halo, flux, ca, cb, la, lb, oa, ob,
):
    lats = one.shape[1]
    chans = lt.shape[1]
    columns = taps.shape[1] // lats
    lists = []
    for ref in (one, two):
        wanted = ref[pl.ds(chans, ASK), :128].astype(F32).astype(jnp.int32)
        wanted = jnp.clip(wanted, 0, lats // TLAT - 1)
        lists.append([wanted[0, k] for k in range(MAXACT)])
    odd = parity()
    put_shifts(halo, pl.multiple_of(lats * (1 - odd), 128), one[pl.ds(0, chans), :])
    put_shifts(halo, pl.multiple_of(lats * odd, 128), two[pl.ds(0, chans), :])
    sides = [
        [(halo, 0), (taps, 0), (taps, lats)],
        [(taps, (columns - 2) * lats), (taps, (columns - 1) * lats), (halo, lats)],
    ]
    work = []
    full = lats // CHUNK * CHUNK
    for lo in range(0, full, CHUNK):
        for side in range(2):
            work.append([(side, lo, CHUNK)])
    if full < lats:
        work.append([(0, full, lats - full), (1, full, lats - full)])
    bufs = [(ca, la, oa), (cb, lb, ob)]

    def feed(j):
        segments = []
        for side, lo, size in work[j]:
            segments.append([(ref, at + lo) for ref, at in sides[side]] + [size])
        multiply(segments, wc, lt, bufs[j % 2][0], bufs[j % 2][1])

    def finish(j):
        stores = []
        at = 0
        for side, lo, size in work[j]:
            stores.append((edges.at[side], lo, at, at + size))
            at += size
        activate(bufs[j % 2][0], bufs[j % 2][1], bufs[j % 2][2], stores)

    def head(j):
        got = dot(fwt[...], bufs[j % 2][2][...])
        at = 0
        for side, lo, size in work[j]:
            flux[side, :, lo : lo + size] = got[:, at : at + size]
            at += size

    group = 128 // TLAT
    north_tile = lats // TLAT - 1

    def swap(g):
        at = slice(g * 128, g * 128 + 128)
        values = [flux[0, :, at]]
        for i in range(columns - 2):
            values.append(flux_in[:, i * lats + g * 128 : i * lats + g * 128 + 128])
        values.append(flux[1, :, at])
        for a, v in enumerate(swap_blocks(values, 128)):
            tiles[g * group + a] = v.astype(BF16)
            if g * group + a == north_tile:
                for ref in (north, send_one.at[MAXACT], send_two.at[MAXACT]):
                    ref[...] = v.astype(BF16)

    ready, seen = [], [0, 0]
    for pieces in work:
        for side, lo, size in pieces:
            seen[side] = lo + size
        ready.append(min(seen) // 128)
    feed(0)
    swapped = 0
    for j in range(len(work)):
        if j + 1 < len(work):
            feed(j + 1)
        finish(j)
        if j:
            head(j - 1)
            for g in range(swapped, ready[j - 1]):
                swap(g)
            swapped = ready[j - 1]
    head(len(work) - 1)
    for g in range(swapped, lats // 128):
        swap(g)
    for k in range(MAXACT):
        send_one[k] = tiles[lists[0][k]]
        send_two[k] = tiles[lists[1][k]]


def edge(one, two, flux_in, taps, wc, lt, fwt):
    lats = one.shape[1]
    columns = taps.shape[1] // lats
    width, chans = lt.shape
    fluxes = fwt.shape[0]
    cells = columns * TLAT
    return pl.pallas_call(
        edge_kernel,
        out_shape=(
            jax.ShapeDtypeStruct((2, width, lats), BF16),
            jax.ShapeDtypeStruct((lats // TLAT, fluxes, cells), BF16),
            jax.ShapeDtypeStruct((fluxes, cells), BF16),
            jax.ShapeDtypeStruct((MAXACT + 1, fluxes, cells), BF16),
            jax.ShapeDtypeStruct((MAXACT + 1, fluxes, cells), BF16),
        ),
        in_specs=[VM] * 7,
        out_specs=(VM,) * 5,
        scratch_shapes=[
            pltpu.VMEM((3 * chans, 2 * lats), BF16),
            pltpu.VMEM((2, fluxes, lats), F32),
            pltpu.VMEM((width, CHUNK), F32),
            pltpu.VMEM((width, CHUNK), F32),
            pltpu.VMEM((width, CHUNK), BF16),
            pltpu.VMEM((width, CHUNK), BF16),
            pltpu.VMEM((width, CHUNK), BF16),
            pltpu.VMEM((width, CHUNK), BF16),
        ],
        compiler_params=pltpu.CompilerParams(vmem_limit_bytes=12 * 2**20),
        cost_estimate=pl.CostEstimate(flops=10**9, bytes_accessed=10**6, transcendentals=3 * 10**5),
        name="edge",
    )(one, two, flux_in, taps, wc, lt, fwt)


def early_kernel(
    hid, edges, plan, tiles, ocean, regrid, ow, cw, mw,
    hid_out, out_hbm, sums, base, cwt, mwt, blocks, folds,
    zero, sems,
):
    count = ocean.shape[0]
    cells = ocean.shape[2]
    columns, _, lats = hid_out.shape
    zero[...] = jnp.zeros(zero.shape, BF16)
    out = [
        pltpu.make_async_copy(edges.at[0], hid_out.at[0], sems.at[0]),
        pltpu.make_async_copy(edges.at[1], hid_out.at[columns - 1], sems.at[1]),
    ]
    for i in range(columns - 2):
        out.append(
            pltpu.make_async_copy(hid.at[:, pl.ds(i * lats, lats)], hid_out.at[i + 1], sems.at[2 + i])
        )
    for c in out:
        c.start()
    facts = plan[...]
    water = [facts[WATER, t] == 1 for t in range(count - FOLDB)]
    for t in range(count - FOLDB):

        @pl.when(jnp.logical_not(water[t]))
        def _():
            pltpu.make_async_copy(zero, out_hbm.at[t], sems.at[columns]).start()

    cwt[...] = cw[...].astype(F32).T.astype(BF16)
    mwt[...] = (0.5 * mw[...].astype(F32)).T.astype(BF16)
    owt = ow[...].astype(F32).T.astype(BF16)
    ones = jnp.ones(tiles.shape[1:], BF16)
    for k in range(MAXACT):
        t = facts[TILE, k]
        at = slice(k * cells, k * cells + cells)
        mine = jnp.concatenate([tiles[facts[OWN, k]], ones], 0)
        sums[:, at] = dot_t(mine, regrid[t, 1])
        base[:, at] = dot(owt, ocean[t])
        for side in range(2):
            blocks[at, side * cells : (side + 1) * cells] = regrid[t, 2 * side]
        if k < FOLDB:
            folds[at, :] = regrid[t, 3]
    for t in range(count - FOLDB):

        @pl.when(jnp.logical_not(water[t]))
        def _():
            pltpu.make_async_copy(zero, out_hbm.at[t], sems.at[columns]).wait()

    for c in out:
        c.wait()


def early(hid, edges, plan, tiles, ocean, regrid, ow, cw, mw):
    count, _, cells = ocean.shape
    width = mw.shape[0]
    fluxes = cw.shape[0]
    lats = edges.shape[2]
    columns = hid.shape[1] // lats + 2
    return pl.pallas_call(
        early_kernel,
        out_shape=(
            jax.ShapeDtypeStruct((columns, width, lats), BF16),
            jax.ShapeDtypeStruct((count, width, cells), BF16),
            jax.ShapeDtypeStruct((2 * fluxes, MAXACT * cells), F32),
            jax.ShapeDtypeStruct((width, MAXACT * cells), F32),
            jax.ShapeDtypeStruct((width, fluxes), BF16),
            jax.ShapeDtypeStruct((width, width), BF16),
            jax.ShapeDtypeStruct((MAXACT * cells, 2 * cells), BF16),
            jax.ShapeDtypeStruct((FOLDB * cells, cells), BF16),
        ),
        in_specs=[VM] * 9,
        out_specs=(HBM, HBM) + (VM,) * 6,
        scratch_shapes=[
            pltpu.VMEM((width, cells), BF16),
            pltpu.SemaphoreType.DMA((columns + 1,)),
        ],
        compiler_params=pltpu.CompilerParams(vmem_limit_bytes=12 * 2**20),
        cost_estimate=pl.CostEstimate(flops=10**9, bytes_accessed=6 * 10**6, transcendentals=0),
        name="early",
    )(hid, edges, plan, tiles, ocean, regrid, ow, cw, mw)


def late_kernel(
    plan, one, two, fold, sums, base, cwt, mwt, blocks, folds, given_hbm,
    out_hbm,
    state, mixed, out, sems,
):
    fluxes = fold.shape[0]
    cells = out.shape[2]
    pairs = MAXACT // 2
    wide = 2 * cells
    strip, strips = lax.axis_index("lon"), lax.axis_size("lon")
    odd = lax.rem(strip, 2)
    met = lax.rem(strip + 2 * odd - 1 + strips, strips) == strips - 1 - strip
    odd = odd == 1
    partner = jnp.where(met, two[MAXACT], fold[...])
    ones = jnp.ones(fold.shape, BF16)

    def got(k):
        west = jnp.where(odd, one[k], two[k])
        east = jnp.where(odd, two[k], one[k])
        return [jnp.concatenate([west, east], 1), jnp.concatenate([ones, ones], 1)]

    half = 2 * fluxes

    def settle(group):
        totals = []
        for p in group:
            at = slice(p * wide, p * wide + wide)
            product = dot_t(jnp.concatenate(got(2 * p) + got(2 * p + 1), 0), blocks[at, :])
            total = jnp.concatenate([product[:half, :cells], product[half:, cells:]], 1) + sums[:, at]
            if 2 * p < FOLDB:
                total = total + dot_t(jnp.concatenate([partner, ones], 0), folds[at, :])
            totals.append(total)
        for p, total in zip(group, totals):
            at = slice(p * wide, p * wide + wide)
            regrid = (total[:fluxes] / total[fluxes : fluxes + 1]).astype(BF16)
            state[:, at] = (base[:, at] + dot(cwt[...], regrid)).astype(BF16)


    def mix(p):
        mixed[p] = dot(mwt[...], state[:, p * wide : p * wide + wide])

    def finish(p):
        for r in range(0, state.shape[0], STRIP):
            at = slice(r, r + STRIP)
            for side in range(2):
                k = 2 * p + side
                own = state[at, k * cells : (k + 1) * cells].astype(F32)
                gate = mixed[p, at, side * cells : (side + 1) * cells]
                out[k, at, :] = (own + gelu_of_half(gate)).astype(BF16)

    facts = plan[...]
    found = facts[COUNT, 0]
    chosen = [facts[TILE, k] for k in range(MAXACT)]

    def send(k):
        return pltpu.make_async_copy(out.at[k], out_hbm.at[chosen[k]], sems.at[k])

    def close(p):
        finish(p)
        for k in (2 * p, 2 * p + 1):
            if k < FOLDB:
                send(k).start()
            else:
                pl.when(k < found)(lambda k=k: send(k).start())

    settle(range(pairs))
    for p in range(pairs):
        mix(p)
    for p in range(pairs // 2):
        finish(p)
    for p in range(pairs // 2):
        for k in (2 * p, 2 * p + 1):
            if k < FOLDB:
                send(k).start()
            else:
                pl.when(k < found)(lambda k=k: send(k).start())

    @pl.when(found > pairs // 2 * 2)
    def _():
        for p in range(pairs // 2, pairs):
            close(p)

    for k in range(MAXACT):
        if k < FOLDB:
            send(k).wait()
        else:
            pl.when(k < found)(lambda k=k: send(k).wait())


def late(plan, one, two, fold, sums, base, cwt, mwt, blocks, folds, given):
    count, width, cells = given.shape
    return pl.pallas_call(
        late_kernel,
        out_shape=jax.ShapeDtypeStruct((count, width, cells), BF16),
        in_specs=[VM] * 10 + [HBM],
        out_specs=HBM,
        scratch_shapes=[
            pltpu.VMEM((width, MAXACT * cells), BF16),
            pltpu.VMEM((MAXACT // 2, width, 2 * cells), F32),
            pltpu.VMEM((MAXACT, width, cells), BF16),
            pltpu.SemaphoreType.DMA((MAXACT,)),
        ],
        input_output_aliases={10: 0},
        compiler_params=pltpu.CompilerParams(vmem_limit_bytes=12 * 2**20),
        cost_estimate=pl.CostEstimate(flops=10**9, bytes_accessed=10**6, transcendentals=3 * 10**5),
        name="late",
    )(plan, one, two, fold, sums, base, cwt, mwt, blocks, folds, given)


def per_device(
    atm_in,
    ocean_in,
    lift_weight,
    conv_weight,
    flux_weight,
    ocean_weight,
    couple_weight,
    mix_weight,
    regrid_weight,
    pair_tile,
    ocean_mask,
):
    strips = lax.axis_size("lon")
    inward = [(i, i ^ 1) for i in range(strips)]
    outward = [(i, (i + 1 if i % 2 else i - 1) % strips) for i in range(strips)]
    met = dict(outward)
    mirror = [
        (i, (i + strips // 2) % strips if met[i] == strips - 1 - i else strips - 1 - i)
        for i in range(strips)
    ]
    fwt = flux_weight.T
    send_one, send_two, plan = first(atm_in, pair_tile.T, ocean_mask)
    two = lax.ppermute(send_two, "lon", outward)
    one = lax.ppermute(send_one, "lon", inward)
    hid, flux, taps, wc, lt = interior(atm_in, lift_weight, conv_weight, fwt)
    edges, tiles, north, send_one, send_two = edge(one, two, flux, taps, wc, lt, fwt)
    one = lax.ppermute(send_one, "lon", inward)
    two = lax.ppermute(send_two, "lon", outward)
    fold = lax.ppermute(north, "lon", mirror)
    atm_hidden, given, sums, base, cwt, mwt, blocks, folds = early(
        hid, edges, plan, tiles, ocean_in, regrid_weight,
        ocean_weight, couple_weight, mix_weight,
    )
    ocean_hidden = late(
        plan, one, two, fold, sums, base, cwt, mwt, blocks, folds, given
    )
    return (atm_hidden, ocean_hidden)


def solution(mesh):
    in_specs = (
        P(("groups", "lon"), None, None),
        P(("groups", "lon"), None, None),
        P(),
        P(),
        P(),
        P(),
        P(),
        P(),
        P("lon", None, None, None),
        P("lon", None),
        P("lon"),
    )
    out_specs = (P(("groups", "lon"), None, None), P(("groups", "lon"), None, None))

    return jax.shard_map(
        per_device, mesh=mesh, in_specs=in_specs, out_specs=out_specs, check_vma=False
    )
```
